32 devices in a mesh: blk: 32 (over z, y, x, core).
Axes of the slice: x: 2, y: 2, z: 4, core: 2. Of those that a mesh axis runs over, the one named last changes fastest.
Arguments:
- features: bfloat16 [128, 352, 2048], P('blk'), may hold values from -6 to 6
- weight: bfloat16 [2048, 2048], replicated, may hold values from -0.375 to 0.375
- bias: float32 [2048], replicated, may hold values from -3 to 3
- cotangent: bfloat16 [128, 352, 2048], P('blk'), may hold values from -6 to 6
- segment_ids: int32 [128, 352], P('blk'), may hold values from 0 to 7, never falling along the last dimension, each value on 1 to 88 neighbouring positions
- neighbour_offsets: int32 [128, 352, 64], P('blk'), may hold values from 0 to 4095
- neighbour_mask: int32 [128, 352, 64], P('blk'), may hold values 0 or 1
- halo_edges: int32 [128, 2, 352, 8], P('blk'), may hold values from 0 to 63
- halo_mask: int32 [128, 2, 352, 8], P('blk'), may hold values 0 or 1
- boundary_rows: int32 [128, 2, 64], P('blk'), may hold values from 0 to 351
Outputs:
- activations: bfloat16 [128, 352, 2048], P('blk')
- grad_features: bfloat16 [128, 352, 2048], P('blk')
- grad_weight: float32 [2048, 2048], replicated
- grad_bias: float32 [2048], replicated
The draws below stay inside these ranges and needn't reach their ends.
Inputs may be any that keep to these rules, and one draw needn't show every extreme that they name: `segment_ids`: within a slot segment ids never fall; each of the 8 clusters has 1 to 88 rows and one has exactly 88.
All inputs are finite; a program needn't handle non-finite values. No bound on the sum of `neighbour_mask` or of `halo_mask` on one device may be relied on, other than what follows from the above.
Results may differ from the reference program's by a relative error of at most 0.011.
Values may be sent and summed in bfloat16 or wider, within the bound.
A program may use at most 192 MiB of HBM per device.

```python
import math
import jax
import jax.numpy as jnp
import numpy as np
from jax import lax

F = 2048
R = 352
NB = 64
KH = 8
B = 64
CLUS = 8
SLOTS = 128


def with_ends(array, stream_key, smallest, high):
    shape = array.shape
    place = [jax.random.randint(jax.random.fold_in(stream_key, axis), (), 0, shape[axis]) for axis in range(len(shape))]
    array = array.at[tuple(place)].set(smallest)
    longest = shape.index(max(shape))
    place[longest] = (place[longest] + 1) % shape[longest]
    return array.at[tuple(place)].set(high)


def shard_levels(rng, dims, split, smallest, high):
    level, own = 1.0, jax.random.fold_in(rng, 6)
    for dim, blocks in split:
        steps = jnp.exp(jax.random.uniform(jax.random.fold_in(own, dim), (blocks,), jnp.float32, smallest / len(split), high / len(split)))
        level = level * jnp.repeat(steps, dims[dim] // blocks).reshape([-1 if axis == dim else 1 for axis in range(len(dims))])
    return level


def profile(amount, total, limit, skew):
    portions = [(1 << 20) // math.isqrt(grade ** skew) + 1 for grade in range(2, amount + 1)]
    surplus, holding = total - limit - (amount - 1), [1] * (amount - 1)
    while surplus > 0:
        free = [i for i in range(amount - 1) if holding[i] < limit]
        mass, remaining = sum([portions[i] for i in free]), surplus
        for i in free:
            extra = min(limit - holding[i], max(1, remaining * portions[i] // mass), surplus)
            holding[i] = holding[i] + extra
            surplus = surplus - extra
    return np.array([limit] + holding)


def ragged_sizes(rng, amount, total, limit, slope):
    if amount == 2:
        one = jax.random.randint(rng, (), max(1, total - limit), min(limit, total - 1) + 1)
        return jnp.stack([one, total - one])
    tallies = jnp.asarray(profile(amount, total, limit, slope), jnp.int32)
    twos = (amount - 1) // 2
    giver, taker = tallies[1:1 + 2 * twos:2], tallies[2:2 + 2 * twos:2]
    slack = jnp.minimum(giver - 1, limit - taker)
    passed = jax.random.randint(jax.random.fold_in(rng, 1), (twos,), 0, 1 << 20) % (slack + 1)
    tallies = tallies.at[1:1 + 2 * twos:2].set(giver - passed).at[2:2 + 2 * twos:2].set(taker + passed)
    return tallies[jax.random.permutation(jax.random.fold_in(rng, 2), amount)]


def noise(rng, dims, scale, most, shards=(), held_as=jnp.bfloat16):
    values = scale * jax.random.normal(rng, dims, jnp.float32)
    if shards:
        values = values * shard_levels(rng, dims, shards, -0.22, 0.18)
    return jnp.clip(values, -most, most).astype(held_as)


def setup_inputs(seed: int = 0) -> dict:
    streams_of = jax.random.split(jax.random.key(seed), 11)
    return {
        "features": noise(streams_of[0], (SLOTS, R, F), 1.0, 6.0, ((0, 32),)),
        "weight": noise(streams_of[1], (F, F), (F // 8) ** -0.5, 0.375),
        "bias": noise(streams_of[2], (F,), 0.5, 3.0, (), jnp.float32),
        "cotangent": noise(streams_of[3], (SLOTS, R, F), 1.0, 6.0, ((0, 32),)),
        "segment_ids": jax.vmap(lambda own: jnp.searchsorted(jnp.cumsum(ragged_sizes(own, CLUS, R, R // 4, 0)), jnp.arange(R), side="right"))(jax.random.split(streams_of[4], SLOTS)).reshape((SLOTS, R)).astype(jnp.int32),
        "neighbour_offsets": with_ends(jax.random.randint(streams_of[5], (SLOTS, R, NB), 0, 4096), jax.random.fold_in(streams_of[5], 1), 0, 4095).astype(jnp.int32),
        "neighbour_mask": with_ends((jax.random.randint(streams_of[6], (SLOTS, R, NB), 0, 8) < 1).astype(jnp.int32), jax.random.fold_in(streams_of[6], 1), 0, 1),
        "halo_edges": with_ends(jax.random.randint(streams_of[7], (SLOTS, 2, R, KH), 0, B), jax.random.fold_in(streams_of[7], 1), 0, B - 1).astype(jnp.int32),
        "halo_mask": with_ends((jax.random.randint(streams_of[8], (SLOTS, 2, R, KH), 0, 4) < 1).astype(jnp.int32), jax.random.fold_in(streams_of[8], 1), 0, 1),
        "boundary_rows": with_ends(jax.random.randint(streams_of[9], (SLOTS, 2, B), 0, R), jax.random.fold_in(streams_of[9], 1), 0, R - 1).astype(jnp.int32),
    }


@jax.custom_vjp
def low(v):
    return lax.optimization_barrier(v.astype(jnp.bfloat16)).astype(jnp.float32)

@jax.custom_vjp
def low_back(v):
    return v

def low_keep(v):
    return (low(v), None)

def low_pass(kept, grad):
    return (grad,)

def back_keep(v):
    return (v, None)

def back_low(kept, grad):
    return (low(grad),)
low.defvjp(low_keep, low_pass)
low_back.defvjp(back_keep, back_low)

def tally(picks, marks, width):
    places = jnp.arange(width, dtype=jnp.int32)
    hot = picks[:, :, None] == places[None, None, :]
    return lax.optimization_barrier(jnp.sum(jnp.where(hot, marks[:, :, None], 0), axis=1)).astype(jnp.int32)

def slot_tables(items):
    seg, offsets, marks, edges, edge_marks = items
    rows = seg.shape[0]
    order = jnp.arange(rows, dtype=jnp.int32)
    same = seg[:, None] == seg[None, :]
    start = lax.optimization_barrier(jnp.min(jnp.where(same, order[None, :], rows), axis=1)).astype(jnp.int32)
    extent = lax.optimization_barrier(jnp.sum(same.astype(jnp.int32), axis=1)).astype(jnp.int32)
    picks = start[:, None] + offsets % extent[:, None]
    local = tally(picks, marks, rows) + 2 * (order[:, None] == order[None, :]).astype(jnp.int32)
    joined = jnp.concatenate([edges[0], edges[1] + B], axis=1)
    joined_marks = jnp.concatenate([edge_marks[0], edge_marks[1]], axis=1)
    halo = tally(joined, joined_marks, 2 * B)
    degree = lax.optimization_barrier(jnp.sum(marks, axis=1)) + lax.optimization_barrier(jnp.sum(edge_marks[0], axis=1)) + lax.optimization_barrier(jnp.sum(edge_marks[1], axis=1))
    scale = 1.0 / (1.0 + degree.astype(jnp.float32))
    return (local.astype(jnp.float32), halo.astype(jnp.float32), scale)

def forward(feats, weight, bias, tables, boundary_rows):
    local, halo, scale = tables
    width = feats.shape[2]
    sent = jax.vmap(lambda block, picks: block[picks])(feats, boundary_rows)
    before = jnp.roll(sent[:, 1], 1, axis=0)
    after = jnp.roll(sent[:, 0], -1, axis=0)
    received = jnp.concatenate([before, after], axis=1)

    def slot(items):
        block, got, loc, hal, sc = items
        total = jnp.dot(loc, block, precision=lax.Precision.HIGHEST) + jnp.dot(hal, got, precision=lax.Precision.HIGHEST)
        return low(low_back(sc[:, None] * low_back(total)))
    mixed = lax.map(jax.checkpoint(slot), (feats, received, local, halo, scale))
    pre = low_back(jnp.dot(mixed.reshape(-1, width), weight, precision=lax.Precision.HIGHEST) + bias[None, :])
    return jax.nn.silu(pre).reshape(feats.shape)

def reference(features, weight, bias, cotangent, segment_ids, neighbour_offsets, neighbour_mask, halo_edges, halo_mask, boundary_rows):
    tables = lax.map(slot_tables, (segment_ids, neighbour_offsets, neighbour_mask, halo_edges, halo_mask))
    feats = features.astype(jnp.float32)
    weight_full = weight.astype(jnp.float32)
    out, pull = jax.vjp(lambda h, w, b: forward(h, w, b, tables, boundary_rows), feats, weight_full, bias.astype(jnp.float32))
    grad_h, grad_w, grad_b = pull(cotangent.astype(jnp.float32))
    return (out.astype(jnp.bfloat16), grad_h.astype(jnp.bfloat16), grad_w, grad_b)
```

```python
import functools

import jax
import jax.numpy as jnp
from jax import lax
from jax.experimental import pallas as pl
from jax.experimental.pallas import tpu as pltpu
from jax.sharding import PartitionSpec as P

bf16 = jnp.bfloat16
f32 = jnp.float32
MESH = pl.DeviceIdType.MESH
CH = 256
H = 128


def neighbours(me):
    core = me % 2
    bits = [core, (me // 2) % 2, (me // 4) % 2, (me // 8) % 2, me // 16]
    return bits, [me + (1 << i) - (2 << i) * b for i, b in enumerate(bits)]


def main_kernel(
    mixed, w, bias, cot,
    act, gp, ag, gb,
    mixed_v, w_v, bias_v, cot_v, act_v, gp_v, pre_v,
    snd, rc, acc, rf, ra, rs, rb, gb_v, gr,
    lsem, wsem, csem, asem, gsem, ksem, ssem, rsem, bsem, brsem,
):
    me = lax.axis_index("blk")
    rows, width = mixed_v.shape
    nch = width // CH
    half = width // 2
    quart = half // 2
    (core, bx, by, bz1, bz2), (pc, px, py, pz1, pz2) = neighbours(me)
    first = [px * (1 - core) + py * core, py * (1 - core) + px * core]
    fbit = [bx * (1 - core) + by * core, by * (1 - core) + bx * core]
    second = [first[1], first[0]]
    sbit = [fbit[1], fbit[0]]

    barrier = pltpu.get_barrier_semaphore()
    for p in (pc, px, py, pz1, pz2):
        pl.semaphore_signal(barrier, inc=1, device_id=(p,), device_id_type=MESH)

    def local(src, dst, sem):
        return pltpu.make_async_copy(src, dst, sem)

    def w_in(k):
        c = pl.multiple_of(k * CH, CH)
        return local(w.at[:, pl.ds(c, CH)], w_v.at[:, pl.ds(c, CH)], wsem.at[k])

    def cot_in(k):
        c = pl.multiple_of(k * CH, CH)
        return local(cot.at[:, pl.ds(c, CH)], cot_v.at[k % 2], csem.at[k % 2])

    def act_out(k):
        c = pl.multiple_of(k * CH, CH)
        return local(act_v.at[k % 2], act.at[:, pl.ds(c, CH)], asem.at[k % 2])

    local(mixed, mixed_v, lsem.at[0]).start()
    local(bias, bias_v, lsem.at[1]).start()
    w_in(0).start()
    cot_in(0).start()
    for k in range(1, nch):
        w_in(k).start()
    local(mixed, mixed_v, lsem.at[0]).wait()
    local(bias, bias_v, lsem.at[1]).wait()
    pl.semaphore_wait(barrier, 5)

    def remote(src, dst, k, s, to):
        return pltpu.make_async_remote_copy(
            src, dst, ssem.at[k, s], rsem.at[k, s], device_id=(to,), device_id_type=MESH
        )

    def rf_rows(i):
        return pl.multiple_of(quart * i, 64)

    def at(i, level, flip):
        r = quart * i
        size = quart
        picks = [bz1, sbit[i], bz2]
        for j in range(level):
            size = size // 2
            b = picks[j]
            if flip and j == level - 1:
                b = 1 - b
            r = r + size * b
        return pl.ds(pl.multiple_of(r, 64), size)

    def core_rs(k):
        return remote(snd.at[k], rc.at[k], k, 0, pc)

    def f_rs(k, i):
        return remote(acc.at[k, 1 - fbit[i], at(i, 0, False)], rf.at[k, i], k, 1 + i, first[i])

    def a_rs(k, i):
        return remote(acc.at[k, fbit[i], at(i, 1, True)], ra.at[k, i], k, 3 + i, pz1)

    def s_rs(k, i):
        return remote(acc.at[k, fbit[i], at(i, 2, True)], rs.at[k, i], k, 5 + i, second[i])

    def b_rs(k, i):
        return remote(acc.at[k, fbit[i], at(i, 3, True)], rb.at[k, i], k, 7 + i, pz2)

    def ag_at(k, i, level):
        d = at(i, level, False)
        return ag.at[2 * k + fbit[i], pl.ds(pl.multiple_of(half * core + d.start, 64), d.size)]

    def keep(k, i):
        return local(acc.at[k, fbit[i], at(i, 3, False)], ag_at(k, i, 3), ksem.at[k, i])

    def b_ag(k, i):
        return remote(acc.at[k, fbit[i], at(i, 3, False)], ag_at(k, i, 3), k, 9 + i, pz2)

    def s_ag(k, i):
        return remote(ag_at(k, i, 2), ag_at(k, i, 2), k, 11 + i, second[i])

    def a_ag(k, i):
        return remote(ag_at(k, i, 1), ag_at(k, i, 1), k, 13 + i, pz1)

    def f_ag(k, i):
        return remote(ag_at(k, i, 0), ag_at(k, i, 0), k, 15 + i, first[i])

    def c_ag(k, j):
        part = ag.at[2 * k + j, pl.ds(pl.multiple_of(half * core, 64), half)]
        return remote(part, part, k, 17 + j, pc)

    def when(t, s, f):
        k = t - s

        @pl.when((k >= 0) & (k < nch))
        def _():
            f(k)

    def s1(k):
        core_rs(k).wait_recv()
        for j in range(2):
            acc[k, j] = acc[k, j] + rc[k, j]
        for i in range(2):
            f_rs(k, i).start()

    def fold(wait, level, buf, nxt):
        def run(k):
            for i in range(2):
                wait(k, i).wait_recv()
                d = at(i, level, False)
                acc[k, fbit[i], d] = acc[k, fbit[i], d] + buf[k, i]
                nxt(k, i)

        return run

    def final(k, i):
        keep(k, i).start()
        b_ag(k, i).start()

    def s6(k):
        for i in range(2):
            keep(k, i).wait()
            b_ag(k, i).wait_recv()
            s_ag(k, i).start()

    def s7(k):
        for i in range(2):
            s_ag(k, i).wait_recv()
            a_ag(k, i).start()

    def s8(k):
        for i in range(2):
            a_ag(k, i).wait_recv()
            f_ag(k, i).start()

    def s9(k):
        for i in range(2):
            f_ag(k, i).wait_recv()
        for j in range(2):
            c_ag(k, j).start()

    def s10(k):
        for j in range(2):
            c_ag(k, j).wait_recv()

    def compute(k):
        c = pl.multiple_of(k * CH, CH)
        w_in(k).wait()
        cot_in(k).wait()

        @pl.when(k + 1 < nch)
        def _():
            cot_in(k + 1).start()

        @pl.when(k >= 2)
        def _():
            act_out(k - 2).wait()

        b = bias_v[pl.ds(k, 1), :]
        mt = rows // 2
        sums = jnp.zeros((1, CH), f32)
        for m in range(2):
            d = pl.ds(m * mt, mt)
            pre = jnp.dot(mixed_v[d, :], w_v[:, pl.ds(c, CH)], preferred_element_type=f32) + b
            sig = 0.5 * jnp.tanh(0.5 * pre) + 0.5
            out = pre * sig
            act_v[k % 2, d, :] = out.astype(bf16)
            g = (cot_v[k % 2, d, :].astype(f32) * (sig + out * (1.0 - sig))).astype(bf16)
            gp_v[d, pl.ds(c, CH)] = g
            sums = sums + jnp.sum(g.astype(f32), axis=0, keepdims=True)
        gb_v[0, pl.ds(k, 1), :] = sums
        act_out(k).start()
        local(gp_v.at[:, pl.ds(c, CH)], gp.at[:, pl.ds(c, CH)], gsem.at[k]).start()
        dims = (((0,), (0,)), ((), ()))
        g = gp_v[:, pl.ds(c, CH)]
        there = pl.multiple_of(half * (1 - core), half)
        part = lax.dot_general(mixed_v[:, pl.ds(there, half)], g, dims, preferred_element_type=f32)
        snd[k, 0] = part[:, :H].astype(bf16)
        snd[k, 1] = part[:, H:].astype(bf16)
        core_rs(k).start()
        here = pl.multiple_of(half * core, half)
        part = lax.dot_general(mixed_v[:, pl.ds(here, half)], g, dims, preferred_element_type=f32)
        acc[k, 0] = part[:, :H].astype(bf16)
        acc[k, 1] = part[:, H:].astype(bf16)

    def step(t, carry):
        when(t, 10, s10)
        when(t, 9, s9)
        when(t, 8, s8)
        when(t, 7, s7)
        when(t, 6, s6)
        when(t, 5, fold(b_rs, 3, rb, final))
        when(t, 4, fold(s_rs, 2, rs, lambda k, i: b_rs(k, i).start()))
        when(t, 3, fold(a_rs, 1, ra, lambda k, i: s_rs(k, i).start()))
        when(t, 2, fold(f_rs, 0, rf, lambda k, i: a_rs(k, i).start()))
        when(t, 1, s1)
        when(t, 0, compute)
        return carry

    def bias_hop(j):
        to = (pc, px, py, pz1, pz2)[j]
        return pltpu.make_async_remote_copy(
            gb_v.at[j], gr.at[j], bsem.at[j], brsem.at[j], device_id=(to,), device_id_type=MESH
        )

    lax.fori_loop(0, nch + 1, step, 0)
    for j in range(5):
        bias_hop(j).start()
        step(nch + 1 + j, 0)
        bias_hop(j).wait_recv()
        gb_v[j + 1] = gb_v[j] + gr[j]
    lax.fori_loop(nch + 6, nch + 11, step, 0)
    last = local(gb_v.at[5], gb, lsem.at[0])
    last.start()
    last.wait()
    for j in range(5):
        bias_hop(j).wait_send()
    act_out(nch - 2).wait()
    act_out(nch - 1).wait()

    def finish(k, carry):
        c = pl.multiple_of(k * CH, CH)
        local(gp_v.at[:, pl.ds(c, CH)], gp.at[:, pl.ds(c, CH)], gsem.at[k]).wait()
        core_rs(k).wait_send()
        for i in range(2):
            for f in (f_rs, a_rs, s_rs, b_rs, b_ag, s_ag, a_ag, f_ag, c_ag):
                f(k, i).wait_send()
        return carry

    lax.fori_loop(0, nch, finish, 0)


def main_call(mixed, weight, bias, cot):
    rows, width = mixed.shape
    nch = width // CH
    half = width // 2
    quart = half // 2
    any_ = pl.BlockSpec(memory_space=pl.ANY)
    dma = pltpu.SemaphoreType.DMA
    return pl.pallas_call(
        main_kernel,
        out_shape=(
            jax.ShapeDtypeStruct((rows, width), bf16),
            jax.ShapeDtypeStruct((rows, width), bf16),
            jax.ShapeDtypeStruct((2 * nch, width, H), bf16),
            jax.ShapeDtypeStruct((nch, CH), f32),
        ),
        in_specs=[any_] * 4,
        out_specs=[any_] * 4,
        scratch_shapes=[
            pltpu.VMEM((rows, width), bf16),
            pltpu.VMEM((width, width), bf16),
            pltpu.VMEM((nch, CH), f32),
            pltpu.VMEM((2, rows, CH), bf16),
            pltpu.VMEM((2, rows, CH), bf16),
            pltpu.VMEM((rows, width), bf16),
            pltpu.VMEM((8, 128), f32),
            pltpu.VMEM((nch, 2, half, H), bf16),
            pltpu.VMEM((nch, 2, half, H), bf16),
            pltpu.VMEM((nch, 2, half, H), bf16),
            pltpu.VMEM((nch, 2, quart, H), bf16),
            pltpu.VMEM((nch, 2, quart // 2, H), bf16),
            pltpu.VMEM((nch, 2, quart // 4, H), bf16),
            pltpu.VMEM((nch, 2, quart // 8, H), bf16),
            pltpu.VMEM((6, nch, CH), f32),
            pltpu.VMEM((5, nch, CH), f32),
            dma((2,)),
            dma((nch,)),
            dma((2,)),
            dma((2,)),
            dma((nch,)),
            dma((nch, 2)),
            dma((nch, 19)),
            dma((nch, 19)),
            dma((5,)),
            dma((5,)),
        ],
        compiler_params=pltpu.CompilerParams(
            collective_id=0, has_side_effects=True, vmem_limit_bytes=60 << 20
        ),
        name="layer",
    )(mixed, weight, bias.reshape(nch, CH), cot)


def widen_kernel(ag, out):
    for j in range(ag.shape[0]):
        out[:, j * H : (j + 1) * H] = ag[j].astype(f32)


def widen(ag):
    n, width, _ = ag.shape
    step = 256
    return pl.pallas_call(
        widen_kernel,
        out_shape=jax.ShapeDtypeStruct((width, n * H), f32),
        grid=(width // step,),
        in_specs=[pl.BlockSpec((n, step, H), lambda i: (0, i, 0))],
        out_specs=pl.BlockSpec((step, n * H), lambda i: (i, 0)),
        name="widen",
    )(ag)


def passed_along(value, axis, steps):
    count = lax.axis_size(axis)
    pairs = [(source, (source + steps) % count) for source in range(count)]
    return lax.ppermute(value, axis, pairs)


def tables(seg, offsets, marks, edges, edge_marks, rim):
    slots, rows = seg.shape
    order = jnp.arange(rows, dtype=jnp.int32)
    same = seg[:, :, None] == seg[:, None, :]
    start = jnp.min(jnp.where(same, order, rows), axis=2)
    extent = jnp.sum(same.astype(jnp.int32), axis=2)
    picks = jnp.where(marks == 1, offsets % extent[:, :, None], -1)
    lanes = jnp.arange(128, dtype=jnp.int32)
    near = jnp.sum((picks[:, :, :, None] == lanes).astype(f32), axis=2).astype(bf16)
    spread = (lanes[None, :, None] == (order - start)[:, None, :]).astype(bf16)
    local = jnp.einsum("sio,soj->sij", near, spread, preferred_element_type=f32)
    local = jnp.where(same, local, 0.0) + 2.0 * (order[:, None] == order[None, :])
    joined = jnp.concatenate([edges[:, 0], edges[:, 1] + rim], axis=2)
    joined_marks = jnp.concatenate([edge_marks[:, 0], edge_marks[:, 1]], axis=2)
    cols = jnp.arange(2 * rim, dtype=jnp.int32)
    far = jnp.sum(jnp.where(joined[..., None] == cols, joined_marks[..., None], 0), axis=2)
    degree = jnp.sum(marks, axis=2) + jnp.sum(joined_marks, axis=2)
    return local.astype(bf16), far.astype(bf16), 1.0 / (1.0 + degree.astype(f32))


def per_device(
    features,
    weight,
    bias,
    cotangent,
    segment_ids,
    neighbour_offsets,
    neighbour_mask,
    halo_edges,
    halo_mask,
    boundary_rows,
):
    slots, rows, width = features.shape
    rim = boundary_rows.shape[2]
    local_counts, halo_counts, scale = tables(
        segment_ids, neighbour_offsets, neighbour_mask, halo_edges, halo_mask, rim
    )
    chosen = (boundary_rows[..., None] == jnp.arange(rows, dtype=jnp.int32)).astype(bf16)
    sent = jnp.einsum("sjbr,srf->sjbf", chosen, features, preferred_element_type=f32).astype(bf16)
    from_prev = passed_along(sent[slots - 1, 1], "blk", 1)
    from_next = passed_along(sent[0, 0], "blk", -1)
    before = jnp.concatenate([from_prev[None], sent[: slots - 1, 1]], axis=0)
    after = jnp.concatenate([sent[1:, 0], from_next[None]], axis=0)
    received = jnp.concatenate([before, after], axis=1)
    summed = jnp.einsum("srk,skf->srf", local_counts, features, preferred_element_type=f32)
    summed = summed + jnp.einsum("srk,skf->srf", halo_counts, received, preferred_element_type=f32)
    mixed = (scale[:, :, None] * summed).astype(bf16).reshape(slots * rows, width)
    incoming = cotangent.reshape(slots * rows, width)
    if lax.axis_size("blk") == 32:
        activations, grad_pre, gathered, grad_bias = main_call(mixed, weight, bias, incoming)
        grad_weight = widen(gathered)
        grad_bias = grad_bias.reshape(-1)
    else:
        pre = jnp.dot(mixed, weight, preferred_element_type=f32) + bias[None, :]
        sigma = jax.nn.sigmoid(pre)
        activations = (pre * sigma).astype(bf16)
        grad_pre = (incoming.astype(f32) * (sigma * (1.0 + pre * (1.0 - sigma)))).astype(bf16)
        bias_term = jnp.sum(grad_pre, axis=0, dtype=f32)
        weight_term = lax.dot_general(
            mixed, grad_pre, (((0,), (0,)), ((), ())), preferred_element_type=f32
        )
        grad_weight, grad_bias = lax.psum((weight_term, bias_term), "blk")
    grad_mixed = lax.dot_general(
        grad_pre, weight, (((1,), (1,)), ((), ())), preferred_element_type=f32
    )
    grad_summed = (scale.reshape(-1)[:, None] * grad_mixed).astype(bf16)
    grad_summed = grad_summed.reshape(slots, rows, width)
    grad_received = jnp.einsum(
        "srk,srf->skf", halo_counts, grad_summed, preferred_element_type=f32
    ).astype(bf16)
    toward_prev = grad_received[:, :rim]
    toward_next = grad_received[:, rim:]
    back_prev = passed_along(toward_next[slots - 1], "blk", 1)
    back_next = passed_along(toward_prev[0], "blk", -1)
    grad_first = jnp.concatenate([back_prev[None], toward_next[: slots - 1]], axis=0)
    grad_second = jnp.concatenate([toward_prev[1:], back_next[None]], axis=0)
    grad_sent = jnp.stack([grad_first, grad_second], axis=1)
    grad_features = jnp.einsum(
        "srk,srf->skf", local_counts, grad_summed, preferred_element_type=f32
    ) + jnp.einsum("sjbr,sjbf->srf", chosen, grad_sent, preferred_element_type=f32)
    return (
        activations.reshape(slots, rows, width),
        grad_features.astype(bf16),
        grad_weight,
        grad_bias,
    )


def solution(mesh):
    in_specs = (
        P("blk", None, None),
        P(),
        P(),
        P("blk", None, None),
        P("blk", None),
        P("blk", None, None),
        P("blk", None, None),
        P("blk", None, None, None),
        P("blk", None, None, None),
        P("blk", None, None),
    )
    out_specs = (P("blk", None, None), P("blk", None, None), P(), P())
    return jax.shard_map(
        per_device, mesh=mesh, in_specs=in_specs, out_specs=out_specs, check_vma=False
    )
```

```python
import functools

import jax
import jax.numpy as jnp
from jax import lax
from jax.experimental import pallas as pl
from jax.experimental.pallas import tpu as pltpu
from jax.sharding import PartitionSpec as P

bf16 = jnp.bfloat16
f32 = jnp.float32
MESH = pl.DeviceIdType.MESH
CH = 256
H = 128


def neighbours(me):
    core = me % 2
    bits = [core, (me // 2) % 2, (me // 4) % 2, (me // 8) % 2, me // 16]
    return bits, [me + (1 << i) - (2 << i) * b for i, b in enumerate(bits)]


def main_kernel(
    x, w, bias, cot, seg, offs, marks, edges, edge_marks, rims,
    act, gf, ag, gb,
    xr, kt, ot, sc, mixed_v, w_v, bias_v, cot_v, act_v, gp_v,
    seg_v, offs_v, marks_v, edges_v, emarks_v, rims_v, qv, vv, hs, hr,
    snd, rc, acc, rf, ra, rs, rb, gb_v, gr,
    xsem, tsem, wsem, csem, asem, fsem, ksem, ssem, rsem, bsem, brsem, hsem, hrsem,
):
    n = lax.axis_size("blk")
    me = lax.axis_index("blk")
    slots, deep, width = xr.shape
    rows = kt.shape[2]
    rim = rims_v.shape[2]
    near = offs_v.shape[2]
    halo = edges_v.shape[3]
    total = slots * rows
    nch = width // CH
    half = width // 2
    unit = half // U
    (core, bx, by, bz1, bz2), (pc, px, py, pz1, pz2) = neighbours(me)
    prev = lax.rem(me + n - 1, n)
    nxt = lax.rem(me + 1, n)
    first = [px * (1 - core) + py * core, py * (1 - core) + px * core]
    fbit = [bx * (1 - core) + by * core, by * (1 - core) + bx * core]
    second = [first[1], first[0]]
    sbit = [fbit[1], fbit[0]]

    barrier = pltpu.get_barrier_semaphore()
    for p in (pc, px, py, pz1, pz2, prev, nxt):
        pl.semaphore_signal(barrier, inc=1, device_id=(p,), device_id_type=MESH)

    def local(src, dst, sem):
        return pltpu.make_async_copy(src, dst, sem)

    def cols(k):
        return pl.ds(pl.multiple_of(k * CH, CH), CH)

    def slot_rows(s):
        return pl.ds(pl.multiple_of(s * rows, 16), rows)

    def x_in(s):
        return local(x.at[slot_rows(s)], xr.at[s, pl.ds(0, rows)], xsem.at[s])

    def w_in(k):
        return local(w.at[:, cols(k)], w_v.at[:, cols(k)], wsem.at[k])

    def cot_in(k):
        return local(cot.at[:, cols(k)], cot_v.at[k % 2], csem.at[k % 2])

    def act_out(k):
        return local(act_v.at[k % 2], act.at[:, cols(k)], asem.at[k % 2])

    def gf_out(s):
        return local(xr.at[s, pl.ds(0, rows)], gf.at[slot_rows(s)], fsem.at[s])

    small = [
        local(src, dst, tsem.at[i])
        for i, (src, dst) in enumerate(
            (
                (rims, rims_v),
                (seg, seg_v),
                (offs, offs_v),
                (marks, marks_v),
                (edges, edges_v),
                (edge_marks, emarks_v),
                (bias, bias_v),
            )
        )
    ]
    small[0].start()
    x_in(0).start()
    x_in(slots - 1).start()
    for c in small[1:]:
        c.start()
    for s in range(1, slots - 1):
        x_in(s).start()
    w_in(0).start()
    cot_in(0).start()
    cot_in(1).start()
    for k in range(1, nch):
        w_in(k).start()

    def offer(s):
        picks = jnp.concatenate([rims_v[s, 0:1, :], rims_v[s, 1:2, :]], axis=1)
        order = lax.broadcasted_iota(jnp.int32, (rows, 2 * rim), 0)
        ot[s] = jnp.where(order == picks, 1.0, 0.0).astype(bf16)
        dims = (((0,), (0,)), ((), ()))
        return lax.dot_general(
            ot[s], xr[s, pl.ds(0, rows), :], dims, preferred_element_type=f32
        ).astype(bf16)

    def halo_send(j):
        s, to = ((0, nxt), (slots - 1, prev))[j]
        dst = xr.at[s, pl.ds(rows + rim * j, rim)]
        return pltpu.make_async_remote_copy(
            hs.at[j], dst, hsem.at[j], hrsem.at[j], device_id=(to,), device_id_type=MESH
        )

    def back_send(j):
        to = (prev, nxt)[j]
        return pltpu.make_async_remote_copy(
            hs.at[2 + j], hr.at[j], hsem.at[2 + j], hrsem.at[2 + j],
            device_id=(to,), device_id_type=MESH,
        )

    small[0].wait()
    x_in(0).wait()
    out = offer(0)
    hs[1] = out[:rim]
    xr[1, pl.ds(rows, rim), :] = out[rim:]
    x_in(slots - 1).wait()
    out = offer(slots - 1)
    hs[0] = out[rim:]
    xr[slots - 2, pl.ds(rows + rim, rim), :] = out[:rim]
    pl.semaphore_wait(barrier, 7)
    halo_send(0).start()
    halo_send(1).start()
    for c in small[1:]:
        c.wait()
    for s in range(1, slots - 1):
        x_in(s).wait()
        out = offer(s)
        xr[s - 1, pl.ds(rows + rim, rim), :] = out[:rim]
        xr[s + 1, pl.ds(rows, rim), :] = out[rim:]

    def eye(size):
        r = lax.broadcasted_iota(jnp.int32, (size, size), 0)
        c = lax.broadcasted_iota(jnp.int32, (size, size), 1)
        return jnp.where(r == c, 1.0, 0.0).astype(bf16)

    def turned(value):
        dims = (((1,), (1,)), ((), ()))
        return lax.dot_general(
            eye(value.shape[1]), value.astype(bf16), dims, preferred_element_type=f32
        ).astype(jnp.int32)

    def tables(s, carry):
        seg_r = seg_v[pl.ds(s, 1), :].astype(f32)
        ri = lax.broadcasted_iota(jnp.int32, (rows, rows), 0)
        ci = lax.broadcasted_iota(jnp.int32, (rows, rows), 1)
        diag = ri == ci
        seg_c = jnp.sum(jnp.where(diag, seg_r, 0.0), axis=1, keepdims=True)
        start = jnp.sum(jnp.where(seg_r < seg_c, 1.0, 0.0), axis=1, keepdims=True)
        same = seg_r == seg_c
        size = jnp.sum(jnp.where(same, 1.0, 0.0), axis=1, keepdims=True)
        off = offs_v[s].astype(f32)
        rest = off - jnp.floor((off + 0.5) * (1.0 / size)) * size
        rest = jnp.where(rest < 0.0, rest + size, rest)
        rest = jnp.where(rest >= size, rest - size, rest)
        marked = marks_v[s]
        pick = turned(jnp.where(marked == 1, rest, 200.0))
        qv[...] = pick >> 2
        vv[...] = 1 << ((pick & 3) << 3)
        q = lax.broadcasted_iota(jnp.int32, (Q, rows), 0)
        packed = jnp.zeros((Q, rows), jnp.int32)
        for k in range(near):
            packed = packed + jnp.where(qv[k : k + 1, :] == q, vv[k : k + 1, :], 0)
        counts = jnp.concatenate(
            [((packed >> (8 * r)) & 255).astype(f32) for r in range(4)], axis=0
        ).astype(bf16)
        rel = lax.broadcasted_iota(jnp.int32, (rows, 1), 0) - start.astype(jnp.int32)
        place = (rel & 3) * Q + (rel >> 2)
        lanes = lax.broadcasted_iota(jnp.int32, (rows, 4 * Q), 1)
        spread = jnp.where(lanes == place, 1.0, 0.0).astype(bf16)
        around = jnp.dot(spread, counts, preferred_element_type=f32)
        around = jnp.where(same, around, 0.0) + jnp.where(diag, 2.0, 0.0)
        kt[s, pl.ds(0, rows), :] = around.astype(bf16)
        degree = jnp.sum(marked.astype(f32), axis=1, keepdims=True)
        r = lax.broadcasted_iota(jnp.int32, (rim, rows), 0)
        for j in range(2):
            hot = emarks_v[s, j]
            degree = degree + jnp.sum(hot.astype(f32), axis=1, keepdims=True)
            pick = turned(jnp.where(hot == 1, edges_v[s, j].astype(f32), 200.0))
            far = jnp.zeros((rim, rows), f32)
            for k in range(halo):
                far = far + jnp.where(pick[k : k + 1, :] == r, 1.0, 0.0)
            kt[s, pl.ds(rows + rim * j, rim), :] = far.astype(bf16)
        sc[slot_rows(s), :] = 1.0 / (1.0 + degree)
        return carry

    lax.fori_loop(0, slots, tables, 0)

    def mix(s):
        d = slot_rows(s)
        dims = (((0,), (0,)), ((), ()))
        for j in range(4):
            c = pl.ds(j * (width // 4), width // 4)
            summed = lax.dot_general(kt[s], xr[s, :, c], dims, preferred_element_type=f32)
            mixed_v[d, c] = (sc[d, :] * summed).astype(bf16)

    for s in range(1, slots - 1):
        mix(s)
    halo_send(0).wait_recv()
    halo_send(1).wait_recv()
    mix(0)
    mix(slots - 1)

    def remote(src, dst, k, s, to):
        return pltpu.make_async_remote_copy(
            src, dst, ssem.at[k, s], rsem.at[k, s], device_id=(to,), device_id_type=MESH
        )

    def at(u, level, flip=False, base=0):
        r = base + unit * u
        size = unit
        picks = [bz1, sbit[u % 2]]
        for j in range(level):
            size = size // 2
            b = picks[j]
            if flip and j == level - 1:
                b = 1 - b
            r = r + size * b
        return pl.ds(pl.multiple_of(r, 16), size)

    def c_rs(k, u):
        return remote(snd.at[k % 2, :, at(u, 0)], rc.at[k, :, at(u, 0)], k, u, pc)

    def f_rs(k, u):
        f = fbit[u % 2]
        return remote(acc.at[k, 1 - f, at(u, 0)], rf.at[k, u], k, U + u, first[u % 2])

    def a_rs(k, u):
        return remote(acc.at[k, fbit[u % 2], at(u, 1, True)], ra.at[k, u], k, 2 * U + u, pz1)

    def s_rs(k, u):
        f = fbit[u % 2]
        return remote(acc.at[k, f, at(u, 2, True)], rs.at[k, u], k, 3 * U + u, second[u % 2])

    def b_rs(k, u):
        return remote(acc.at[k, fbit[u % 2], at(u, 2)], rb.at[k, u], k, 4 * U + u, pz2)

    def ag_at(k, u, level):
        return ag.at[2 * k + fbit[u % 2], at(u, level, False, half * core)]

    def keep(k, u):
        return local(rs.at[k, u], ag_at(k, u, 2), ksem.at[k, u])

    def s_ag(k, u):
        return remote(rs.at[k, u], ag_at(k, u, 2), k, 5 * U + u, second[u % 2])

    def a_ag(k, u):
        return remote(ag_at(k, u, 1), ag_at(k, u, 1), k, 6 * U + u, pz1)

    def f_ag(k, u):
        return remote(ag_at(k, u, 0), ag_at(k, u, 0), k, 7 * U + u, first[u % 2])

    def c_ag(k, u):
        part = ag.at[pl.ds(2 * k, 2), at(u, 0, False, half * core)]
        return remote(part, part, k, 8 * U + u, pc)

    def fold(level, buf):
        def run(k, u):
            f = fbit[u % 2]
            d = at(u, level)
            acc[k, f, d] = acc[k, f, d] + buf[k, u]

        return run

    def fold_core(k, u):
        d = at(u, 0)
        for j in range(2):
            acc[k, j, d] = acc[k, j, d] + rc[k, j, d]

    def last_fold(k, u):
        rs[k, u] = acc[k, fbit[u % 2], at(u, 2)] + rb[k, u]
        keep(k, u).start()

    def settle(k, u):
        keep(k, u).wait()

    hops = [
        (c_rs, fold_core, f_rs),
        (f_rs, fold(0, rf), a_rs),
        (a_rs, fold(1, ra), s_rs),
        (s_rs, fold(2, rs), b_rs),
        (b_rs, last_fold, s_ag),
        (s_ag, settle, a_ag),
        (a_ag, None, f_ag),
        (f_ag, None, c_ag),
        (c_ag, None, None),
    ]

    def serve(t, v, order):
        for h in order:
            took, work, send = hops[h]
            back = v - DELAY[h]
            k = t + back // U
            u = back % U

            @pl.when((k >= 0) & (k < nch))
            def _():
                took(k, u).wait_recv()
                if work is not None:
                    work(k, u)
                if send is not None:
                    send(k, u).start()

    def pre_part(k, m):
        mt = total // 2
        d = pl.ds(m * mt, mt)
        b = bias_v[pl.ds(k, 1), :]
        pre = jnp.dot(mixed_v[d, :], w_v[:, cols(k)], preferred_element_type=f32) + b
        sig = 0.5 * jnp.tanh(0.5 * pre) + 0.5
        out = pre * sig
        act_v[k % 2, d, :] = out.astype(bf16)
        g = (cot_v[k % 2, d, :].astype(f32) * (sig + out * (1.0 - sig))).astype(bf16)
        gp_v[d, cols(k)] = g
        sums = jnp.sum(g.astype(f32), axis=0, keepdims=True)
        if m:
            sums = sums + gb_v[0, pl.ds(k, 1), :]
        gb_v[0, pl.ds(k, 1), :] = sums

    def grad_part(k, side):
        start = pl.multiple_of(half * side, half)
        dims = (((0,), (0,)), ((), ()))
        return lax.dot_general(
            mixed_v[:, pl.ds(start, half)], gp_v[:, cols(k)], dims, preferred_element_type=f32
        )

    def there(k):
        part = grad_part(k, 1 - core)
        snd[k % 2, 0] = part[:, :H].astype(bf16)
        snd[k % 2, 1] = part[:, H:].astype(bf16)

    def here(k):
        part = grad_part(k, core)
        acc[k, 0] = part[:, :H].astype(bf16)
        acc[k, 1] = part[:, H:].astype(bf16)

    def early(t, more):
        serve(t, 0, ORDER)
        serve(t, 1, ORDER)

        @pl.when(t >= 2)
        def _():
            for u in range(U):
                c_rs(t - 2, u).wait_send()

        if more:
            w_in(t + 1).wait()
            cot_in(t + 1).wait()

            @pl.when(t >= 1)
            def _():
                act_out(t - 1).wait()

        there(t)
        if more:
            pre_part(t + 1, 0)
        for u in range(U):
            c_rs(t, u).start()
        serve(t, 2, ORDER)
        serve(t, 3, ORDER)
        here(t)
        if more:
            pre_part(t + 1, 1)
            act_out(t + 1).start()

            @pl.when(t + 2 < nch)
            def _():
                cot_in(t + 2).start()

    w_in(0).wait()
    cot_in(0).wait()
    pre_part(0, 0)
    pre_part(0, 1)
    act_out(0).start()

    def early_step(t, carry):
        early(t, True)
        return carry

    lax.fori_loop(0, nch - 1, early_step, 0)
    early(nch - 1, False)

    def bias_hop(j):
        to = pc
        for i, p in enumerate((px, py, pz1, pz2)):
            to = jnp.where(j == i + 1, p, to)
        return pltpu.make_async_remote_copy(
            gb_v.at[j], gr.at[j], bsem.at[j], brsem.at[j], device_id=(to,), device_id_type=MESH
        )

    def bias_step(i):
        @pl.when((i >= 1) & (i <= 5))
        def _():
            bias_hop(i - 1).wait_recv()
            gb_v[i] = gb_v[i - 1] + gr[i - 1]

        @pl.when(i < 5)
        def _():
            bias_hop(i).start()

    def late_mixed(i, carry):
        bias_step(i)
        s = jnp.where(i == 0, 0, jnp.where(i == 1, slots - 1, i - 1))
        d = slot_rows(s)
        tile = width // 4
        for v in range(U):
            serve(nch + i, v, ORDER)
            c = pl.ds(v * tile, tile)
            dims = (((1,), (1,)), ((), ()))
            back = lax.dot_general(gp_v[d, :], w_v[c, :], dims, preferred_element_type=f32)
            mixed_v[d, c] = (sc[d, :] * back).astype(bf16)
        out = jnp.dot(
            kt[s, pl.ds(rows, 2 * rim), :], mixed_v[d, :], preferred_element_type=f32
        ).astype(bf16)

        @pl.when(s > 0)
        def _():
            xr[s - 1, pl.ds(rows + rim, rim), :] = out[:rim]

        @pl.when(s < slots - 1)
        def _():
            xr[s + 1, pl.ds(rows, rim), :] = out[rim:]

        @pl.when(s == 0)
        def _():
            hs[2] = out[:rim]
            back_send(0).start()

        @pl.when(s == slots - 1)
        def _():
            hs[3] = out[rim:]
            back_send(1).start()

        return carry

    lax.fori_loop(0, slots, late_mixed, 0)
    back_send(0).wait_recv()
    back_send(1).wait_recv()
    xr[slots - 1, pl.ds(rows + rim, rim), :] = hr[0]
    xr[0, pl.ds(rows, rim), :] = hr[1]

    def late_features(s, carry):
        bias_step(s + slots)
        d = slot_rows(s)
        tile = width // 4
        for v in range(U):
            serve(nch + slots + s, v, ORDER)
            c = pl.ds(v * tile, tile)
            grad = jnp.dot(kt[s, pl.ds(0, rows), :], mixed_v[d, c], preferred_element_type=f32)
            grad = grad + jnp.dot(
                ot[s], xr[s, pl.ds(rows, 2 * rim), c], preferred_element_type=f32
            )
            xr[s, pl.ds(0, rows), c] = grad.astype(bf16)
        gf_out(s).start()
        return carry

    lax.fori_loop(0, slots, late_features, 0)

    def late(t, carry):
        for v in range(U):
            serve(t, v, ORDER)
        return carry

    lax.fori_loop(nch + 2 * slots, nch + (DELAY[-1] + U - 1) // U + 1, late, 0)
    last = local(gb_v.at[5], gb, tsem.at[0])
    last.start()
    last.wait()
    for j in range(5):
        bias_hop(j).wait_send()
    for j in range(2):
        halo_send(j).wait_send()
        back_send(j).wait_send()
        act_out(nch - 2 + j).wait()
    for s in range(slots):
        gf_out(s).wait()
    for k in range(nch - 2, nch):
        for u in range(U):
            c_rs(k, u).wait_send()

    def finish(k, carry):
        for u in range(U):
            for f in (f_rs, a_rs, s_rs, b_rs, s_ag, a_ag, f_ag, c_ag):
                f(k, u).wait_send()
        return carry

    lax.fori_loop(0, nch, finish, 0)


U = 4
Q = 24
DELAY = [4 + 4 * h for h in range(9)]
ORDER = list(range(8, -1, -1))


def main_call(features, weight, bias, cot, seg, offs, marks, edges, edge_marks, rims):
    slots, rows = seg.shape
    total, width = cot.shape
    rim = rims.shape[2]
    nch = width // CH
    half = width // 2
    unit = half // U
    any_ = pl.BlockSpec(memory_space=pl.ANY)
    dma = pltpu.SemaphoreType.DMA
    i32 = jnp.int32
    return pl.pallas_call(
        main_kernel,
        out_shape=(
            jax.ShapeDtypeStruct((total, width), bf16),
            jax.ShapeDtypeStruct((total, width), bf16),
            jax.ShapeDtypeStruct((2 * nch, width, H), bf16),
            jax.ShapeDtypeStruct((nch, CH), f32),
        ),
        in_specs=[any_] * 10,
        out_specs=[any_] * 4,
        scratch_shapes=[
            pltpu.VMEM((slots, rows + 2 * rim, width), bf16),
            pltpu.VMEM((slots, rows + 2 * rim, rows), bf16),
            pltpu.VMEM((slots, rows, 2 * rim), bf16),
            pltpu.VMEM((total, 1), f32),
            pltpu.VMEM((total, width), bf16),
            pltpu.VMEM((width, width), bf16),
            pltpu.VMEM((nch, CH), f32),
            pltpu.VMEM((2, total, CH), bf16),
            pltpu.VMEM((2, total, CH), bf16),
            pltpu.VMEM((total, width), bf16),
            pltpu.VMEM(seg.shape, i32),
            pltpu.VMEM(offs.shape, i32),
            pltpu.VMEM(marks.shape, i32),
            pltpu.VMEM(edges.shape, i32),
            pltpu.VMEM(edge_marks.shape, i32),
            pltpu.VMEM(rims.shape, i32),
            pltpu.VMEM((offs.shape[2], rows), i32),
            pltpu.VMEM((offs.shape[2], rows), i32),
            pltpu.VMEM((4, rim, width), bf16),
            pltpu.VMEM((2, rim, width), bf16),
            pltpu.VMEM((2, 2, half, H), bf16),
            pltpu.VMEM((nch, 2, half, H), bf16),
            pltpu.VMEM((nch, 2, half, H), bf16),
            pltpu.VMEM((nch, U, unit, H), bf16),
            pltpu.VMEM((nch, U, unit // 2, H), bf16),
            pltpu.VMEM((nch, U, unit // 4, H), bf16),
            pltpu.VMEM((nch, U, unit // 4, H), bf16),
            pltpu.VMEM((6, nch, CH), f32),
            pltpu.VMEM((5, nch, CH), f32),
            dma((slots,)),
            dma((7,)),
            dma((nch,)),
            dma((2,)),
            dma((2,)),
            dma((slots,)),
            dma((nch, U)),
            dma((nch, 9 * U)),
            dma((nch, 9 * U)),
            dma((5,)),
            dma((5,)),
            dma((4,)),
            dma((4,)),
        ],
        compiler_params=pltpu.CompilerParams(
            collective_id=0, has_side_effects=True, vmem_limit_bytes=62 << 20
        ),
        name="layer",
    )(features, weight, bias.reshape(nch, CH), cot, seg, offs, marks, edges, edge_marks, rims)


def widen_kernel(ag, out):
    for j in range(ag.shape[0]):
        out[:, j * H : (j + 1) * H] = ag[j].astype(f32)


def widen(ag):
    n, width, _ = ag.shape
    step = 256
    return pl.pallas_call(
        widen_kernel,
        out_shape=jax.ShapeDtypeStruct((width, n * H), f32),
        grid=(width // step,),
        in_specs=[pl.BlockSpec((n, step, H), lambda i: (0, i, 0))],
        out_specs=pl.BlockSpec((step, n * H), lambda i: (i, 0)),
        name="widen",
    )(ag)


def passed_along(value, axis, steps):
    count = lax.axis_size(axis)
    pairs = [(source, (source + steps) % count) for source in range(count)]
    return lax.ppermute(value, axis, pairs)


def tables(seg, offsets, marks, edges, edge_marks, rim):
    slots, rows = seg.shape
    order = jnp.arange(rows, dtype=jnp.int32)
    same = seg[:, :, None] == seg[:, None, :]
    start = jnp.min(jnp.where(same, order, rows), axis=2)
    extent = jnp.sum(same.astype(jnp.int32), axis=2)
    picks = jnp.where(marks == 1, offsets % extent[:, :, None], -1)
    lanes = jnp.arange(128, dtype=jnp.int32)
    near = jnp.sum((picks[:, :, :, None] == lanes).astype(f32), axis=2).astype(bf16)
    spread = (lanes[None, :, None] == (order - start)[:, None, :]).astype(bf16)
    local = jnp.einsum("sio,soj->sij", near, spread, preferred_element_type=f32)
    local = jnp.where(same, local, 0.0) + 2.0 * (order[:, None] == order[None, :])
    joined = jnp.concatenate([edges[:, 0], edges[:, 1] + rim], axis=2)
    joined_marks = jnp.concatenate([edge_marks[:, 0], edge_marks[:, 1]], axis=2)
    cols = jnp.arange(2 * rim, dtype=jnp.int32)
    far = jnp.sum(jnp.where(joined[..., None] == cols, joined_marks[..., None], 0), axis=2)
    degree = jnp.sum(marks, axis=2) + jnp.sum(joined_marks, axis=2)
    return local.astype(bf16), far.astype(bf16), 1.0 / (1.0 + degree.astype(f32))


def spread_out(
    features,
    weight,
    bias,
    cotangent,
    segment_ids,
    neighbour_offsets,
    neighbour_mask,
    halo_edges,
    halo_mask,
    boundary_rows,
):
    slots, rows, width = features.shape
    rim = boundary_rows.shape[2]
    local_counts, halo_counts, scale = tables(
        segment_ids, neighbour_offsets, neighbour_mask, halo_edges, halo_mask, rim
    )
    chosen = (boundary_rows[..., None] == jnp.arange(rows, dtype=jnp.int32)).astype(bf16)
    sent = jnp.einsum("sjbr,srf->sjbf", chosen, features, preferred_element_type=f32).astype(bf16)
    from_prev = passed_along(sent[slots - 1, 1], "blk", 1)
    from_next = passed_along(sent[0, 0], "blk", -1)
    before = jnp.concatenate([from_prev[None], sent[: slots - 1, 1]], axis=0)
    after = jnp.concatenate([sent[1:, 0], from_next[None]], axis=0)
    received = jnp.concatenate([before, after], axis=1)
    summed = jnp.einsum("srk,skf->srf", local_counts, features, preferred_element_type=f32)
    summed = summed + jnp.einsum("srk,skf->srf", halo_counts, received, preferred_element_type=f32)
    mixed = (scale[:, :, None] * summed).astype(bf16).reshape(slots * rows, width)
    incoming = cotangent.reshape(slots * rows, width)
    pre = jnp.dot(mixed, weight, preferred_element_type=f32) + bias[None, :]
    sigma = jax.nn.sigmoid(pre)
    activations = (pre * sigma).astype(bf16)
    grad_pre = (incoming.astype(f32) * (sigma * (1.0 + pre * (1.0 - sigma)))).astype(bf16)
    bias_term = jnp.sum(grad_pre, axis=0, dtype=f32)
    weight_term = lax.dot_general(
        mixed, grad_pre, (((0,), (0,)), ((), ())), preferred_element_type=f32
    )
    grad_weight, grad_bias = lax.psum((weight_term, bias_term), "blk")
    grad_mixed = lax.dot_general(
        grad_pre, weight, (((1,), (1,)), ((), ())), preferred_element_type=f32
    )
    grad_summed = (scale.reshape(-1)[:, None] * grad_mixed).astype(bf16)
    grad_summed = grad_summed.reshape(slots, rows, width)
    grad_received = jnp.einsum(
        "srk,srf->skf", halo_counts, grad_summed, preferred_element_type=f32
    ).astype(bf16)
    toward_prev = grad_received[:, :rim]
    toward_next = grad_received[:, rim:]
    back_prev = passed_along(toward_next[slots - 1], "blk", 1)
    back_next = passed_along(toward_prev[0], "blk", -1)
    grad_first = jnp.concatenate([back_prev[None], toward_next[: slots - 1]], axis=0)
    grad_second = jnp.concatenate([toward_prev[1:], back_next[None]], axis=0)
    grad_sent = jnp.stack([grad_first, grad_second], axis=1)
    grad_features = jnp.einsum(
        "srk,srf->skf", local_counts, grad_summed, preferred_element_type=f32
    ) + jnp.einsum("sjbr,sjbf->srf", chosen, grad_sent, preferred_element_type=f32)
    return (
        activations.reshape(slots, rows, width),
        grad_features.astype(bf16),
        grad_weight,
        grad_bias,
    )


def per_device(
    features,
    weight,
    bias,
    cotangent,
    segment_ids,
    neighbour_offsets,
    neighbour_mask,
    halo_edges,
    halo_mask,
    boundary_rows,
):
    operands = (
        segment_ids,
        neighbour_offsets,
        neighbour_mask,
        halo_edges,
        halo_mask,
        boundary_rows,
    )
    if lax.axis_size("blk") != 32:
        return spread_out(features, weight, bias, cotangent, *operands)
    slots, rows, width = features.shape
    flat = (slots * rows, width)
    activations, grad_features, gathered, grad_bias = main_call(
        features.reshape(flat), weight, bias, cotangent.reshape(flat), *operands
    )
    return (
        activations.reshape(features.shape),
        grad_features.reshape(features.shape),
        widen(gathered),
        grad_bias.reshape(-1),
    )


def solution(mesh):
    in_specs = (
        P("blk", None, None),
        P(),
        P(),
        P("blk", None, None),
        P("blk", None),
        P("blk", None, None),
        P("blk", None, None),
        P("blk", None, None, None),
        P("blk", None, None, None),
        P("blk", None, None),
    )
    out_specs = (P("blk", None, None), P("blk", None, None), P(), P())
    return jax.shard_map(
        per_device, mesh=mesh, in_specs=in_specs, out_specs=out_specs, check_vma=False
    )
```

```python
import functools

import jax
import jax.numpy as jnp
from jax import lax
from jax.experimental import pallas as pl
from jax.experimental.pallas import tpu as pltpu
from jax.sharding import PartitionSpec as P

bf16 = jnp.bfloat16
f32 = jnp.float32
MESH = pl.DeviceIdType.MESH
CH = 256
H = 128


def neighbours(me):
    core = me % 2
    bits = [core, (me // 2) % 2, (me // 4) % 2, (me // 8) % 2, me // 16]
    return bits, [me + (1 << i) - (2 << i) * b for i, b in enumerate(bits)]


def main_kernel(
    x, w, bias, cot, seg, offs, marks, edges, edge_marks, rims,
    act, xr, ag, gb,
    kt, ot, sc, mixed_v, w_v, bias_v, cot_v, gp_v,
    seg_v, offs_v, marks_v, edges_v, emarks_v, rims_v, qv, vv, hs, hr,
    snd, rc, fb, rf, ab, ra, sb, rs, rb, gb_v, gr,
    xsem, tsem, wsem, csem, ssem, rsem, bsem, brsem, hsem, hrsem,
):
    n = lax.axis_size("blk")
    me = lax.axis_index("blk")
    slots, deep, width = xr.shape
    rows = kt.shape[2]
    rim = rims_v.shape[2]
    near = offs_v.shape[1]
    halo = edges_v.shape[2]
    total = slots * rows
    nch = width // CH
    half = width // 2
    unit = half // U
    (core, bx, by, bz1, bz2), (pc, px, py, pz1, pz2) = neighbours(me)
    prev = lax.rem(me + n - 1, n)
    nxt = lax.rem(me + 1, n)
    first = [px * (1 - core) + py * core, py * (1 - core) + px * core]
    fbit = [bx * (1 - core) + by * core, by * (1 - core) + bx * core]
    second = [first[1], first[0]]
    sbit = [fbit[1], fbit[0]]

    barrier = pltpu.get_barrier_semaphore()
    for p in (pc, px, py, pz1, pz2, prev, nxt):
        pl.semaphore_signal(barrier, inc=1, device_id=(p,), device_id_type=MESH)

    def local(src, dst, sem):
        return pltpu.make_async_copy(src, dst, sem)

    def cols(k):
        return pl.ds(pl.multiple_of(k * CH, CH), CH)

    def slot_rows(s):
        return pl.ds(pl.multiple_of(s * rows, 16), rows)

    def x_in(s):
        return local(x.at[slot_rows(s)], xr.at[s, pl.ds(0, rows)], xsem.at[s])

    def w_in(k):
        return local(w.at[:, cols(k)], w_v.at[:, cols(k)], wsem.at[k])

    def cot_in(k):
        return local(cot.at[:, cols(k)], cot_v.at[k % 2], csem.at[k % 2])

    small = [
        local(src, dst, tsem.at[i])
        for i, (src, dst) in enumerate(
            (
                (rims, rims_v),
                (seg, seg_v),
                (offs, offs_v),
                (marks, marks_v),
                (edges, edges_v),
                (edge_marks, emarks_v),
                (bias, bias_v),
            )
        )
    ]
    small[0].start()
    x_in(0).start()
    x_in(slots - 1).start()
    for c in small[1:]:
        c.start()
    for s in range(1, slots - 1):
        x_in(s).start()
    w_in(0).start()
    cot_in(0).start()
    cot_in(1).start()
    for k in range(1, nch):
        w_in(k).start()

    def offer(s):
        picks = jnp.concatenate([rims_v[s, 0:1, :], rims_v[s, 1:2, :]], axis=1)
        order = lax.broadcasted_iota(jnp.int32, (rows, 2 * rim), 0)
        ot[s] = jnp.where(order == picks, 1.0, 0.0).astype(bf16)
        dims = (((0,), (0,)), ((), ()))
        return lax.dot_general(
            ot[s], xr[s, pl.ds(0, rows), :], dims, preferred_element_type=f32
        ).astype(bf16)

    def halo_send(j):
        s, to = ((0, nxt), (slots - 1, prev))[j]
        dst = xr.at[s, pl.ds(rows + rim * j, rim)]
        return pltpu.make_async_remote_copy(
            hs.at[j], dst, hsem.at[j], hrsem.at[j], device_id=(to,), device_id_type=MESH
        )

    def back_send(j):
        to = (prev, nxt)[j]
        return pltpu.make_async_remote_copy(
            hs.at[2 + j], hr.at[j], hsem.at[2 + j], hrsem.at[2 + j],
            device_id=(to,), device_id_type=MESH,
        )

    small[0].wait()
    x_in(0).wait()
    out = offer(0)
    hs[1] = out[:rim]
    xr[1, pl.ds(rows, rim), :] = out[rim:]
    x_in(slots - 1).wait()
    out = offer(slots - 1)
    hs[0] = out[rim:]
    xr[slots - 2, pl.ds(rows + rim, rim), :] = out[:rim]
    pl.semaphore_wait(barrier, 7)
    halo_send(0).start()
    halo_send(1).start()
    for c in small[1:]:
        c.wait()
    for s in range(1, slots - 1):
        x_in(s).wait()
        out = offer(s)
        xr[s - 1, pl.ds(rows + rim, rim), :] = out[:rim]
        xr[s + 1, pl.ds(rows, rim), :] = out[rim:]

    def tables(s, carry):
        seg_r = seg_v[pl.ds(s, 1), :].astype(f32)
        ri = lax.broadcasted_iota(jnp.int32, (rows, rows), 0)
        ci = lax.broadcasted_iota(jnp.int32, (rows, rows), 1)
        diag = ri == ci
        seg_c = jnp.sum(jnp.where(diag, seg_r, 0.0), axis=1, keepdims=True)
        start = jnp.sum(jnp.where(seg_r < seg_c, 1.0, 0.0), axis=1, keepdims=True)
        same = seg_r == seg_c
        size = jnp.sum(jnp.where(same, 1.0, 0.0), axis=0, keepdims=True)
        off = offs_v[s].astype(f32)
        rest = off - jnp.floor((off + 0.5) * (1.0 / size)) * size
        rest = jnp.where(rest < 0.0, rest + size, rest)
        rest = jnp.where(rest >= size, rest - size, rest)
        marked = marks_v[s]
        pick = jnp.where(marked == 1, rest.astype(jnp.int32), 200)
        qv[...] = pick >> 2
        vv[...] = 1 << ((pick & 3) << 3)
        q = lax.broadcasted_iota(jnp.int32, (Q, rows), 0)
        packed = jnp.zeros((Q, rows), jnp.int32)
        for k in range(near):
            packed = packed + jnp.where(qv[k : k + 1, :] == q, vv[k : k + 1, :], 0)
        counts = jnp.concatenate(
            [((packed >> (8 * r)) & 255).astype(f32) for r in range(4)], axis=0
        ).astype(bf16)
        rel = lax.broadcasted_iota(jnp.int32, (rows, 1), 0) - start.astype(jnp.int32)
        place = (rel & 3) * Q + (rel >> 2)
        lanes = lax.broadcasted_iota(jnp.int32, (rows, 4 * Q), 1)
        spread = jnp.where(lanes == place, 1.0, 0.0).astype(bf16)
        around = jnp.dot(spread, counts, preferred_element_type=f32)
        around = jnp.where(same, around, 0.0) + jnp.where(diag, 2.0, 0.0)
        kt[s, pl.ds(0, rows), :] = around.astype(bf16)
        degree = jnp.sum(marked, axis=0, keepdims=True)
        r = lax.broadcasted_iota(jnp.int32, (rim, rows), 0)
        for j in range(2):
            hot = emarks_v[s, j]
            degree = degree + jnp.sum(hot, axis=0, keepdims=True)
            pick = jnp.where(hot == 1, edges_v[s, j], 200)
            far = jnp.zeros((rim, rows), f32)
            for k in range(halo):
                far = far + jnp.where(pick[k : k + 1, :] == r, 1.0, 0.0)
            kt[s, pl.ds(rows + rim * j, rim), :] = far.astype(bf16)
        degree = jnp.sum(jnp.where(diag, degree.astype(f32), 0.0), axis=1, keepdims=True)
        sc[slot_rows(s), :] = 1.0 / (1.0 + degree)
        return carry

    lax.fori_loop(0, slots, tables, 0)

    def mix(s):
        d = slot_rows(s)
        dims = (((0,), (0,)), ((), ()))
        for j in range(4):
            c = pl.ds(j * (width // 4), width // 4)
            summed = lax.dot_general(kt[s], xr[s, :, c], dims, preferred_element_type=f32)
            mixed_v[d, c] = (sc[d, :] * summed).astype(bf16)

    for s in range(1, slots - 1):
        mix(s)
    halo_send(0).wait_recv()
    halo_send(1).wait_recv()
    mix(0)
    mix(slots - 1)

    def remote(src, dst, k, s, to):
        return pltpu.make_async_remote_copy(
            src, dst, ssem.at[k, s], rsem.at[k, s], device_id=(to,), device_id_type=MESH
        )

    def at(u, level, flip=False, base=0):
        r = base + unit * u
        size = unit
        picks = [bz1, sbit[u % 2]]
        for j in range(level):
            size = size // 2
            b = picks[j]
            if flip and j == level - 1:
                b = 1 - b
            r = r + size * b
        return pl.ds(pl.multiple_of(r, 16), size)

    def part(k, j, u, level, flip=False):
        return ag.at[2 * k + j, at(u, level, flip, half * core)]

    def c_rs(k, u):
        return remote(snd.at[k % 2, :, at(u, 0)], rc.at[k % 4, :, at(u, 0)], k, u, pc)

    def f_rs(k, u):
        return remote(fb.at[k % 2, u], rf.at[k, u], k, U + u, first[u % 2])

    def a_rs(k, u):
        return remote(ab.at[k % 2, u], ra.at[k, u], k, 2 * U + u, pz1)

    def s_rs(k, u):
        return remote(sb.at[k % 2, u], rs.at[k, u], k, 3 * U + u, second[u % 2])

    def b_rs(k, u):
        return remote(part(k, fbit[u % 2], u, 2), rb.at[k, u], k, 4 * U + u, pz2)

    def s_ag(k, u):
        p = part(k, fbit[u % 2], u, 2)
        return remote(p, p, k, 5 * U + u, second[u % 2])

    def a_ag(k, u):
        p = part(k, fbit[u % 2], u, 1)
        return remote(p, p, k, 6 * U + u, pz1)

    def f_ag(k, u):
        p = part(k, fbit[u % 2], u, 0)
        return remote(p, p, k, 7 * U + u, first[u % 2])

    def c_ag(k, u):
        p = ag.at[pl.ds(2 * k, 2), at(u, 0, False, half * core)]
        return remote(p, p, k, 8 * U + u, pc)

    def free(send, k, u):
        @pl.when(k >= 2)
        def _():
            send(k - 2, u).wait_send()

    def fold_core(k, u):
        f = fbit[u % 2]
        free(f_rs, k, u)
        fb[k % 2, u] = part(k, 1 - f, u, 0)[...] + rc[k % 4, 1 - f, at(u, 0)]
        p = part(k, f, u, 0)
        p[...] = p[...] + rc[k % 4, f, at(u, 0)]

    def fold(level, buf, out, send, pick):
        def run(k, u):
            f = fbit[u % 2]
            bit = pick(u)
            size = (unit >> level) // 2
            free(send, k, u)
            away = pl.ds(pl.multiple_of(size * (1 - bit), 16), size)
            stay = pl.ds(pl.multiple_of(size * bit, 16), size)
            out[k % 2, u] = part(k, f, u, level + 1, True)[...] + buf[k, u, away]
            p = part(k, f, u, level + 1)
            p[...] = p[...] + buf[k, u, stay]

        return run

    def whole(buf):
        def run(k, u):
            p = part(k, fbit[u % 2], u, 2)
            p[...] = p[...] + buf[k, u]

        return run

    def last_fold(k, u):
        b_rs(k, u).wait_send()
        whole(rb)(k, u)

    hops = [
        (c_rs, fold_core, f_rs),
        (f_rs, fold(0, rf, ab, a_rs, lambda u: bz1), a_rs),
        (a_rs, fold(1, ra, sb, s_rs, lambda u: sbit[u % 2]), s_rs),
        (s_rs, whole(rs), b_rs),
        (b_rs, last_fold, s_ag),
        (s_ag, None, a_ag),
        (a_ag, None, f_ag),
        (f_ag, None, c_ag),
        (c_ag, None, None),
    ]

    def serve(t, v, order):
        for h in order:
            took, work, send = hops[h]
            back = v - DELAY[h]
            k = t + back // U
            u = back % U

            @pl.when((k >= 0) & (k < nch))
            def _():
                took(k, u).wait_recv()
                if work is not None:
                    work(k, u)
                if send is not None:
                    send(k, u).start()

    def pre_part(k, m):
        mt = total // 2
        d = pl.ds(m * mt, mt)
        b = bias_v[:, cols(k)]
        pre = jnp.dot(mixed_v[d, :], w_v[:, cols(k)], preferred_element_type=f32) + b
        sig = 0.5 * jnp.tanh(0.5 * pre) + 0.5
        out = pre * sig
        act[d, cols(k)] = out.astype(bf16)
        g = (cot_v[k % 2, d, :].astype(f32) * (sig + out * (1.0 - sig))).astype(bf16)
        gp_v[d, cols(k)] = g
        sums = jnp.sum(g.astype(f32), axis=0, keepdims=True)
        if m:
            sums = sums + gb_v[0, :, cols(k)]
        gb_v[0, :, cols(k)] = sums

    def grad_part(k, side):
        start = pl.multiple_of(half * side, half)
        dims = (((0,), (0,)), ((), ()))
        return lax.dot_general(
            mixed_v[:, pl.ds(start, half)], gp_v[:, cols(k)], dims, preferred_element_type=f32
        )

    def there(k):
        grad = grad_part(k, 1 - core)
        snd[k % 2, 0] = grad[:, :H].astype(bf16)
        snd[k % 2, 1] = grad[:, H:].astype(bf16)

    def here(k):
        grad = grad_part(k, core)
        own = pl.ds(pl.multiple_of(half * core, half), half)
        ag[2 * k, own] = grad[:, :H].astype(bf16)
        ag[2 * k + 1, own] = grad[:, H:].astype(bf16)

    def early(t, more):
        serve(t, 0, ORDER)
        serve(t, 1, ORDER)

        @pl.when(t >= 2)
        def _():
            for u in range(U):
                c_rs(t - 2, u).wait_send()

        if more:
            w_in(t + 1).wait()
            cot_in(t + 1).wait()

        there(t)
        if more:
            pre_part(t + 1, 0)
        for u in range(U):
            c_rs(t, u).start()
        serve(t, 2, ORDER)
        serve(t, 3, ORDER)
        here(t)
        if more:
            pre_part(t + 1, 1)

            @pl.when(t + 2 < nch)
            def _():
                cot_in(t + 2).start()

    w_in(0).wait()
    cot_in(0).wait()
    pre_part(0, 0)
    pre_part(0, 1)

    def early_step(t, carry):
        early(t, True)
        return carry

    lax.fori_loop(0, nch - 1, early_step, 0)
    early(nch - 1, False)

    def bias_hop(j):
        to = pc
        for i, p in enumerate((px, py, pz1, pz2)):
            to = jnp.where(j == i + 1, p, to)
        return pltpu.make_async_remote_copy(
            gb_v.at[j], gr.at[j], bsem.at[j], brsem.at[j], device_id=(to,), device_id_type=MESH
        )

    def bias_step(i):
        @pl.when((i >= 1) & (i <= 5))
        def _():
            bias_hop(i - 1).wait_recv()
            gb_v[i] = gb_v[i - 1] + gr[i - 1]

        @pl.when(i < 5)
        def _():
            bias_hop(i).start()

    def late_mixed(i, carry):
        bias_step(i)
        s = jnp.where(i == 0, 0, jnp.where(i == 1, slots - 1, i - 1))
        d = slot_rows(s)
        tile = width // 4
        for v in range(U):
            serve(nch + i, v, ORDER)
            c = pl.ds(v * tile, tile)
            dims = (((1,), (1,)), ((), ()))
            back = lax.dot_general(gp_v[d, :], w_v[c, :], dims, preferred_element_type=f32)
            mixed_v[d, c] = (sc[d, :] * back).astype(bf16)
        out = jnp.dot(
            kt[s, pl.ds(rows, 2 * rim), :], mixed_v[d, :], preferred_element_type=f32
        ).astype(bf16)

        @pl.when(s > 0)
        def _():
            xr[s - 1, pl.ds(rows + rim, rim), :] = out[:rim]

        @pl.when(s < slots - 1)
        def _():
            xr[s + 1, pl.ds(rows, rim), :] = out[rim:]

        @pl.when(s == 0)
        def _():
            hs[2] = out[:rim]
            back_send(0).start()

        @pl.when(s == slots - 1)
        def _():
            hs[3] = out[rim:]
            back_send(1).start()

        return carry

    lax.fori_loop(0, slots, late_mixed, 0)
    back_send(0).wait_recv()
    back_send(1).wait_recv()
    xr[slots - 1, pl.ds(rows + rim, rim), :] = hr[0]
    xr[0, pl.ds(rows, rim), :] = hr[1]

    def late_features(s, carry):
        bias_step(s + slots)
        d = slot_rows(s)
        tile = width // 4
        for v in range(U):
            serve(nch + slots + s, v, ORDER)
            c = pl.ds(v * tile, tile)
            grad = jnp.dot(kt[s, pl.ds(0, rows), :], mixed_v[d, c], preferred_element_type=f32)
            grad = grad + jnp.dot(
                ot[s], xr[s, pl.ds(rows, 2 * rim), c], preferred_element_type=f32
            )
            xr[s, pl.ds(0, rows), c] = grad.astype(bf16)
        return carry

    lax.fori_loop(0, slots, late_features, 0)

    def late(t, carry):
        for v in range(U):
            serve(t, v, ORDER)
        return carry

    lax.fori_loop(nch + 2 * slots, nch + (DELAY[-1] + U - 1) // U + 1, late, 0)
    gb[...] = gb_v[5]
    for j in range(5):
        bias_hop(j).wait_send()
    for j in range(2):
        halo_send(j).wait_send()
        back_send(j).wait_send()
    for k in range(nch - 2, nch):
        for u in range(U):
            for f in (c_rs, f_rs, a_rs, s_rs):
                f(k, u).wait_send()

    def finish(k, carry):
        for u in range(U):
            for f in (s_ag, a_ag, f_ag, c_ag):
                f(k, u).wait_send()
        return carry

    lax.fori_loop(0, nch, finish, 0)


U = 4
Q = 24
DELAY = [4 + 4 * h for h in range(9)]
ORDER = list(range(8, -1, -1))


def main_call(features, weight, bias, cot, seg, offs, marks, edges, edge_marks, rims):
    slots, rows = seg.shape
    total, width = cot.shape
    rim = rims.shape[2]
    nch = width // CH
    half = width // 2
    unit = half // U
    any_ = pl.BlockSpec(memory_space=pl.ANY)
    dma = pltpu.SemaphoreType.DMA
    i32 = jnp.int32
    return pl.pallas_call(
        main_kernel,
        out_shape=(
            pltpu.VMEM((total, width), bf16),
            pltpu.VMEM((slots, rows + 2 * rim, width), bf16),
            pltpu.VMEM((2 * nch, width, H), bf16),
            pltpu.VMEM((1, width), f32),
        ),
        in_specs=[any_] * 10,
        out_specs=[pl.BlockSpec(memory_space=pltpu.VMEM)] * 4,
        scratch_shapes=[
            pltpu.VMEM((slots, rows + 2 * rim, rows), bf16),
            pltpu.VMEM((slots, rows, 2 * rim), bf16),
            pltpu.VMEM((total, 1), f32),
            pltpu.VMEM((total, width), bf16),
            pltpu.VMEM((width, width), bf16),
            pltpu.VMEM((1, width), f32),
            pltpu.VMEM((2, total, CH), bf16),
            pltpu.VMEM((total, width), bf16),
            pltpu.VMEM(seg.shape, i32),
            pltpu.VMEM(offs.shape, i32),
            pltpu.VMEM(marks.shape, i32),
            pltpu.VMEM(edges.shape, i32),
            pltpu.VMEM(edge_marks.shape, i32),
            pltpu.VMEM(rims.shape, i32),
            pltpu.VMEM((offs.shape[1], rows), i32),
            pltpu.VMEM((offs.shape[1], rows), i32),
            pltpu.VMEM((4, rim, width), bf16),
            pltpu.VMEM((2, rim, width), bf16),
            pltpu.VMEM((2, 2, half, H), bf16),
            pltpu.VMEM((4, 2, half, H), bf16),
            pltpu.VMEM((2, U, unit, H), bf16),
            pltpu.VMEM((nch, U, unit, H), bf16),
            pltpu.VMEM((2, U, unit // 2, H), bf16),
            pltpu.VMEM((nch, U, unit // 2, H), bf16),
            pltpu.VMEM((2, U, unit // 4, H), bf16),
            pltpu.VMEM((nch, U, unit // 4, H), bf16),
            pltpu.VMEM((nch, U, unit // 4, H), bf16),
            pltpu.VMEM((6, 1, width), f32),
            pltpu.VMEM((5, 1, width), f32),
            dma((slots,)),
            dma((7,)),
            dma((nch,)),
            dma((2,)),
            dma((nch, 9 * U)),
            dma((nch, 9 * U)),
            dma((5,)),
            dma((5,)),
            dma((4,)),
            dma((4,)),
        ],
        compiler_params=pltpu.CompilerParams(
            collective_id=0, has_side_effects=True, vmem_limit_bytes=40 << 20
        ),
        name="layer",
    )(features, weight, bias, cot, seg, offs, marks, edges, edge_marks, rims)


def finish_kernel(act, xr, ag, gb, act_o, gf_o, gw_o, gb_o, stage, sem, ssem):
    slots, rows, _ = gf_o.shape
    step = stage.shape[1]
    plain = [(gb, gb_o), (act, act_o)]
    plain += [(xr.at[s, pl.ds(0, rows)], gf_o.at[s]) for s in range(slots)]
    plain = [pltpu.make_async_copy(a, b, sem.at[i]) for i, (a, b) in enumerate(plain)]

    def out(i):
        return pltpu.make_async_copy(
            stage.at[i % 2], gw_o.at[pl.ds(i * step, step)], ssem.at[i % 2]
        )

    steps = gw_o.shape[0] // step
    for i in range(steps):
        if i >= 2:
            out(i - 2).wait()
        for j in range(ag.shape[0]):
            stage[i % 2, :, j * H : (j + 1) * H] = ag[j, i * step : (i + 1) * step].astype(f32)
        out(i).start()
        if i == 0:
            for c in plain:
                c.start()
    out(steps - 2).wait()
    out(steps - 1).wait()
    for c in plain:
        c.wait()


def finish(act, xr, ag, gb, rows):
    slots, _, width = xr.shape
    vmem = pl.BlockSpec(memory_space=pltpu.VMEM)
    any_ = pl.BlockSpec(memory_space=pl.ANY)
    return pl.pallas_call(
        finish_kernel,
        out_shape=(
            jax.ShapeDtypeStruct(act.shape, bf16),
            jax.ShapeDtypeStruct((slots, rows, width), bf16),
            jax.ShapeDtypeStruct((width, width), f32),
            jax.ShapeDtypeStruct((1, width), f32),
        ),
        in_specs=[vmem] * 4,
        out_specs=[any_] * 4,
        scratch_shapes=[
            pltpu.VMEM((2, 256, width), f32),
            pltpu.SemaphoreType.DMA((2 + slots,)),
            pltpu.SemaphoreType.DMA((2,)),
        ],
        compiler_params=pltpu.CompilerParams(vmem_limit_bytes=6 << 20),
        name="finish",
    )(act, xr, ag, gb)


def passed_along(value, axis, steps):
    count = lax.axis_size(axis)
    pairs = [(source, (source + steps) % count) for source in range(count)]
    return lax.ppermute(value, axis, pairs)


def tables(seg, offsets, marks, edges, edge_marks, rim):
    slots, rows = seg.shape
    order = jnp.arange(rows, dtype=jnp.int32)
    same = seg[:, :, None] == seg[:, None, :]
    start = jnp.min(jnp.where(same, order, rows), axis=2)
    extent = jnp.sum(same.astype(jnp.int32), axis=2)
    picks = jnp.where(marks == 1, offsets % extent[:, :, None], -1)
    lanes = jnp.arange(128, dtype=jnp.int32)
    near = jnp.sum((picks[:, :, :, None] == lanes).astype(f32), axis=2).astype(bf16)
    spread = (lanes[None, :, None] == (order - start)[:, None, :]).astype(bf16)
    local = jnp.einsum("sio,soj->sij", near, spread, preferred_element_type=f32)
    local = jnp.where(same, local, 0.0) + 2.0 * (order[:, None] == order[None, :])
    joined = jnp.concatenate([edges[:, 0], edges[:, 1] + rim], axis=2)
    joined_marks = jnp.concatenate([edge_marks[:, 0], edge_marks[:, 1]], axis=2)
    cols = jnp.arange(2 * rim, dtype=jnp.int32)
    far = jnp.sum(jnp.where(joined[..., None] == cols, joined_marks[..., None], 0), axis=2)
    degree = jnp.sum(marks, axis=2) + jnp.sum(joined_marks, axis=2)
    return local.astype(bf16), far.astype(bf16), 1.0 / (1.0 + degree.astype(f32))


def spread_out(
    features,
    weight,
    bias,
    cotangent,
    segment_ids,
    neighbour_offsets,
    neighbour_mask,
    halo_edges,
    halo_mask,
    boundary_rows,
):
    slots, rows, width = features.shape
    rim = boundary_rows.shape[2]
    local_counts, halo_counts, scale = tables(
        segment_ids, neighbour_offsets, neighbour_mask, halo_edges, halo_mask, rim
    )
    chosen = (boundary_rows[..., None] == jnp.arange(rows, dtype=jnp.int32)).astype(bf16)
    sent = jnp.einsum("sjbr,srf->sjbf", chosen, features, preferred_element_type=f32).astype(bf16)
    from_prev = passed_along(sent[slots - 1, 1], "blk", 1)
    from_next = passed_along(sent[0, 0], "blk", -1)
    before = jnp.concatenate([from_prev[None], sent[: slots - 1, 1]], axis=0)
    after = jnp.concatenate([sent[1:, 0], from_next[None]], axis=0)
    received = jnp.concatenate([before, after], axis=1)
    summed = jnp.einsum("srk,skf->srf", local_counts, features, preferred_element_type=f32)
    summed = summed + jnp.einsum("srk,skf->srf", halo_counts, received, preferred_element_type=f32)
    mixed = (scale[:, :, None] * summed).astype(bf16).reshape(slots * rows, width)
    incoming = cotangent.reshape(slots * rows, width)
    pre = jnp.dot(mixed, weight, preferred_element_type=f32) + bias[None, :]
    sigma = jax.nn.sigmoid(pre)
    activations = (pre * sigma).astype(bf16)
    grad_pre = (incoming.astype(f32) * (sigma * (1.0 + pre * (1.0 - sigma)))).astype(bf16)
    bias_term = jnp.sum(grad_pre, axis=0, dtype=f32)
    weight_term = lax.dot_general(
        mixed, grad_pre, (((0,), (0,)), ((), ())), preferred_element_type=f32
    )
    grad_weight, grad_bias = lax.psum((weight_term, bias_term), "blk")
    grad_mixed = lax.dot_general(
        grad_pre, weight, (((1,), (1,)), ((), ())), preferred_element_type=f32
    )
    grad_summed = (scale.reshape(-1)[:, None] * grad_mixed).astype(bf16)
    grad_summed = grad_summed.reshape(slots, rows, width)
    grad_received = jnp.einsum(
        "srk,srf->skf", halo_counts, grad_summed, preferred_element_type=f32
    ).astype(bf16)
    toward_prev = grad_received[:, :rim]
    toward_next = grad_received[:, rim:]
    back_prev = passed_along(toward_next[slots - 1], "blk", 1)
    back_next = passed_along(toward_prev[0], "blk", -1)
    grad_first = jnp.concatenate([back_prev[None], toward_next[: slots - 1]], axis=0)
    grad_second = jnp.concatenate([toward_prev[1:], back_next[None]], axis=0)
    grad_sent = jnp.stack([grad_first, grad_second], axis=1)
    grad_features = jnp.einsum(
        "srk,srf->skf", local_counts, grad_summed, preferred_element_type=f32
    ) + jnp.einsum("sjbr,sjbf->srf", chosen, grad_sent, preferred_element_type=f32)
    return (
        activations.reshape(slots, rows, width),
        grad_features.astype(bf16),
        grad_weight,
        grad_bias,
    )


def per_device(
    features,
    weight,
    bias,
    cotangent,
    segment_ids,
    neighbour_offsets,
    neighbour_mask,
    halo_edges,
    halo_mask,
    boundary_rows,
):
    operands = (
        segment_ids,
        neighbour_offsets,
        neighbour_mask,
        halo_edges,
        halo_mask,
        boundary_rows,
    )
    if lax.axis_size("blk") != 32:
        return spread_out(features, weight, bias, cotangent, *operands)
    slots, rows, width = features.shape
    flat = (slots * rows, width)
    held = main_call(
        features.reshape(flat),
        weight,
        bias.reshape(1, width),
        cotangent.reshape(flat),
        segment_ids,
        jnp.swapaxes(neighbour_offsets, 1, 2),
        jnp.swapaxes(neighbour_mask, 1, 2),
        jnp.swapaxes(halo_edges, 2, 3),
        jnp.swapaxes(halo_mask, 2, 3),
        boundary_rows,
    )
    activations, grad_features, grad_weight, grad_bias = finish(*held, rows)
    return (
        activations.reshape(features.shape),
        grad_features,
        grad_weight,
        grad_bias.reshape(-1),
    )


def solution(mesh):
    in_specs = (
        P("blk", None, None),
        P(),
        P(),
        P("blk", None, None),
        P("blk", None),
        P("blk", None, None),
        P("blk", None, None),
        P("blk", None, None, None),
        P("blk", None, None, None),
        P("blk", None, None),
    )
    out_specs = (P("blk", None, None), P("blk", None, None), P(), P())
    return jax.shard_map(
        per_device, mesh=mesh, in_specs=in_specs, out_specs=out_specs, check_vma=False
    )
```

```python
import functools

import jax
import jax.numpy as jnp
from jax import lax
from jax.experimental import pallas as pl
from jax.experimental.pallas import tpu as pltpu
from jax.sharding import PartitionSpec as P

bf16 = jnp.bfloat16
f32 = jnp.float32
MESH = pl.DeviceIdType.MESH
CH = 256
H = 128


def neighbours(me):
    core = me % 2
    bits = [core, (me // 2) % 2, (me // 4) % 2, (me // 8) % 2, me // 16]
    return bits, [me + (1 << i) - (2 << i) * b for i, b in enumerate(bits)]


def main_kernel(
    x, w, bias, cot, seg, offs, marks, edges, edge_marks, rims,
    act, xr, ag, gb,
    kt, ot, sc, mixed_v, w_v, bias_v, cot_v, gp_v,
    seg_v, offs_v, marks_v, edges_v, emarks_v, rims_v, qv, vv, hs, hr,
    snd, rc, fb, rf, ab, ra, sb, rs, rb, gb_v, gr,
    xsem, tsem, wsem, csem, ssem, rcsem, rsem, bsem, brsem, hsem, hrsem,
):
    n = lax.axis_size("blk")
    me = lax.axis_index("blk")
    slots, deep, width = xr.shape
    rows = kt.shape[2]
    rim = rims_v.shape[2]
    near = offs_v.shape[1]
    halo = edges_v.shape[2]
    total = slots * rows
    nch = width // CH
    half = width // 2
    unit = half // U
    (core, bx, by, bz1, bz2), (pc, px, py, pz1, pz2) = neighbours(me)
    prev = lax.rem(me + n - 1, n)
    nxt = lax.rem(me + 1, n)
    first = [px * (1 - core) + py * core, py * (1 - core) + px * core]
    fbit = [bx * (1 - core) + by * core, by * (1 - core) + bx * core]
    second = [first[1], first[0]]
    sbit = [fbit[1], fbit[0]]

    barrier = pltpu.get_barrier_semaphore()
    for p in (pc, px, py, pz1, pz2, prev, nxt):
        pl.semaphore_signal(barrier, inc=1, device_id=(p,), device_id_type=MESH)

    def local(src, dst, sem):
        return pltpu.make_async_copy(src, dst, sem)

    def cols(k):
        return pl.ds(pl.multiple_of(k * CH, CH), CH)

    def slot_rows(s):
        return pl.ds(pl.multiple_of(s * rows, 16), rows)

    def x_in(s):
        return local(x.at[slot_rows(s)], xr.at[s, pl.ds(0, rows)], xsem.at[s])

    def w_in(k):
        return local(w.at[:, cols(k)], w_v.at[:, cols(k)], wsem.at[k])

    def cot_in(k):
        return local(cot.at[:, cols(k)], cot_v.at[k % 2], csem.at[k % 2])

    small = [
        local(src, dst, tsem.at[i])
        for i, (src, dst) in enumerate(
            (
                (rims, rims_v),
                (seg, seg_v),
                (offs, offs_v),
                (marks, marks_v),
                (edges, edges_v),
                (edge_marks, emarks_v),
                (bias, bias_v),
            )
        )
    ]
    small[0].start()
    x_in(0).start()
    x_in(slots - 1).start()
    for c in small[1:]:
        c.start()
    for s in range(1, slots - 1):
        x_in(s).start()

    def offer(s):
        picks = jnp.concatenate([rims_v[s, 0:1, :], rims_v[s, 1:2, :]], axis=1)
        order = lax.broadcasted_iota(jnp.int32, (rows, 2 * rim), 0)
        ot[s] = jnp.where(order == picks, 1.0, 0.0).astype(bf16)
        dims = (((0,), (0,)), ((), ()))
        return lax.dot_general(
            ot[s], xr[s, pl.ds(0, rows), :], dims, preferred_element_type=f32
        ).astype(bf16)

    def halo_send(j):
        s, to = ((0, nxt), (slots - 1, prev))[j]
        dst = xr.at[s, pl.ds(rows + rim * j, rim)]
        return pltpu.make_async_remote_copy(
            hs.at[j], dst, hsem.at[j], hrsem.at[j], device_id=(to,), device_id_type=MESH
        )

    def back_send(j):
        to = (prev, nxt)[j]
        return pltpu.make_async_remote_copy(
            hs.at[2 + j], hr.at[j], hsem.at[2 + j], hrsem.at[2 + j],
            device_id=(to,), device_id_type=MESH,
        )

    small[0].wait()
    x_in(0).wait()
    out = offer(0)
    hs[1] = out[:rim]
    xr[1, pl.ds(rows, rim), :] = out[rim:]
    x_in(slots - 1).wait()
    out = offer(slots - 1)
    hs[0] = out[rim:]
    xr[slots - 2, pl.ds(rows + rim, rim), :] = out[:rim]
    pl.semaphore_wait(barrier, 7)
    halo_send(0).start()
    halo_send(1).start()
    w_in(0).start()
    cot_in(0).start()
    for k in range(1, nch):
        w_in(k).start()
    cot_in(1).start()
    for c in small[1:]:
        c.wait()
    for s in range(1, slots - 1):
        x_in(s).wait()
        out = offer(s)
        xr[s - 1, pl.ds(rows + rim, rim), :] = out[:rim]
        xr[s + 1, pl.ds(rows, rim), :] = out[rim:]

    def tables(s, carry):
        seg_r = seg_v[pl.ds(s, 1), :].astype(f32)
        ri = lax.broadcasted_iota(jnp.int32, (rows, rows), 0)
        ci = lax.broadcasted_iota(jnp.int32, (rows, rows), 1)
        diag = ri == ci
        seg_c = jnp.sum(jnp.where(diag, seg_r, 0.0), axis=1, keepdims=True)
        start = jnp.sum(jnp.where(seg_r < seg_c, 1.0, 0.0), axis=1, keepdims=True)
        same = seg_r == seg_c
        size = jnp.sum(jnp.where(same, 1.0, 0.0), axis=0, keepdims=True)
        off = offs_v[s].astype(f32)
        rest = off - jnp.floor((off + 0.5) * (1.0 / size)) * size
        rest = jnp.where(rest < 0.0, rest + size, rest)
        rest = jnp.where(rest >= size, rest - size, rest)
        marked = marks_v[s]
        pick = jnp.where(marked == 1, rest.astype(jnp.int32), 200)
        qv[...] = pick >> 2
        vv[...] = 1 << ((pick & 3) << 3)
        q = lax.broadcasted_iota(jnp.int32, (Q, rows), 0)
        packed = jnp.zeros((Q, rows), jnp.int32)
        for k in range(near):
            packed = packed + jnp.where(qv[k : k + 1, :] == q, vv[k : k + 1, :], 0)
        counts = jnp.concatenate(
            [((packed >> (8 * r)) & 255).astype(f32) for r in range(4)], axis=0
        ).astype(bf16)
        rel = lax.broadcasted_iota(jnp.int32, (rows, 1), 0) - start.astype(jnp.int32)
        place = (rel & 3) * Q + (rel >> 2)
        lanes = lax.broadcasted_iota(jnp.int32, (rows, 4 * Q), 1)
        spread = jnp.where(lanes == place, 1.0, 0.0).astype(bf16)
        around = jnp.dot(spread, counts, preferred_element_type=f32)
        around = jnp.where(same, around, 0.0) + jnp.where(diag, 2.0, 0.0)
        kt[s, pl.ds(0, rows), :] = around.astype(bf16)
        degree = jnp.sum(marked, axis=0, keepdims=True)
        r = lax.broadcasted_iota(jnp.int32, (rim, rows), 0)
        for j in range(2):
            hot = emarks_v[s, j]
            degree = degree + jnp.sum(hot, axis=0, keepdims=True)
            pick = jnp.where(hot == 1, edges_v[s, j], 200)
            far = jnp.zeros((rim, rows), f32)
            for k in range(halo):
                far = far + jnp.where(pick[k : k + 1, :] == r, 1.0, 0.0)
            kt[s, pl.ds(rows + rim * j, rim), :] = far.astype(bf16)
        degree = jnp.sum(jnp.where(diag, degree.astype(f32), 0.0), axis=1, keepdims=True)
        sc[slot_rows(s), :] = 1.0 / (1.0 + degree)
        return carry

    lax.fori_loop(0, slots, tables, 0, unroll=True)

    def mix(s):
        d = slot_rows(s)
        dims = (((0,), (0,)), ((), ()))
        for j in range(4):
            c = pl.ds(j * (width // 4), width // 4)
            summed = lax.dot_general(kt[s], xr[s, :, c], dims, preferred_element_type=f32)
            mixed_v[d, c] = (sc[d, :] * summed).astype(bf16)

    def pre_part(k, start, count, more):
        d = pl.ds(start, count)
        b = bias_v[:, cols(k)]
        pre = jnp.dot(mixed_v[d, :], w_v[:, cols(k)], preferred_element_type=f32) + b
        sig = 0.5 * jnp.tanh(0.5 * pre) + 0.5
        out = pre * sig
        act[d, cols(k)] = out.astype(bf16)
        g = (cot_v[k % 2, d, :].astype(f32) * (sig + out * (1.0 - sig))).astype(bf16)
        gp_v[d, cols(k)] = g
        sums = jnp.sum(g.astype(f32), axis=0, keepdims=True)
        if more:
            sums = sums + gb_v[0, :, cols(k)]
        gb_v[0, :, cols(k)] = sums

    for s in range(1, slots - 1):
        mix(s)
    w_in(0).wait()
    cot_in(0).wait()
    pre_part(0, rows, total - 2 * rows, False)
    halo_send(0).wait_recv()
    halo_send(1).wait_recv()
    mix(0)
    mix(slots - 1)
    pre_part(0, 0, rows, True)
    pre_part(0, total - rows, rows, True)

    def remote(src, dst, k, s, to):
        return pltpu.make_async_remote_copy(
            src,
            dst,
            ssem.at[k % 2, s],
            rsem.at[k % 2, s],
            device_id=(to,),
            device_id_type=MESH,
        )

    def at(u, level, flip=False, base=0):
        r = base + unit * u
        size = unit
        picks = [bz1, sbit[u % 2]]
        for j in range(level):
            size = size // 2
            b = picks[j]
            if flip and j == level - 1:
                b = 1 - b
            r = r + size * b
        return pl.ds(pl.multiple_of(r, 16), size)

    def part(k, j, u, level, flip=False):
        return ag.at[2 * k + j, at(u, level, flip, half * core)]

    def c_rs(k, u):
        return pltpu.make_async_remote_copy(
            snd.at[k % 2, :, at(u, 0)],
            rc.at[k % 4, :, at(u, 0)],
            ssem.at[k % 2, u],
            rcsem.at[k % 4, u],
            device_id=(pc,),
            device_id_type=MESH,
        )

    def f_rs(k, u):
        return remote(fb.at[k % 2, u], rf.at[k, u], k, U + u, first[u % 2])

    def a_rs(k, u):
        return remote(ab.at[k % 2, u], ra.at[k, u], k, 2 * U + u, pz1)

    def s_rs(k, u):
        return remote(sb.at[k % 2, u], rs.at[k, u], k, 3 * U + u, second[u % 2])

    def b_rs(k, u):
        return remote(part(k, fbit[u % 2], u, 2), rb.at[k, u], k, 4 * U + u, pz2)

    def s_ag(k, u):
        p = part(k, fbit[u % 2], u, 2)
        return remote(p, p, k, 5 * U + u, second[u % 2])

    def a_ag(k, u):
        p = part(k, fbit[u % 2], u, 1)
        return remote(p, p, k, 6 * U + u, pz1)

    def f_ag(k, u):
        p = part(k, fbit[u % 2], u, 0)
        return remote(p, p, k, 7 * U + u, first[u % 2])

    def c_ag(k, u):
        p = ag.at[pl.ds(2 * k, 2), at(u, 0, False, half * core)]
        return remote(p, p, k, 8 * U + u, pc)

    def free(send, k, u):
        @pl.when(k >= 2)
        def _():
            send(k - 2, u).wait_send()

    def fold_core(k, u):
        f = fbit[u % 2]
        free(f_rs, k, u)
        fb[k % 2, u] = part(k, 1 - f, u, 0)[...] + rc[k % 4, 1 - f, at(u, 0)]
        p = part(k, f, u, 0)
        p[...] = p[...] + rc[k % 4, f, at(u, 0)]

    def fold(level, buf, out, send, pick):
        def run(k, u):
            f = fbit[u % 2]
            bit = pick(u)
            size = (unit >> level) // 2
            free(send, k, u)
            away = pl.ds(pl.multiple_of(size * (1 - bit), 16), size)
            stay = pl.ds(pl.multiple_of(size * bit, 16), size)
            out[k % 2, u] = part(k, f, u, level + 1, True)[...] + buf[k, u, away]
            p = part(k, f, u, level + 1)
            p[...] = p[...] + buf[k, u, stay]

        return run

    def whole(buf):
        def run(k, u):
            p = part(k, fbit[u % 2], u, 2)
            p[...] = p[...] + buf[k, u]

        return run

    def last_fold(k, u):
        b_rs(k, u).wait_send()
        whole(rb)(k, u)

    hops = [
        (c_rs, fold_core, f_rs),
        (f_rs, fold(0, rf, ab, a_rs, lambda u: bz1), a_rs),
        (a_rs, fold(1, ra, sb, s_rs, lambda u: sbit[u % 2]), s_rs),
        (s_rs, whole(rs), b_rs),
        (b_rs, last_fold, s_ag),
        (s_ag, None, a_ag),
        (a_ag, None, f_ag),
        (f_ag, None, c_ag),
        (c_ag, None, None),
    ]

    def serve(t, v, order):
        for h in order:
            took, work, send = hops[h]
            back = v - DELAY[h]
            k = t + back // U
            u = back % U

            @pl.when((k >= 0) & (k < nch))
            def _():
                took(k, u).wait_recv()
                if work is not None:
                    work(k, u)
                if h >= 4 and send is not None:
                    free(send, k, u)
                if send is not None:
                    send(k, u).start()

    def grad_part(k, side):
        start = pl.multiple_of(half * side, half)
        dims = (((0,), (0,)), ((), ()))
        return lax.dot_general(
            mixed_v[:, pl.ds(start, half)], gp_v[:, cols(k)], dims, preferred_element_type=f32
        )

    def there(k):
        grad = grad_part(k, 1 - core)
        snd[k % 2, 0] = grad[:, :H].astype(bf16)
        snd[k % 2, 1] = grad[:, H:].astype(bf16)

    def here(k):
        grad = grad_part(k, core)
        own = pl.ds(pl.multiple_of(half * core, half), half)
        ag[2 * k, own] = grad[:, :H].astype(bf16)
        ag[2 * k + 1, own] = grad[:, H:].astype(bf16)

    def early(t, more):
        serve(t, 0, ORDER)
        serve(t, 1, ORDER)

        @pl.when(t >= 2)
        def _():
            for u in range(U):
                c_rs(t - 2, u).wait_send()

        if more:
            w_in(t + 1).wait()
            cot_in(t + 1).wait()

        there(t)
        if more:
            pre_part(t + 1, 0, total // 2, False)
        for u in range(U):
            c_rs(t, u).start()
        serve(t, 2, ORDER)
        serve(t, 3, ORDER)
        here(t)
        if more:
            pre_part(t + 1, total // 2, total // 2, True)

            @pl.when(t + 2 < nch)
            def _():
                cot_in(t + 2).start()

    def early_step(t, carry):
        early(t, True)
        return carry

    lax.fori_loop(0, nch - 1, early_step, 0)
    early(nch - 1, False)

    def bias_hop(j):
        to = pc
        for i, p in enumerate((px, py, pz1, pz2)):
            to = jnp.where(j == i + 1, p, to)
        return pltpu.make_async_remote_copy(
            gb_v.at[j], gr.at[j], bsem.at[j], brsem.at[j], device_id=(to,), device_id_type=MESH
        )

    def bias_step(i):
        @pl.when((i >= 1) & (i <= 5))
        def _():
            bias_hop(i - 1).wait_recv()
            gb_v[i] = gb_v[i - 1] + gr[i - 1]

        @pl.when(i < 5)
        def _():
            bias_hop(i).start()

    def late_mixed(i, carry):
        bias_step(i)
        s = jnp.where(i == 0, 0, jnp.where(i == 1, slots - 1, i - 1))
        d = slot_rows(s)
        tile = width // 4
        for v in range(U):
            serve(nch + i, v, ORDER)
            c = pl.ds(v * tile, tile)
            dims = (((1,), (1,)), ((), ()))
            back = lax.dot_general(gp_v[d, :], w_v[c, :], dims, preferred_element_type=f32)
            mixed_v[d, c] = (sc[d, :] * back).astype(bf16)
        out = jnp.dot(
            kt[s, pl.ds(rows, 2 * rim), :], mixed_v[d, :], preferred_element_type=f32
        ).astype(bf16)

        @pl.when(s > 0)
        def _():
            xr[s - 1, pl.ds(rows + rim, rim), :] = out[:rim]

        @pl.when(s < slots - 1)
        def _():
            xr[s + 1, pl.ds(rows, rim), :] = out[rim:]

        @pl.when(s == 0)
        def _():
            hs[2] = out[:rim]
            back_send(0).start()

        @pl.when(s == slots - 1)
        def _():
            hs[3] = out[rim:]
            back_send(1).start()

        return carry

    lax.fori_loop(0, slots, late_mixed, 0)
    back_send(0).wait_recv()
    back_send(1).wait_recv()
    xr[slots - 1, pl.ds(rows + rim, rim), :] = hr[0]
    xr[0, pl.ds(rows, rim), :] = hr[1]

    def late_features(s, carry):
        bias_step(s + slots)
        d = slot_rows(s)
        tile = width // 4
        for v in range(U):
            serve(nch + slots + s, v, ORDER)
            c = pl.ds(v * tile, tile)
            grad = jnp.dot(kt[s, pl.ds(0, rows), :], mixed_v[d, c], preferred_element_type=f32)
            grad = grad + jnp.dot(
                ot[s], xr[s, pl.ds(rows, 2 * rim), c], preferred_element_type=f32
            )
            xr[s, pl.ds(0, rows), c] = grad.astype(bf16)
        return carry

    lax.fori_loop(0, slots, late_features, 0)

    def late(t, carry):
        for v in range(U):
            serve(t, v, ORDER)
        return carry

    lax.fori_loop(nch + 2 * slots, nch + (DELAY[-1] + U - 1) // U + 1, late, 0)
    gb[...] = gb_v[5]
    for j in range(5):
        bias_hop(j).wait_send()
    for j in range(2):
        halo_send(j).wait_send()
        back_send(j).wait_send()
    for k in range(nch - 2, nch):
        for u in range(U):
            for f in (c_rs, f_rs, a_rs, s_rs, s_ag, a_ag, f_ag, c_ag):
                f(k, u).wait_send()


U = 4
Q = 24
DELAY = [4 + 4 * h for h in range(9)]
ORDER = list(range(8, -1, -1))


def main_call(features, weight, bias, cot, seg, offs, marks, edges, edge_marks, rims):
    slots, rows = seg.shape
    total, width = cot.shape
    rim = rims.shape[2]
    nch = width // CH
    half = width // 2
    unit = half // U
    any_ = pl.BlockSpec(memory_space=pl.ANY)
    dma = pltpu.SemaphoreType.DMA
    i32 = jnp.int32
    return pl.pallas_call(
        main_kernel,
        out_shape=(
            pltpu.VMEM((total, width), bf16),
            pltpu.VMEM((slots, rows + 2 * rim, width), bf16),
            pltpu.VMEM((2 * nch, width, H), bf16),
            pltpu.VMEM((1, width), f32),
        ),
        in_specs=[any_] * 10,
        out_specs=[pl.BlockSpec(memory_space=pltpu.VMEM)] * 4,
        scratch_shapes=[
            pltpu.VMEM((slots, rows + 2 * rim, rows), bf16),
            pltpu.VMEM((slots, rows, 2 * rim), bf16),
            pltpu.VMEM((total, 1), f32),
            pltpu.VMEM((total, width), bf16),
            pltpu.VMEM((width, width), bf16),
            pltpu.VMEM((1, width), f32),
            pltpu.VMEM((2, total, CH), bf16),
            pltpu.VMEM((total, width), bf16),
            pltpu.VMEM(seg.shape, i32),
            pltpu.VMEM(offs.shape, i32),
            pltpu.VMEM(marks.shape, i32),
            pltpu.VMEM(edges.shape, i32),
            pltpu.VMEM(edge_marks.shape, i32),
            pltpu.VMEM(rims.shape, i32),
            pltpu.VMEM((offs.shape[1], rows), i32),
            pltpu.VMEM((offs.shape[1], rows), i32),
            pltpu.VMEM((4, rim, width), bf16),
            pltpu.VMEM((2, rim, width), bf16),
            pltpu.VMEM((2, 2, half, H), bf16),
            pltpu.VMEM((4, 2, half, H), bf16),
            pltpu.VMEM((2, U, unit, H), bf16),
            pltpu.VMEM((nch, U, unit, H), bf16),
            pltpu.VMEM((2, U, unit // 2, H), bf16),
            pltpu.VMEM((nch, U, unit // 2, H), bf16),
            pltpu.VMEM((2, U, unit // 4, H), bf16),
            pltpu.VMEM((nch, U, unit // 4, H), bf16),
            pltpu.VMEM((nch, U, unit // 4, H), bf16),
            pltpu.VMEM((6, 1, width), f32),
            pltpu.VMEM((5, 1, width), f32),
            dma((slots,)),
            dma((7,)),
            dma((nch,)),
            dma((2,)),
            dma((2, 9 * U)),
            dma((4, U)),
            dma((2, 9 * U)),
            dma((5,)),
            dma((5,)),
            dma((4,)),
            dma((4,)),
        ],
        compiler_params=pltpu.CompilerParams(
            collective_id=0, has_side_effects=True, vmem_limit_bytes=40 << 20
        ),
        name="layer",
    )(features, weight, bias, cot, seg, offs, marks, edges, edge_marks, rims)


def finish_kernel(act, xr, ag, gb, act_o, gf_o, gw_o, gb_o, stage, sem, ssem):
    slots, rows, _ = gf_o.shape
    step = stage.shape[1]
    plain = [(gb, gb_o), (act, act_o)]
    plain += [(xr.at[s, pl.ds(0, rows)], gf_o.at[s]) for s in range(slots)]
    plain = [pltpu.make_async_copy(a, b, sem.at[i]) for i, (a, b) in enumerate(plain)]

    def out(i):
        return pltpu.make_async_copy(
            stage.at[i % 2], gw_o.at[pl.ds(i * step, step)], ssem.at[i % 2]
        )

    steps = gw_o.shape[0] // step
    for i in range(steps):
        if i >= 2:
            out(i - 2).wait()
        for j in range(ag.shape[0]):
            stage[i % 2, :, j * H : (j + 1) * H] = ag[j, i * step : (i + 1) * step].astype(f32)
        out(i).start()
        if i == 0:
            for c in plain:
                c.start()
    out(steps - 2).wait()
    out(steps - 1).wait()
    for c in plain:
        c.wait()


def finish(act, xr, ag, gb, rows):
    slots, _, width = xr.shape
    vmem = pl.BlockSpec(memory_space=pltpu.VMEM)
    any_ = pl.BlockSpec(memory_space=pl.ANY)
    return pl.pallas_call(
        finish_kernel,
        out_shape=(
            jax.ShapeDtypeStruct(act.shape, bf16),
            jax.ShapeDtypeStruct((slots, rows, width), bf16),
            jax.ShapeDtypeStruct((width, width), f32),
            jax.ShapeDtypeStruct((1, width), f32),
        ),
        in_specs=[vmem] * 4,
        out_specs=[any_] * 4,
        scratch_shapes=[
            pltpu.VMEM((2, 256, width), f32),
            pltpu.SemaphoreType.DMA((2 + slots,)),
            pltpu.SemaphoreType.DMA((2,)),
        ],
        compiler_params=pltpu.CompilerParams(vmem_limit_bytes=6 << 20),
        name="finish",
    )(act, xr, ag, gb)


def passed_along(value, axis, steps):
    count = lax.axis_size(axis)
    pairs = [(source, (source + steps) % count) for source in range(count)]
    return lax.ppermute(value, axis, pairs)


def tables(seg, offsets, marks, edges, edge_marks, rim):
    slots, rows = seg.shape
    order = jnp.arange(rows, dtype=jnp.int32)
    same = seg[:, :, None] == seg[:, None, :]
    start = jnp.min(jnp.where(same, order, rows), axis=2)
    extent = jnp.sum(same.astype(jnp.int32), axis=2)
    picks = jnp.where(marks == 1, offsets % extent[:, :, None], -1)
    lanes = jnp.arange(128, dtype=jnp.int32)
    near = jnp.sum((picks[:, :, :, None] == lanes).astype(f32), axis=2).astype(bf16)
    spread = (lanes[None, :, None] == (order - start)[:, None, :]).astype(bf16)
    local = jnp.einsum("sio,soj->sij", near, spread, preferred_element_type=f32)
    local = jnp.where(same, local, 0.0) + 2.0 * (order[:, None] == order[None, :])
    joined = jnp.concatenate([edges[:, 0], edges[:, 1] + rim], axis=2)
    joined_marks = jnp.concatenate([edge_marks[:, 0], edge_marks[:, 1]], axis=2)
    cols = jnp.arange(2 * rim, dtype=jnp.int32)
    far = jnp.sum(jnp.where(joined[..., None] == cols, joined_marks[..., None], 0), axis=2)
    degree = jnp.sum(marks, axis=2) + jnp.sum(joined_marks, axis=2)
    return local.astype(bf16), far.astype(bf16), 1.0 / (1.0 + degree.astype(f32))


def spread_out(
    features,
    weight,
    bias,
    cotangent,
    segment_ids,
    neighbour_offsets,
    neighbour_mask,
    halo_edges,
    halo_mask,
    boundary_rows,
):
    slots, rows, width = features.shape
    rim = boundary_rows.shape[2]
    local_counts, halo_counts, scale = tables(
        segment_ids, neighbour_offsets, neighbour_mask, halo_edges, halo_mask, rim
    )
    chosen = (boundary_rows[..., None] == jnp.arange(rows, dtype=jnp.int32)).astype(bf16)
    sent = jnp.einsum("sjbr,srf->sjbf", chosen, features, preferred_element_type=f32).astype(bf16)
    from_prev = passed_along(sent[slots - 1, 1], "blk", 1)
    from_next = passed_along(sent[0, 0], "blk", -1)
    before = jnp.concatenate([from_prev[None], sent[: slots - 1, 1]], axis=0)
    after = jnp.concatenate([sent[1:, 0], from_next[None]], axis=0)
    received = jnp.concatenate([before, after], axis=1)
    summed = jnp.einsum("srk,skf->srf", local_counts, features, preferred_element_type=f32)
    summed = summed + jnp.einsum("srk,skf->srf", halo_counts, received, preferred_element_type=f32)
    mixed = (scale[:, :, None] * summed).astype(bf16).reshape(slots * rows, width)
    incoming = cotangent.reshape(slots * rows, width)
    pre = jnp.dot(mixed, weight, preferred_element_type=f32) + bias[None, :]
    sigma = jax.nn.sigmoid(pre)
    activations = (pre * sigma).astype(bf16)
    grad_pre = (incoming.astype(f32) * (sigma * (1.0 + pre * (1.0 - sigma)))).astype(bf16)
    bias_term = jnp.sum(grad_pre, axis=0, dtype=f32)
    weight_term = lax.dot_general(
        mixed, grad_pre, (((0,), (0,)), ((), ())), preferred_element_type=f32
    )
    grad_weight, grad_bias = lax.psum((weight_term, bias_term), "blk")
    grad_mixed = lax.dot_general(
        grad_pre, weight, (((1,), (1,)), ((), ())), preferred_element_type=f32
    )
    grad_summed = (scale.reshape(-1)[:, None] * grad_mixed).astype(bf16)
    grad_summed = grad_summed.reshape(slots, rows, width)
    grad_received = jnp.einsum(
        "srk,srf->skf", halo_counts, grad_summed, preferred_element_type=f32
    ).astype(bf16)
    toward_prev = grad_received[:, :rim]
    toward_next = grad_received[:, rim:]
    back_prev = passed_along(toward_next[slots - 1], "blk", 1)
    back_next = passed_along(toward_prev[0], "blk", -1)
    grad_first = jnp.concatenate([back_prev[None], toward_next[: slots - 1]], axis=0)
    grad_second = jnp.concatenate([toward_prev[1:], back_next[None]], axis=0)
    grad_sent = jnp.stack([grad_first, grad_second], axis=1)
    grad_features = jnp.einsum(
        "srk,srf->skf", local_counts, grad_summed, preferred_element_type=f32
    ) + jnp.einsum("sjbr,sjbf->srf", chosen, grad_sent, preferred_element_type=f32)
    return (
        activations.reshape(slots, rows, width),
        grad_features.astype(bf16),
        grad_weight,
        grad_bias,
    )


def per_device(
    features,
    weight,
    bias,
    cotangent,
    segment_ids,
    neighbour_offsets,
    neighbour_mask,
    halo_edges,
    halo_mask,
    boundary_rows,
):
    operands = (
        segment_ids,
        neighbour_offsets,
        neighbour_mask,
        halo_edges,
        halo_mask,
        boundary_rows,
    )
    if lax.axis_size("blk") != 32:
        return spread_out(features, weight, bias, cotangent, *operands)
    slots, rows, width = features.shape
    flat = (slots * rows, width)
    held = main_call(
        features.reshape(flat),
        weight,
        bias.reshape(1, width),
        cotangent.reshape(flat),
        segment_ids,
        jnp.swapaxes(neighbour_offsets, 1, 2),
        jnp.swapaxes(neighbour_mask, 1, 2),
        jnp.swapaxes(halo_edges, 2, 3),
        jnp.swapaxes(halo_mask, 2, 3),
        boundary_rows,
    )
    activations, grad_features, grad_weight, grad_bias = finish(*held, rows)
    return (
        activations.reshape(features.shape),
        grad_features,
        grad_weight,
        grad_bias.reshape(-1),
    )


def solution(mesh):
    in_specs = (
        P("blk", None, None),
        P(),
        P(),
        P("blk", None, None),
        P("blk", None),
        P("blk", None, None),
        P("blk", None, None),
        P("blk", None, None, None),
        P("blk", None, None, None),
        P("blk", None, None),
    )
    out_specs = (P("blk", None, None), P("blk", None, None), P(), P())
    return jax.shard_map(
        per_device, mesh=mesh, in_specs=in_specs, out_specs=out_specs, check_vma=False
    )
```

```python
import functools

import jax
import jax.numpy as jnp
from jax import lax
from jax.experimental import pallas as pl
from jax.experimental.pallas import tpu as pltpu
from jax.sharding import PartitionSpec as P

bf16 = jnp.bfloat16
f32 = jnp.float32
MESH = pl.DeviceIdType.MESH
CH = 256
H = 128


def neighbours(me):
    core = me % 2
    bits = [core, (me // 2) % 2, (me // 4) % 2, (me // 8) % 2, me // 16]
    return bits, [me + (1 << i) - (2 << i) * b for i, b in enumerate(bits)]


def main_kernel(
    x, w, bias, cot, seg, offs, marks, edges, edge_marks, rims,
    act, xr, ag, gb,
    kt, ot, sc, mixed_v, w_v, bias_v, cot_v, gp_v,
    seg_v, offs_v, marks_v, edges_v, emarks_v, rims_v, qv, vv, hs, hr,
    snd, rc, fb, rf, ab, ra, sb, rs, rb, gb_v, gr,
    xsem, tsem, wsem, csem, ssem, rcsem, rsem, bsem, brsem, hsem, hrsem,
):
    n = lax.axis_size("blk")
    me = lax.axis_index("blk")
    slots, deep, width = xr.shape
    rows = kt.shape[2]
    rim = rims_v.shape[2]
    near = offs_v.shape[1]
    halo = edges_v.shape[2]
    total = slots * rows
    nch = width // CH
    half = width // 2
    unit = half // U
    (core, bx, by, bz1, bz2), (pc, px, py, pz1, pz2) = neighbours(me)
    prev = lax.rem(me + n - 1, n)
    nxt = lax.rem(me + 1, n)
    first = [px * (1 - core) + py * core, py * (1 - core) + px * core]
    fbit = [bx * (1 - core) + by * core, by * (1 - core) + bx * core]
    second = [first[1], first[0]]
    sbit = [fbit[1], fbit[0]]

    def middle(u):
        pair = [(bz1, pz1), (sbit[u % 2], second[u % 2])]
        return pair[::-1] if u in TURNED else pair


    barrier = pltpu.get_barrier_semaphore()
    for p in (pc, px, py, pz1, pz2, prev, nxt):
        pl.semaphore_signal(barrier, inc=1, device_id=(p,), device_id_type=MESH)

    def local(src, dst, sem):
        return pltpu.make_async_copy(src, dst, sem)

    def cols(k):
        return pl.ds(pl.multiple_of(k * CH, CH), CH)

    def slot_rows(s):
        return pl.ds(pl.multiple_of(s * rows, 16), rows)

    def x_in(s):
        return local(x.at[slot_rows(s)], xr.at[s, pl.ds(0, rows)], xsem.at[s])

    def w_in(i):
        c = (pl.ds(0, CH), pl.ds(CH, width - CH))[i]
        return local(w.at[:, c], w_v.at[:, c], wsem.at[i])

    def cot_in(k):
        return local(cot.at[:, cols(k)], cot_v.at[k % 2], csem.at[k % 2])

    small = [
        local(src, dst, tsem.at[i])
        for i, (src, dst) in enumerate(
            (
                (rims, rims_v),
                (seg, seg_v),
                (offs, offs_v),
                (marks, marks_v),
                (edges, edges_v),
                (edge_marks, emarks_v),
                (bias, bias_v),
            )
        )
    ]
    small[0].start()
    x_in(0).start()
    x_in(slots - 1).start()
    for c in small[1:]:
        c.start()
    for s in range(1, slots - 1):
        x_in(s).start()

    def offer(s):
        picks = jnp.concatenate([rims_v[s, 0:1, :], rims_v[s, 1:2, :]], axis=1)
        order = lax.broadcasted_iota(jnp.int32, (rows, 2 * rim), 0)
        ot[s] = jnp.where(order == picks, 1.0, 0.0).astype(bf16)
        dims = (((0,), (0,)), ((), ()))
        return lax.dot_general(
            ot[s], xr[s, pl.ds(0, rows), :], dims, preferred_element_type=f32
        ).astype(bf16)

    def halo_send(j, q):
        s, to = ((0, nxt), (slots - 1, prev))[j]
        c = pl.ds(q * half, half)
        i = 2 * j + q
        return pltpu.make_async_remote_copy(
            hs.at[j, :, c], xr.at[s, pl.ds(rows + rim * j, rim), c], hsem.at[i], hrsem.at[i],
            device_id=(to,), device_id_type=MESH,
        )

    def back_send(j):
        to = (prev, nxt)[j]
        return pltpu.make_async_remote_copy(
            hs.at[2 + j], hr.at[j], hsem.at[4 + j], hrsem.at[4 + j],
            device_id=(to,), device_id_type=MESH,
        )

    small[0].wait()
    x_in(0).wait()
    out = offer(0)
    hs[1] = out[:rim]
    xr[1, pl.ds(rows, rim), :] = out[rim:]
    x_in(slots - 1).wait()
    out = offer(slots - 1)
    hs[0] = out[rim:]
    xr[slots - 2, pl.ds(rows + rim, rim), :] = out[:rim]
    pl.semaphore_wait(barrier, 7)
    for q in range(2):
        for j in range(2):
            halo_send(j, q).start()
    w_in(0).start()
    cot_in(0).start()
    cot_in(1).start()
    w_in(1).start()
    for c in small[1:]:
        c.wait()
    for s in range(1, slots - 1):
        x_in(s).wait()
        out = offer(s)
        xr[s - 1, pl.ds(rows + rim, rim), :] = out[:rim]
        xr[s + 1, pl.ds(rows, rim), :] = out[rim:]

    def tables(s, carry):
        seg_r = seg_v[pl.ds(s, 1), :].astype(f32)
        ri = lax.broadcasted_iota(jnp.int32, (rows, rows), 0)
        ci = lax.broadcasted_iota(jnp.int32, (rows, rows), 1)
        diag = ri == ci
        seg_c = jnp.sum(jnp.where(diag, seg_r, 0.0), axis=1, keepdims=True)
        start = jnp.sum(jnp.where(seg_r < seg_c, 1.0, 0.0), axis=1, keepdims=True)
        same = seg_r == seg_c
        size = jnp.sum(jnp.where(same, 1.0, 0.0), axis=0, keepdims=True)
        off = offs_v[s].astype(f32)
        rest = off - jnp.floor((off + 0.5) * (1.0 / size)) * size
        rest = jnp.where(rest < 0.0, rest + size, rest)
        rest = jnp.where(rest >= size, rest - size, rest)
        marked = marks_v[s]
        pick = jnp.where(marked == 1, rest.astype(jnp.int32), 200)
        qv[...] = pick >> 2
        vv[...] = 1 << ((pick & 3) << 3)
        q = lax.broadcasted_iota(jnp.int32, (Q, rows), 0)
        packed = jnp.zeros((Q, rows), jnp.int32)
        for k in range(near):
            packed = packed + jnp.where(qv[k : k + 1, :] == q, vv[k : k + 1, :], 0)
        counts = jnp.concatenate(
            [((packed >> (8 * r)) & 255).astype(f32) for r in range(4)], axis=0
        ).astype(bf16)
        rel = lax.broadcasted_iota(jnp.int32, (rows, 1), 0) - start.astype(jnp.int32)
        place = (rel & 3) * Q + (rel >> 2)
        lanes = lax.broadcasted_iota(jnp.int32, (rows, 4 * Q), 1)
        spread = jnp.where(lanes == place, 1.0, 0.0).astype(bf16)
        around = jnp.dot(spread, counts, preferred_element_type=f32)
        around = jnp.where(same, around, 0.0) + jnp.where(diag, 2.0, 0.0)
        kt[s, pl.ds(0, rows), :] = around.astype(bf16)
        degree = jnp.sum(marked, axis=0, keepdims=True)
        r = lax.broadcasted_iota(jnp.int32, (rim, rows), 0)
        for j in range(2):
            hot = emarks_v[s, j]
            degree = degree + jnp.sum(hot, axis=0, keepdims=True)
            pick = jnp.where(hot == 1, edges_v[s, j], 200)
            far = jnp.zeros((rim, rows), f32)
            for k in range(halo):
                far = far + jnp.where(pick[k : k + 1, :] == r, 1.0, 0.0)
            kt[s, pl.ds(rows + rim * j, rim), :] = far.astype(bf16)
        degree = jnp.sum(jnp.where(diag, degree.astype(f32), 0.0), axis=1, keepdims=True)
        sc[slot_rows(s), :] = 1.0 / (1.0 + degree)
        return carry

    lax.fori_loop(0, slots, tables, 0, unroll=True)

    def mix(s, tiles):
        d = slot_rows(s)
        dims = (((0,), (0,)), ((), ()))
        for j in tiles:
            c = pl.ds(j * (width // 4), width // 4)
            summed = lax.dot_general(kt[s], xr[s, :, c], dims, preferred_element_type=f32)
            mixed_v[d, c] = (sc[d, :] * summed).astype(bf16)

    def pre_part(k, start, count, more):
        d = pl.ds(start, count)
        b = bias_v[:, cols(k)]
        pre = jnp.dot(mixed_v[d, :], w_v[:, cols(k)], preferred_element_type=f32) + b
        sig = 0.5 * jnp.tanh(0.5 * pre) + 0.5
        out = pre * sig
        act[d, cols(k)] = out.astype(bf16)
        g = (cot_v[k % 2, d, :].astype(f32) * (sig + out * (1.0 - sig))).astype(bf16)
        gp_v[d, cols(k)] = g
        sums = jnp.sum(g.astype(f32), axis=0, keepdims=True)
        if more:
            sums = sums + gb_v[0, :, cols(k)]
        gb_v[0, :, cols(k)] = sums

    for s in range(1, slots - 1):
        mix(s, range(4))
    w_in(0).wait()
    cot_in(0).wait()
    pre_part(0, rows, total - 2 * rows, False)
    for q in range(2):
        for j in range(2):
            halo_send(j, q).wait_recv()
        mix(0, (2 * q, 2 * q + 1))
        mix(slots - 1, (2 * q, 2 * q + 1))
    pre_part(0, 0, rows, True)
    pre_part(0, total - rows, rows, True)

    def remote(src, dst, k, s, to):
        return pltpu.make_async_remote_copy(
            src,
            dst,
            ssem.at[k % 2, s],
            rsem.at[k % 2, s - U],
            device_id=(to,),
            device_id_type=MESH,
        )

    def at(u, level, flip=False, base=0):
        r = base + unit * u
        size = unit
        picks = [bit for bit, _ in middle(u)]
        for j in range(level):
            size = size // 2
            b = picks[j]
            if flip and j == level - 1:
                b = 1 - b
            r = r + size * b
        return pl.ds(pl.multiple_of(r, 16), size)

    def part(k, j, u, level, flip=False):
        return ag.at[2 * k + j, at(u, level, flip, half * core)]

    def c_rs(k, u):
        return pltpu.make_async_remote_copy(
            snd.at[k % 2, :, at(u, 0)],
            rc.at[k % 4, :, at(u, 0)],
            ssem.at[k % 2, u],
            rcsem.at[k % 4, u],
            device_id=(pc,),
            device_id_type=MESH,
        )

    def f_rs(k, u):
        return remote(fb.at[k % 2, u], rf.at[k, u], k, U + u, first[u % 2])

    def a_rs(k, u):
        return remote(ab.at[k % 2, u], ra.at[k, u], k, 2 * U + u, middle(u)[0][1])

    def s_rs(k, u):
        return remote(sb.at[k % 2, u], rs.at[k, u], k, 3 * U + u, middle(u)[1][1])

    def b_rs(k, u):
        return remote(part(k, fbit[u % 2], u, 2), rb.at[k, u], k, 4 * U + u, pz2)

    def s_ag(k, u):
        p = part(k, fbit[u % 2], u, 2)
        return remote(p, p, k, 5 * U + u, middle(u)[1][1])

    def a_ag(k, u):
        p = part(k, fbit[u % 2], u, 1)
        return remote(p, p, k, 6 * U + u, middle(u)[0][1])

    def f_ag(k, u):
        p = part(k, fbit[u % 2], u, 0)
        return remote(p, p, k, 7 * U + u, first[u % 2])

    def c_ag(k, u):
        p = ag.at[pl.ds(2 * k, 2), at(u, 0, False, half * core)]
        return remote(p, p, k, 8 * U + u, pc)

    def free(send, k, u):
        @pl.when(k >= 2)
        def _():
            send(k - 2, u).wait_send()

    def fold_core(k, u):
        f = fbit[u % 2]
        free(f_rs, k, u)
        fb[k % 2, u] = part(k, 1 - f, u, 0)[...] + rc[k % 4, 1 - f, at(u, 0)]
        p = part(k, f, u, 0)
        p[...] = p[...] + rc[k % 4, f, at(u, 0)]

    def fold(level, buf, out, send):
        def run(k, u):
            f = fbit[u % 2]
            bit = middle(u)[level][0]
            size = (unit >> level) // 2
            free(send, k, u)
            away = pl.ds(pl.multiple_of(size * (1 - bit), 16), size)
            stay = pl.ds(pl.multiple_of(size * bit, 16), size)
            out[k % 2, u] = part(k, f, u, level + 1, True)[...] + buf[k, u, away]
            p = part(k, f, u, level + 1)
            p[...] = p[...] + buf[k, u, stay]

        return run

    def whole(buf):
        def run(k, u):
            p = part(k, fbit[u % 2], u, 2)
            p[...] = p[...] + buf[k, u]

        return run

    def last_fold(k, u):
        b_rs(k, u).wait_send()
        whole(rb)(k, u)

    hops = [
        (c_rs, fold_core, f_rs),
        (f_rs, fold(0, rf, ab, a_rs), a_rs),
        (a_rs, fold(1, ra, sb, s_rs), s_rs),
        (s_rs, whole(rs), b_rs),
        (b_rs, last_fold, s_ag),
        (s_ag, None, a_ag),
        (a_ag, None, f_ag),
        (f_ag, None, c_ag),
        (c_ag, None, None),
    ]

    def serve(t, v, order):
        for h in order:
            took, work, send = hops[h]
            back = v - DELAY[h]
            k = t + back // U
            u = back % U

            @pl.when((k >= 0) & (k < nch))
            def _():
                took(k, u).wait_recv()
                if work is not None:
                    work(k, u)
                if h >= 4 and send is not None:
                    free(send, k, u)
                if send is not None:
                    send(k, u).start()

    def grad_part(k, side):
        start = pl.multiple_of(half * side, half)
        dims = (((0,), (0,)), ((), ()))
        return lax.dot_general(
            mixed_v[:, pl.ds(start, half)], gp_v[:, cols(k)], dims, preferred_element_type=f32
        )

    def there(k):
        grad = grad_part(k, 1 - core)
        snd[k % 2, 0] = grad[:, :H].astype(bf16)
        snd[k % 2, 1] = grad[:, H:].astype(bf16)

    def here(k):
        grad = grad_part(k, core)
        own = pl.ds(pl.multiple_of(half * core, half), half)
        ag[2 * k, own] = grad[:, :H].astype(bf16)
        ag[2 * k + 1, own] = grad[:, H:].astype(bf16)

    def early(t, more):
        serve(t, 0, ORDER)
        serve(t, 1, ORDER)

        @pl.when(t >= 2)
        def _():
            for u in range(U):
                c_rs(t - 2, u).wait_send()

        if more:
            cot_in(t + 1).wait()

            @pl.when(t == 0)
            def _():
                w_in(1).wait()

        there(t)
        if more:
            pre_part(t + 1, 0, total // 2, False)
        for u in range(U):
            c_rs(t, u).start()
        serve(t, 2, ORDER)
        serve(t, 3, ORDER)
        here(t)
        if more:
            pre_part(t + 1, total // 2, total // 2, True)

            @pl.when(t + 2 < nch)
            def _():
                cot_in(t + 2).start()

    def early_step(t, carry):
        early(t, True)
        return carry

    lax.fori_loop(0, nch - 1, early_step, 0)
    early(nch - 1, False)

    def bias_hop(j):
        to = pc
        for i, p in enumerate((px, py, pz1, pz2)):
            to = jnp.where(j == i + 1, p, to)
        return pltpu.make_async_remote_copy(
            gb_v.at[j], gr.at[j], bsem.at[j], brsem.at[j], device_id=(to,), device_id_type=MESH
        )

    def bias_step(i):
        @pl.when((i >= 1) & (i <= 5))
        def _():
            bias_hop(i - 1).wait_recv()
            gb_v[i] = gb_v[i - 1] + gr[i - 1]

        @pl.when(i < 5)
        def _():
            bias_hop(i).start()

    def late_mixed(i, carry):
        bias_step(i)
        s = jnp.where(i == 0, 0, jnp.where(i == 1, slots - 1, i - 1))
        d = slot_rows(s)
        tile = width // 4
        for v in range(U):
            serve(nch + i, v, ORDER)
            c = pl.ds(v * tile, tile)
            dims = (((1,), (1,)), ((), ()))
            back = lax.dot_general(gp_v[d, :], w_v[c, :], dims, preferred_element_type=f32)
            mixed_v[d, c] = (sc[d, :] * back).astype(bf16)
        out = jnp.dot(
            kt[s, pl.ds(rows, 2 * rim), :], mixed_v[d, :], preferred_element_type=f32
        ).astype(bf16)

        @pl.when(s > 0)
        def _():
            xr[s - 1, pl.ds(rows + rim, rim), :] = out[:rim]

        @pl.when(s < slots - 1)
        def _():
            xr[s + 1, pl.ds(rows, rim), :] = out[rim:]

        @pl.when(s == 0)
        def _():
            hs[2] = out[:rim]
            back_send(0).start()

        @pl.when(s == slots - 1)
        def _():
            hs[3] = out[rim:]
            back_send(1).start()

        return carry

    lax.fori_loop(0, slots, late_mixed, 0)
    back_send(0).wait_recv()
    back_send(1).wait_recv()
    xr[slots - 1, pl.ds(rows + rim, rim), :] = hr[0]
    xr[0, pl.ds(rows, rim), :] = hr[1]

    def late_features(s, carry):
        bias_step(s + slots)
        d = slot_rows(s)
        tile = width // 4
        for v in range(U):
            serve(nch + slots + s, v, ORDER)
            c = pl.ds(v * tile, tile)
            grad = jnp.dot(kt[s, pl.ds(0, rows), :], mixed_v[d, c], preferred_element_type=f32)
            grad = grad + jnp.dot(
                ot[s], xr[s, pl.ds(rows, 2 * rim), c], preferred_element_type=f32
            )
            xr[s, pl.ds(0, rows), c] = grad.astype(bf16)
        return carry

    lax.fori_loop(0, slots, late_features, 0)

    def late(t, carry):
        for v in range(U):
            serve(t, v, ORDER)
        return carry

    lax.fori_loop(nch + 2 * slots, nch + (DELAY[-1] + U - 1) // U + 1, late, 0)
    gb[...] = gb_v[5]
    for j in range(5):
        bias_hop(j).wait_send()
    for j in range(2):
        for q in range(2):
            halo_send(j, q).wait_send()
        back_send(j).wait_send()
    for k in range(nch - 2, nch):
        for u in range(U):
            for f in (c_rs, f_rs, a_rs, s_rs, s_ag, a_ag, f_ag, c_ag):
                f(k, u).wait_send()


U = 4
TURNED = (0,)
Q = 24
DELAY = [4 + 4 * h for h in range(9)]
ORDER = list(range(8, -1, -1))


def main_call(features, weight, bias, cot, seg, offs, marks, edges, edge_marks, rims):
    slots, rows = seg.shape
    total, width = cot.shape
    rim = rims.shape[2]
    nch = width // CH
    half = width // 2
    unit = half // U
    any_ = pl.BlockSpec(memory_space=pl.ANY)
    dma = pltpu.SemaphoreType.DMA
    i32 = jnp.int32
    return pl.pallas_call(
        main_kernel,
        out_shape=(
            pltpu.VMEM((total, width), bf16),
            pltpu.VMEM((slots, rows + 2 * rim, width), bf16),
            pltpu.VMEM((2 * nch, width, H), bf16),
            pltpu.VMEM((1, width), f32),
        ),
        in_specs=[any_] * 10,
        out_specs=[pl.BlockSpec(memory_space=pltpu.VMEM)] * 4,
        scratch_shapes=[
            pltpu.VMEM((slots, rows + 2 * rim, rows), bf16),
            pltpu.VMEM((slots, rows, 2 * rim), bf16),
            pltpu.VMEM((total, 1), f32),
            pltpu.VMEM((total, width), bf16),
            pltpu.VMEM((width, width), bf16),
            pltpu.VMEM((1, width), f32),
            pltpu.VMEM((2, total, CH), bf16),
            pltpu.VMEM((total, width), bf16),
            pltpu.VMEM(seg.shape, i32),
            pltpu.VMEM(offs.shape, i32),
            pltpu.VMEM(marks.shape, i32),
            pltpu.VMEM(edges.shape, i32),
            pltpu.VMEM(edge_marks.shape, i32),
            pltpu.VMEM(rims.shape, i32),
            pltpu.VMEM((offs.shape[1], rows), i32),
            pltpu.VMEM((offs.shape[1], rows), i32),
            pltpu.VMEM((4, rim, width), bf16),
            pltpu.VMEM((2, rim, width), bf16),
            pltpu.VMEM((2, 2, half, H), bf16),
            pltpu.VMEM((4, 2, half, H), bf16),
            pltpu.VMEM((2, U, unit, H), bf16),
            pltpu.VMEM((nch, U, unit, H), bf16),
            pltpu.VMEM((2, U, unit // 2, H), bf16),
            pltpu.VMEM((nch, U, unit // 2, H), bf16),
            pltpu.VMEM((2, U, unit // 4, H), bf16),
            pltpu.VMEM((nch, U, unit // 4, H), bf16),
            pltpu.VMEM((nch, U, unit // 4, H), bf16),
            pltpu.VMEM((6, 1, width), f32),
            pltpu.VMEM((5, 1, width), f32),
            dma((slots,)),
            dma((7,)),
            dma((2,)),
            dma((2,)),
            dma((2, 9 * U)),
            dma((4, U)),
            dma((2, 8 * U)),
            dma((5,)),
            dma((5,)),
            dma((6,)),
            dma((6,)),
        ],
        compiler_params=pltpu.CompilerParams(
            collective_id=0, has_side_effects=True, vmem_limit_bytes=40 << 20
        ),
        name="layer",
    )(features, weight, bias, cot, seg, offs, marks, edges, edge_marks, rims)


def finish_kernel(act, xr, ag, gb, act_o, gf_o, gw_o, gb_o, stage, sem, ssem):
    slots, rows, _ = gf_o.shape
    n, step, _ = stage.shape
    plain = [(gb, gb_o), (act, act_o)]
    plain += [(xr.at[s, pl.ds(0, rows)], gf_o.at[s]) for s in range(slots)]
    plain = [pltpu.make_async_copy(a, b, sem.at[i]) for i, (a, b) in enumerate(plain)]

    def out(i):
        return pltpu.make_async_copy(
            stage.at[i % n], gw_o.at[pl.ds(i * step, step)], ssem.at[i % n]
        )

    steps = gw_o.shape[0] // step
    for i in range(steps):
        if i >= n:
            out(i - n).wait()
        for j in range(ag.shape[0]):
            stage[i % n, :, j * H : (j + 1) * H] = ag[j, i * step : (i + 1) * step].astype(f32)
        out(i).start()
        if i == 0:
            for c in plain:
                c.start()
    for i in range(steps - n, steps):
        out(i).wait()
    for c in plain:
        c.wait()


def finish(act, xr, ag, gb, rows):
    slots, _, width = xr.shape
    vmem = pl.BlockSpec(memory_space=pltpu.VMEM)
    any_ = pl.BlockSpec(memory_space=pl.ANY)
    return pl.pallas_call(
        finish_kernel,
        out_shape=(
            jax.ShapeDtypeStruct(act.shape, bf16),
            jax.ShapeDtypeStruct((slots, rows, width), bf16),
            jax.ShapeDtypeStruct((width, width), f32),
            jax.ShapeDtypeStruct((1, width), f32),
        ),
        in_specs=[vmem] * 4,
        out_specs=[any_] * 4,
        scratch_shapes=[
            pltpu.VMEM((4, 128, width), f32),
            pltpu.SemaphoreType.DMA((2 + slots,)),
            pltpu.SemaphoreType.DMA((4,)),
        ],
        compiler_params=pltpu.CompilerParams(vmem_limit_bytes=6 << 20),
        name="finish",
    )(act, xr, ag, gb)


def passed_along(value, axis, steps):
    count = lax.axis_size(axis)
    pairs = [(source, (source + steps) % count) for source in range(count)]
    return lax.ppermute(value, axis, pairs)


def tables(seg, offsets, marks, edges, edge_marks, rim):
    slots, rows = seg.shape
    order = jnp.arange(rows, dtype=jnp.int32)
    same = seg[:, :, None] == seg[:, None, :]
    start = jnp.min(jnp.where(same, order, rows), axis=2)
    extent = jnp.sum(same.astype(jnp.int32), axis=2)
    picks = jnp.where(marks == 1, offsets % extent[:, :, None], -1)
    lanes = jnp.arange(128, dtype=jnp.int32)
    near = jnp.sum((picks[:, :, :, None] == lanes).astype(f32), axis=2).astype(bf16)
    spread = (lanes[None, :, None] == (order - start)[:, None, :]).astype(bf16)
    local = jnp.einsum("sio,soj->sij", near, spread, preferred_element_type=f32)
    local = jnp.where(same, local, 0.0) + 2.0 * (order[:, None] == order[None, :])
    joined = jnp.concatenate([edges[:, 0], edges[:, 1] + rim], axis=2)
    joined_marks = jnp.concatenate([edge_marks[:, 0], edge_marks[:, 1]], axis=2)
    cols = jnp.arange(2 * rim, dtype=jnp.int32)
    far = jnp.sum(jnp.where(joined[..., None] == cols, joined_marks[..., None], 0), axis=2)
    degree = jnp.sum(marks, axis=2) + jnp.sum(joined_marks, axis=2)
    return local.astype(bf16), far.astype(bf16), 1.0 / (1.0 + degree.astype(f32))


def spread_out(
    features,
    weight,
    bias,
    cotangent,
    segment_ids,
    neighbour_offsets,
    neighbour_mask,
    halo_edges,
    halo_mask,
    boundary_rows,
):
    slots, rows, width = features.shape
    rim = boundary_rows.shape[2]
    local_counts, halo_counts, scale = tables(
        segment_ids, neighbour_offsets, neighbour_mask, halo_edges, halo_mask, rim
    )
    chosen = (boundary_rows[..., None] == jnp.arange(rows, dtype=jnp.int32)).astype(bf16)
    sent = jnp.einsum("sjbr,srf->sjbf", chosen, features, preferred_element_type=f32).astype(bf16)
    from_prev = passed_along(sent[slots - 1, 1], "blk", 1)
    from_next = passed_along(sent[0, 0], "blk", -1)
    before = jnp.concatenate([from_prev[None], sent[: slots - 1, 1]], axis=0)
    after = jnp.concatenate([sent[1:, 0], from_next[None]], axis=0)
    received = jnp.concatenate([before, after], axis=1)
    summed = jnp.einsum("srk,skf->srf", local_counts, features, preferred_element_type=f32)
    summed = summed + jnp.einsum("srk,skf->srf", halo_counts, received, preferred_element_type=f32)
    mixed = (scale[:, :, None] * summed).astype(bf16).reshape(slots * rows, width)
    incoming = cotangent.reshape(slots * rows, width)
    pre = jnp.dot(mixed, weight, preferred_element_type=f32) + bias[None, :]
    sigma = jax.nn.sigmoid(pre)
    activations = (pre * sigma).astype(bf16)
    grad_pre = (incoming.astype(f32) * (sigma * (1.0 + pre * (1.0 - sigma)))).astype(bf16)
    bias_term = jnp.sum(grad_pre, axis=0, dtype=f32)
    weight_term = lax.dot_general(
        mixed, grad_pre, (((0,), (0,)), ((), ())), preferred_element_type=f32
    )
    grad_weight, grad_bias = lax.psum((weight_term, bias_term), "blk")
    grad_mixed = lax.dot_general(
        grad_pre, weight, (((1,), (1,)), ((), ())), preferred_element_type=f32
    )
    grad_summed = (scale.reshape(-1)[:, None] * grad_mixed).astype(bf16)
    grad_summed = grad_summed.reshape(slots, rows, width)
    grad_received = jnp.einsum(
        "srk,srf->skf", halo_counts, grad_summed, preferred_element_type=f32
    ).astype(bf16)
    toward_prev = grad_received[:, :rim]
    toward_next = grad_received[:, rim:]
    back_prev = passed_along(toward_next[slots - 1], "blk", 1)
    back_next = passed_along(toward_prev[0], "blk", -1)
    grad_first = jnp.concatenate([back_prev[None], toward_next[: slots - 1]], axis=0)
    grad_second = jnp.concatenate([toward_prev[1:], back_next[None]], axis=0)
    grad_sent = jnp.stack([grad_first, grad_second], axis=1)
    grad_features = jnp.einsum(
        "srk,srf->skf", local_counts, grad_summed, preferred_element_type=f32
    ) + jnp.einsum("sjbr,sjbf->srf", chosen, grad_sent, preferred_element_type=f32)
    return (
        activations.reshape(slots, rows, width),
        grad_features.astype(bf16),
        grad_weight,
        grad_bias,
    )


def per_device(
    features,
    weight,
    bias,
    cotangent,
    segment_ids,
    neighbour_offsets,
    neighbour_mask,
    halo_edges,
    halo_mask,
    boundary_rows,
):
    operands = (
        segment_ids,
        neighbour_offsets,
        neighbour_mask,
        halo_edges,
        halo_mask,
        boundary_rows,
    )
    if lax.axis_size("blk") != 32:
        return spread_out(features, weight, bias, cotangent, *operands)
    slots, rows, width = features.shape
    flat = (slots * rows, width)
    held = main_call(
        features.reshape(flat),
        weight,
        bias.reshape(1, width),
        cotangent.reshape(flat),
        segment_ids,
        jnp.swapaxes(neighbour_offsets, 1, 2),
        jnp.swapaxes(neighbour_mask, 1, 2),
        jnp.swapaxes(halo_edges, 2, 3),
        jnp.swapaxes(halo_mask, 2, 3),
        boundary_rows,
    )
    activations, grad_features, grad_weight, grad_bias = finish(*held, rows)
    return (
        activations.reshape(features.shape),
        grad_features,
        grad_weight,
        grad_bias.reshape(-1),
    )


def solution(mesh):
    in_specs = (
        P("blk", None, None),
        P(),
        P(),
        P("blk", None, None),
        P("blk", None),
        P("blk", None, None),
        P("blk", None, None),
        P("blk", None, None, None),
        P("blk", None, None, None),
        P("blk", None, None),
    )
    out_specs = (P("blk", None, None), P("blk", None, None), P(), P())
    return jax.shard_map(
        per_device, mesh=mesh, in_specs=in_specs, out_specs=out_specs, check_vma=False
    )
```

```python
import functools

import jax
import jax.numpy as jnp
from jax import lax
from jax.experimental import pallas as pl
from jax.experimental.pallas import tpu as pltpu
from jax.sharding import PartitionSpec as P

bf16 = jnp.bfloat16
f32 = jnp.float32
MESH = pl.DeviceIdType.MESH
CH = 256
H = 128


def neighbours(me):
    core = me % 2
    bits = [core, (me // 2) % 2, (me // 4) % 2, (me // 8) % 2, me // 16]
    return bits, [me + (1 << i) - (2 << i) * b for i, b in enumerate(bits)]


def main_kernel(
    x, w, bias, cot, seg, offs, marks, edges, edge_marks, rims,
    act, xr, ag, gb,
    kt, ot, sc, mixed_v, w_v, bias_v, cot_v, gp_v,
    seg_v, offs_v, marks_v, edges_v, emarks_v, rims_v, qv, vv, hs, hr,
    snd, rc, fb, rf, ab, ra, sb, rs, rb, gb_v, gr,
    xsem, tsem, wsem, csem, ssem, rcsem, resem, rsem, bsem, brsem, hsem, hrsem,
):
    n = lax.axis_size("blk")
    me = lax.axis_index("blk")
    slots, deep, width = xr.shape
    rows = kt.shape[2]
    rim = rims_v.shape[2]
    near = offs_v.shape[1]
    halo = edges_v.shape[2]
    total = slots * rows
    nch = width // CH
    half = width // 2
    unit = half // U
    (core, bx, by, bz1, bz2), (pc, px, py, pz1, pz2) = neighbours(me)
    prev = lax.rem(me + n - 1, n)
    nxt = lax.rem(me + 1, n)
    first = [px * (1 - core) + py * core, py * (1 - core) + px * core]
    fbit = [bx * (1 - core) + by * core, by * (1 - core) + bx * core]
    second = [first[1], first[0]]
    sbit = [fbit[1], fbit[0]]

    def middle(u):
        pair = [(bz1, pz1), (sbit[u % 2], second[u % 2])]
        return pair[::-1] if u in TURNED else pair


    barrier = pltpu.get_barrier_semaphore()
    for p in (pc, px, py, pz1, pz2, prev, nxt):
        pl.semaphore_signal(barrier, inc=1, device_id=(p,), device_id_type=MESH)

    def local(src, dst, sem):
        return pltpu.make_async_copy(src, dst, sem)

    def cols(k):
        return pl.ds(pl.multiple_of(k * CH, CH), CH)

    def slot_rows(s):
        return pl.ds(pl.multiple_of(s * rows, 16), rows)

    def x_in(s):
        return local(x.at[slot_rows(s)], xr.at[s, pl.ds(0, rows)], xsem.at[s])

    def w_in(i):
        c = (pl.ds(0, CH), pl.ds(CH, width - CH))[i]
        return local(w.at[:, c], w_v.at[:, c], wsem.at[i])

    def cot_in(k):
        return local(cot.at[:, cols(k)], cot_v.at[k % 2], csem.at[k % 2])

    small = [
        local(src, dst, tsem.at[i])
        for i, (src, dst) in enumerate(
            (
                (rims, rims_v),
                (seg, seg_v),
                (offs, offs_v),
                (marks, marks_v),
                (edges, edges_v),
                (edge_marks, emarks_v),
                (bias, bias_v),
            )
        )
    ]
    small[0].start()
    x_in(0).start()
    x_in(slots - 1).start()
    for c in small[1:]:
        c.start()
    for s in range(1, slots - 1):
        x_in(s).start()

    def offer(s):
        picks = jnp.concatenate([rims_v[s, 0:1, :], rims_v[s, 1:2, :]], axis=1)
        order = lax.broadcasted_iota(jnp.int32, (rows, 2 * rim), 0)
        ot[s] = jnp.where(order == picks, 1.0, 0.0).astype(bf16)
        dims = (((0,), (0,)), ((), ()))
        return lax.dot_general(
            ot[s], xr[s, pl.ds(0, rows), :], dims, preferred_element_type=f32
        ).astype(bf16)

    def halo_send(j, q):
        s, to = ((0, nxt), (slots - 1, prev))[j]
        c = pl.ds(q * half, half)
        i = 2 * j + q
        return pltpu.make_async_remote_copy(
            hs.at[j, :, c], xr.at[s, pl.ds(rows + rim * j, rim), c], hsem.at[i], hrsem.at[i],
            device_id=(to,), device_id_type=MESH,
        )

    def back_send(j):
        to = (prev, nxt)[j]
        return pltpu.make_async_remote_copy(
            hs.at[2 + j], hr.at[j], hsem.at[4 + j], hrsem.at[4 + j],
            device_id=(to,), device_id_type=MESH,
        )

    small[0].wait()
    x_in(0).wait()
    out = offer(0)
    hs[1] = out[:rim]
    xr[1, pl.ds(rows, rim), :] = out[rim:]
    x_in(slots - 1).wait()
    out = offer(slots - 1)
    hs[0] = out[rim:]
    xr[slots - 2, pl.ds(rows + rim, rim), :] = out[:rim]
    pl.semaphore_wait(barrier, 7)
    for q in range(2):
        for j in range(2):
            halo_send(j, q).start()
    w_in(0).start()
    cot_in(0).start()
    cot_in(1).start()
    w_in(1).start()
    for c in small[1:]:
        c.wait()
    for s in range(1, slots - 1):
        x_in(s).wait()
        out = offer(s)
        xr[s - 1, pl.ds(rows + rim, rim), :] = out[:rim]
        xr[s + 1, pl.ds(rows, rim), :] = out[rim:]

    def tables(s, carry):
        seg_r = seg_v[pl.ds(s, 1), :].astype(f32)
        ri = lax.broadcasted_iota(jnp.int32, (rows, rows), 0)
        ci = lax.broadcasted_iota(jnp.int32, (rows, rows), 1)
        diag = ri == ci
        seg_c = jnp.sum(jnp.where(diag, seg_r, 0.0), axis=1, keepdims=True)
        start = jnp.sum(jnp.where(seg_r < seg_c, 1.0, 0.0), axis=1, keepdims=True)
        same = seg_r == seg_c
        size = jnp.sum(jnp.where(same, 1.0, 0.0), axis=0, keepdims=True)
        off = offs_v[s].astype(f32)
        rest = off - jnp.floor((off + 0.5) * (1.0 / size)) * size
        rest = jnp.where(rest < 0.0, rest + size, rest)
        rest = jnp.where(rest >= size, rest - size, rest)
        marked = marks_v[s]
        pick = jnp.where(marked == 1, rest.astype(jnp.int32), 200)
        qv[...] = pick >> 2
        vv[...] = 1 << ((pick & 3) << 3)
        q = lax.broadcasted_iota(jnp.int32, (Q, rows), 0)
        packed = jnp.zeros((Q, rows), jnp.int32)
        for k in range(near):
            packed = packed + jnp.where(qv[k : k + 1, :] == q, vv[k : k + 1, :], 0)
        counts = jnp.concatenate(
            [((packed >> (8 * r)) & 255).astype(f32) for r in range(4)], axis=0
        ).astype(bf16)
        rel = lax.broadcasted_iota(jnp.int32, (rows, 1), 0) - start.astype(jnp.int32)
        place = (rel & 3) * Q + (rel >> 2)
        lanes = lax.broadcasted_iota(jnp.int32, (rows, 4 * Q), 1)
        spread = jnp.where(lanes == place, 1.0, 0.0).astype(bf16)
        around = jnp.dot(spread, counts, preferred_element_type=f32)
        around = jnp.where(same, around, 0.0) + jnp.where(diag, 2.0, 0.0)
        kt[s, pl.ds(0, rows), :] = around.astype(bf16)
        degree = jnp.sum(marked, axis=0, keepdims=True)
        r = lax.broadcasted_iota(jnp.int32, (rim, rows), 0)
        for j in range(2):
            hot = emarks_v[s, j]
            degree = degree + jnp.sum(hot, axis=0, keepdims=True)
            pick = jnp.where(hot == 1, edges_v[s, j], 200)
            far = jnp.zeros((rim, rows), f32)
            for k in range(halo):
                far = far + jnp.where(pick[k : k + 1, :] == r, 1.0, 0.0)
            kt[s, pl.ds(rows + rim * j, rim), :] = far.astype(bf16)
        degree = jnp.sum(jnp.where(diag, degree.astype(f32), 0.0), axis=1, keepdims=True)
        sc[slot_rows(s), :] = 1.0 / (1.0 + degree)
        return carry

    lax.fori_loop(0, slots, tables, 0, unroll=True)

    def mix(s, tiles):
        d = slot_rows(s)
        dims = (((0,), (0,)), ((), ()))
        for j in tiles:
            c = pl.ds(j * (width // 4), width // 4)
            summed = lax.dot_general(kt[s], xr[s, :, c], dims, preferred_element_type=f32)
            mixed_v[d, c] = (sc[d, :] * summed).astype(bf16)

    def pre_part(k, start, count, more):
        d = pl.ds(start, count)
        b = bias_v[:, cols(k)]
        pre = jnp.dot(mixed_v[d, :], w_v[:, cols(k)], preferred_element_type=f32) + b
        sig = 0.5 * jnp.tanh(0.5 * pre) + 0.5
        out = pre * sig
        act[d, cols(k)] = out.astype(bf16)
        g = (cot_v[k % 2, d, :].astype(f32) * (sig + out * (1.0 - sig))).astype(bf16)
        gp_v[d, cols(k)] = g
        sums = jnp.sum(g.astype(f32), axis=0, keepdims=True)
        if more:
            sums = sums + gb_v[0, :, cols(k)]
        gb_v[0, :, cols(k)] = sums

    for s in range(1, slots - 1):
        mix(s, range(4))
    w_in(0).wait()
    cot_in(0).wait()
    pre_part(0, rows, total - 2 * rows, False)
    for q in range(2):
        for j in range(2):
            halo_send(j, q).wait_recv()
        mix(0, (2 * q, 2 * q + 1))
        mix(slots - 1, (2 * q, 2 * q + 1))
    pre_part(0, 0, rows, True)
    pre_part(0, total - rows, rows, True)

    def remote(src, dst, k, s, to):
        return pltpu.make_async_remote_copy(
            src,
            dst,
            ssem.at[k % 2, s],
            rsem.at[k % 2, s - U],
            device_id=(to,),
            device_id_type=MESH,
        )

    def at(u, level, flip=False, base=0):
        r = base + unit * u
        size = unit
        picks = [bit for bit, _ in middle(u)]
        for j in range(level):
            size = size // 2
            b = picks[j]
            if flip and j == level - 1:
                b = 1 - b
            r = r + size * b
        return pl.ds(pl.multiple_of(r, 16), size)

    def part(k, j, u, level, flip=False):
        return ag.at[2 * k + j, at(u, level, flip, half * core)]

    def c_rs(k, u):
        return pltpu.make_async_remote_copy(
            snd.at[k % 2, :, at(u, 0)],
            rc.at[k % 4, :, at(u, 0)],
            ssem.at[k % 2, u],
            rcsem.at[k % 4, u],
            device_id=(pc,),
            device_id_type=MESH,
        )

    def f_rs(k, u):
        return remote(fb.at[k % 2, u], rf.at[k, u], k, U + u, first[u % 2])

    def a_rs(k, u):
        return remote(ab.at[k % 2, u], ra.at[k, u], k, 2 * U + u, middle(u)[0][1])

    def s_rs(k, u):
        return remote(sb.at[k % 2, u], rs.at[k, u], k, 3 * U + u, middle(u)[1][1])

    def b_rs(k, u):
        return remote(part(k, fbit[u % 2], u, 2), rb.at[k, u], k, 4 * U + u, pz2)

    def s_ag(k, u):
        p = part(k, fbit[u % 2], u, 2)
        return remote(p, p, k, 5 * U + u, middle(u)[1][1])

    def a_ag(k, u):
        p = part(k, fbit[u % 2], u, 1)
        return remote(p, p, k, 6 * U + u, middle(u)[0][1])

    def e_ag(k, u):
        p = part(k, fbit[u % 2], u, 1)
        return pltpu.make_async_remote_copy(
            p,
            p,
            ssem.at[k % 2, 9 * U + u],
            resem.at[k % 4, u],
            device_id=(first[u % 2],),
            device_id_type=MESH,
        )

    def f_ag(k, u):
        p = part(k, fbit[u % 2], u, 1, True)
        return remote(p, p, k, 7 * U + u, first[u % 2])

    def c_ag(k, u):
        p = ag.at[pl.ds(2 * k, 2), at(u, 0, False, half * core)]
        return remote(p, p, k, 8 * U + u, pc)

    def free(send, k, u):
        @pl.when(k >= 2)
        def _():
            send(k - 2, u).wait_send()

    def fold_core(k, u):
        f = fbit[u % 2]
        free(f_rs, k, u)
        fb[k % 2, u] = part(k, 1 - f, u, 0)[...] + rc[k % 4, 1 - f, at(u, 0)]
        p = part(k, f, u, 0)
        p[...] = p[...] + rc[k % 4, f, at(u, 0)]

    def fold(level, buf, out, send):
        def run(k, u):
            f = fbit[u % 2]
            bit = middle(u)[level][0]
            size = (unit >> level) // 2
            free(send, k, u)
            away = pl.ds(pl.multiple_of(size * (1 - bit), 16), size)
            stay = pl.ds(pl.multiple_of(size * bit, 16), size)
            out[k % 2, u] = part(k, f, u, level + 1, True)[...] + buf[k, u, away]
            p = part(k, f, u, level + 1)
            p[...] = p[...] + buf[k, u, stay]

        return run

    def whole(buf):
        def run(k, u):
            p = part(k, fbit[u % 2], u, 2)
            p[...] = p[...] + buf[k, u]

        return run

    def last_fold(k, u):
        b_rs(k, u).wait_send()
        whole(rb)(k, u)

    hops = [
        ((c_rs,), fold_core, (f_rs,)),
        ((f_rs,), fold(0, rf, ab, a_rs), (a_rs,)),
        ((a_rs,), fold(1, ra, sb, s_rs), (s_rs,)),
        ((s_rs,), whole(rs), (b_rs,)),
        ((b_rs,), last_fold, (s_ag,)),
        ((s_ag,), None, (a_ag, e_ag)),
        ((a_ag,), None, (f_ag,)),
        ((e_ag, f_ag), None, (c_ag,)),
        ((c_ag,), None, ()),
    ]

    def serve(t, v, order):
        for h in order:
            took, work, sent = hops[h]
            back = v - DELAY[h]
            k = t + back // U
            u = back % U

            @pl.when((k >= 0) & (k < nch))
            def _():
                for copy in took:
                    copy(k, u).wait_recv()
                if work is not None:
                    work(k, u)
                for send in sent:
                    if h >= 4:
                        free(send, k, u)
                    send(k, u).start()

    def grad_part(k, side):
        start = pl.multiple_of(half * side, half)
        dims = (((0,), (0,)), ((), ()))
        return lax.dot_general(
            mixed_v[:, pl.ds(start, half)], gp_v[:, cols(k)], dims, preferred_element_type=f32
        )

    def there(k):
        grad = grad_part(k, 1 - core)
        snd[k % 2, 0] = grad[:, :H].astype(bf16)
        snd[k % 2, 1] = grad[:, H:].astype(bf16)

    def here(k):
        grad = grad_part(k, core)
        own = pl.ds(pl.multiple_of(half * core, half), half)
        ag[2 * k, own] = grad[:, :H].astype(bf16)
        ag[2 * k + 1, own] = grad[:, H:].astype(bf16)

    def early(t, more):
        serve(t, 0, ORDER)
        serve(t, 1, ORDER)

        @pl.when(t >= 2)
        def _():
            for u in range(U):
                c_rs(t - 2, u).wait_send()

        if more:
            cot_in(t + 1).wait()

            @pl.when(t == 0)
            def _():
                w_in(1).wait()

        there(t)
        if more:
            pre_part(t + 1, 0, total // 2, False)
        for u in range(U):
            c_rs(t, u).start()
        serve(t, 2, ORDER)
        serve(t, 3, ORDER)
        here(t)
        if more:
            pre_part(t + 1, total // 2, total // 2, True)

            @pl.when(t + 2 < nch)
            def _():
                cot_in(t + 2).start()

    def early_step(t, carry):
        early(t, True)
        return carry

    lax.fori_loop(0, nch - 1, early_step, 0)
    early(nch - 1, False)

    def bias_hop(j):
        to = pc
        for i, p in enumerate((px, py, pz1, pz2)):
            to = jnp.where(j == i + 1, p, to)
        return pltpu.make_async_remote_copy(
            gb_v.at[j], gr.at[j], bsem.at[j], brsem.at[j], device_id=(to,), device_id_type=MESH
        )

    def bias_step(i):
        @pl.when((i >= 1) & (i <= 5))
        def _():
            bias_hop(i - 1).wait_recv()
            gb_v[i] = gb_v[i - 1] + gr[i - 1]

        @pl.when(i < 5)
        def _():
            bias_hop(i).start()

    def late_mixed(i, carry):
        bias_step(i)
        s = jnp.where(i == 0, 0, jnp.where(i == 1, slots - 1, i - 1))
        d = slot_rows(s)
        tile = width // 4
        for v in range(U):
            serve(nch + i, v, ORDER)
            c = pl.ds(v * tile, tile)
            dims = (((1,), (1,)), ((), ()))
            back = lax.dot_general(gp_v[d, :], w_v[c, :], dims, preferred_element_type=f32)
            mixed_v[d, c] = (sc[d, :] * back).astype(bf16)
        out = jnp.dot(
            kt[s, pl.ds(rows, 2 * rim), :], mixed_v[d, :], preferred_element_type=f32
        ).astype(bf16)

        @pl.when(s > 0)
        def _():
            xr[s - 1, pl.ds(rows + rim, rim), :] = out[:rim]

        @pl.when(s < slots - 1)
        def _():
            xr[s + 1, pl.ds(rows, rim), :] = out[rim:]

        @pl.when(s == 0)
        def _():
            hs[2] = out[:rim]
            back_send(0).start()

        @pl.when(s == slots - 1)
        def _():
            hs[3] = out[rim:]
            back_send(1).start()

        return carry

    lax.fori_loop(0, slots, late_mixed, 0)
    back_send(0).wait_recv()
    back_send(1).wait_recv()
    xr[slots - 1, pl.ds(rows + rim, rim), :] = hr[0]
    xr[0, pl.ds(rows, rim), :] = hr[1]

    def late_features(s, carry):
        bias_step(s + slots)
        d = slot_rows(s)
        tile = width // 4
        for v in range(U):
            serve(nch + slots + s, v, ORDER)
            c = pl.ds(v * tile, tile)
            grad = jnp.dot(kt[s, pl.ds(0, rows), :], mixed_v[d, c], preferred_element_type=f32)
            grad = grad + jnp.dot(
                ot[s], xr[s, pl.ds(rows, 2 * rim), c], preferred_element_type=f32
            )
            xr[s, pl.ds(0, rows), c] = grad.astype(bf16)
        return carry

    lax.fori_loop(0, slots, late_features, 0)

    def late(t, carry):
        for v in range(U):
            serve(t, v, ORDER)
        return carry

    lax.fori_loop(nch + 2 * slots, nch + (DELAY[-1] + U - 1) // U, late, 0)
    gb[...] = gb_v[5]
    for j in range(5):
        bias_hop(j).wait_send()
    for j in range(2):
        for q in range(2):
            halo_send(j, q).wait_send()
        back_send(j).wait_send()
    for k in range(nch - 2, nch):
        for u in range(U):
            for f in (c_rs, f_rs, a_rs, s_rs, s_ag, a_ag, e_ag, f_ag, c_ag):
                f(k, u).wait_send()


U = 4
TURNED = (0,)
Q = 24
DELAY = [4 + 4 * h for h in range(9)]
ORDER = list(range(8, -1, -1))


def main_call(features, weight, bias, cot, seg, offs, marks, edges, edge_marks, rims):
    slots, rows = seg.shape
    total, width = cot.shape
    rim = rims.shape[2]
    nch = width // CH
    half = width // 2
    unit = half // U
    any_ = pl.BlockSpec(memory_space=pl.ANY)
    dma = pltpu.SemaphoreType.DMA
    i32 = jnp.int32
    return pl.pallas_call(
        main_kernel,
        out_shape=(
            pltpu.VMEM((total, width), bf16),
            pltpu.VMEM((slots, rows + 2 * rim, width), bf16),
            pltpu.VMEM((2 * nch, width, H), bf16),
            pltpu.VMEM((1, width), f32),
        ),
        in_specs=[any_] * 10,
        out_specs=[pl.BlockSpec(memory_space=pltpu.VMEM)] * 4,
        scratch_shapes=[
            pltpu.VMEM((slots, rows + 2 * rim, rows), bf16),
            pltpu.VMEM((slots, rows, 2 * rim), bf16),
            pltpu.VMEM((total, 1), f32),
            pltpu.VMEM((total, width), bf16),
            pltpu.VMEM((width, width), bf16),
            pltpu.VMEM((1, width), f32),
            pltpu.VMEM((2, total, CH), bf16),
            pltpu.VMEM((total, width), bf16),
            pltpu.VMEM(seg.shape, i32),
            pltpu.VMEM(offs.shape, i32),
            pltpu.VMEM(marks.shape, i32),
            pltpu.VMEM(edges.shape, i32),
            pltpu.VMEM(edge_marks.shape, i32),
            pltpu.VMEM(rims.shape, i32),
            pltpu.VMEM((offs.shape[1], rows), i32),
            pltpu.VMEM((offs.shape[1], rows), i32),
            pltpu.VMEM((4, rim, width), bf16),
            pltpu.VMEM((2, rim, width), bf16),
            pltpu.VMEM((2, 2, half, H), bf16),
            pltpu.VMEM((4, 2, half, H), bf16),
            pltpu.VMEM((2, U, unit, H), bf16),
            pltpu.VMEM((nch, U, unit, H), bf16),
            pltpu.VMEM((2, U, unit // 2, H), bf16),
            pltpu.VMEM((nch, U, unit // 2, H), bf16),
            pltpu.VMEM((2, U, unit // 4, H), bf16),
            pltpu.VMEM((nch, U, unit // 4, H), bf16),
            pltpu.VMEM((nch, U, unit // 4, H), bf16),
            pltpu.VMEM((6, 1, width), f32),
            pltpu.VMEM((5, 1, width), f32),
            dma((slots,)),
            dma((7,)),
            dma((2,)),
            dma((2,)),
            dma((2, 10 * U)),
            dma((4, U)),
            dma((4, U)),
            dma((2, 8 * U)),
            dma((5,)),
            dma((5,)),
            dma((6,)),
            dma((6,)),
        ],
        compiler_params=pltpu.CompilerParams(
            collective_id=0, has_side_effects=True, vmem_limit_bytes=40 << 20
        ),
        name="layer",
    )(features, weight, bias, cot, seg, offs, marks, edges, edge_marks, rims)


def finish_kernel(act, xr, ag, gb, act_o, gf_o, gw_o, gb_o, stage, sem, ssem):
    slots, rows, _ = gf_o.shape
    n, step, _ = stage.shape
    plain = [(gb, gb_o), (act, act_o)]
    plain += [(xr.at[s, pl.ds(0, rows)], gf_o.at[s]) for s in range(slots)]
    plain = [pltpu.make_async_copy(a, b, sem.at[i]) for i, (a, b) in enumerate(plain)]

    def out(i):
        return pltpu.make_async_copy(
            stage.at[i % n], gw_o.at[pl.ds(i * step, step)], ssem.at[i % n]
        )

    steps = gw_o.shape[0] // step
    for i in range(steps):
        if i >= n:
            out(i - n).wait()
        for j in range(ag.shape[0]):
            stage[i % n, :, j * H : (j + 1) * H] = ag[j, i * step : (i + 1) * step].astype(f32)
        out(i).start()
        if i == 0:
            for c in plain:
                c.start()
    for i in range(steps - n, steps):
        out(i).wait()
    for c in plain:
        c.wait()


def finish(act, xr, ag, gb, rows):
    slots, _, width = xr.shape
    vmem = pl.BlockSpec(memory_space=pltpu.VMEM)
    any_ = pl.BlockSpec(memory_space=pl.ANY)
    return pl.pallas_call(
        finish_kernel,
        out_shape=(
            jax.ShapeDtypeStruct(act.shape, bf16),
            jax.ShapeDtypeStruct((slots, rows, width), bf16),
            jax.ShapeDtypeStruct((width, width), f32),
            jax.ShapeDtypeStruct((1, width), f32),
        ),
        in_specs=[vmem] * 4,
        out_specs=[any_] * 4,
        scratch_shapes=[
            pltpu.VMEM((4, 128, width), f32),
            pltpu.SemaphoreType.DMA((2 + slots,)),
            pltpu.SemaphoreType.DMA((4,)),
        ],
        compiler_params=pltpu.CompilerParams(vmem_limit_bytes=6 << 20),
        name="finish",
    )(act, xr, ag, gb)


def passed_along(value, axis, steps):
    count = lax.axis_size(axis)
    pairs = [(source, (source + steps) % count) for source in range(count)]
    return lax.ppermute(value, axis, pairs)


def tables(seg, offsets, marks, edges, edge_marks, rim):
    slots, rows = seg.shape
    order = jnp.arange(rows, dtype=jnp.int32)
    same = seg[:, :, None] == seg[:, None, :]
    start = jnp.min(jnp.where(same, order, rows), axis=2)
    extent = jnp.sum(same.astype(jnp.int32), axis=2)
    picks = jnp.where(marks == 1, offsets % extent[:, :, None], -1)
    lanes = jnp.arange(128, dtype=jnp.int32)
    near = jnp.sum((picks[:, :, :, None] == lanes).astype(f32), axis=2).astype(bf16)
    spread = (lanes[None, :, None] == (order - start)[:, None, :]).astype(bf16)
    local = jnp.einsum("sio,soj->sij", near, spread, preferred_element_type=f32)
    local = jnp.where(same, local, 0.0) + 2.0 * (order[:, None] == order[None, :])
    joined = jnp.concatenate([edges[:, 0], edges[:, 1] + rim], axis=2)
    joined_marks = jnp.concatenate([edge_marks[:, 0], edge_marks[:, 1]], axis=2)
    cols = jnp.arange(2 * rim, dtype=jnp.int32)
    far = jnp.sum(jnp.where(joined[..., None] == cols, joined_marks[..., None], 0), axis=2)
    degree = jnp.sum(marks, axis=2) + jnp.sum(joined_marks, axis=2)
    return local.astype(bf16), far.astype(bf16), 1.0 / (1.0 + degree.astype(f32))


def spread_out(
    features,
    weight,
    bias,
    cotangent,
    segment_ids,
    neighbour_offsets,
    neighbour_mask,
    halo_edges,
    halo_mask,
    boundary_rows,
):
    slots, rows, width = features.shape
    rim = boundary_rows.shape[2]
    local_counts, halo_counts, scale = tables(
        segment_ids, neighbour_offsets, neighbour_mask, halo_edges, halo_mask, rim
    )
    chosen = (boundary_rows[..., None] == jnp.arange(rows, dtype=jnp.int32)).astype(bf16)
    sent = jnp.einsum("sjbr,srf->sjbf", chosen, features, preferred_element_type=f32).astype(bf16)
    from_prev = passed_along(sent[slots - 1, 1], "blk", 1)
    from_next = passed_along(sent[0, 0], "blk", -1)
    before = jnp.concatenate([from_prev[None], sent[: slots - 1, 1]], axis=0)
    after = jnp.concatenate([sent[1:, 0], from_next[None]], axis=0)
    received = jnp.concatenate([before, after], axis=1)
    summed = jnp.einsum("srk,skf->srf", local_counts, features, preferred_element_type=f32)
    summed = summed + jnp.einsum("srk,skf->srf", halo_counts, received, preferred_element_type=f32)
    mixed = (scale[:, :, None] * summed).astype(bf16).reshape(slots * rows, width)
    incoming = cotangent.reshape(slots * rows, width)
    pre = jnp.dot(mixed, weight, preferred_element_type=f32) + bias[None, :]
    sigma = jax.nn.sigmoid(pre)
    activations = (pre * sigma).astype(bf16)
    grad_pre = (incoming.astype(f32) * (sigma * (1.0 + pre * (1.0 - sigma)))).astype(bf16)
    bias_term = jnp.sum(grad_pre, axis=0, dtype=f32)
    weight_term = lax.dot_general(
        mixed, grad_pre, (((0,), (0,)), ((), ())), preferred_element_type=f32
    )
    grad_weight, grad_bias = lax.psum((weight_term, bias_term), "blk")
    grad_mixed = lax.dot_general(
        grad_pre, weight, (((1,), (1,)), ((), ())), preferred_element_type=f32
    )
    grad_summed = (scale.reshape(-1)[:, None] * grad_mixed).astype(bf16)
    grad_summed = grad_summed.reshape(slots, rows, width)
    grad_received = jnp.einsum(
        "srk,srf->skf", halo_counts, grad_summed, preferred_element_type=f32
    ).astype(bf16)
    toward_prev = grad_received[:, :rim]
    toward_next = grad_received[:, rim:]
    back_prev = passed_along(toward_next[slots - 1], "blk", 1)
    back_next = passed_along(toward_prev[0], "blk", -1)
    grad_first = jnp.concatenate([back_prev[None], toward_next[: slots - 1]], axis=0)
    grad_second = jnp.concatenate([toward_prev[1:], back_next[None]], axis=0)
    grad_sent = jnp.stack([grad_first, grad_second], axis=1)
    grad_features = jnp.einsum(
        "srk,srf->skf", local_counts, grad_summed, preferred_element_type=f32
    ) + jnp.einsum("sjbr,sjbf->srf", chosen, grad_sent, preferred_element_type=f32)
    return (
        activations.reshape(slots, rows, width),
        grad_features.astype(bf16),
        grad_weight,
        grad_bias,
    )


def per_device(
    features,
    weight,
    bias,
    cotangent,
    segment_ids,
    neighbour_offsets,
    neighbour_mask,
    halo_edges,
    halo_mask,
    boundary_rows,
):
    operands = (
        segment_ids,
        neighbour_offsets,
        neighbour_mask,
        halo_edges,
        halo_mask,
        boundary_rows,
    )
    if lax.axis_size("blk") != 32:
        return spread_out(features, weight, bias, cotangent, *operands)
    slots, rows, width = features.shape
    flat = (slots * rows, width)
    held = main_call(
        features.reshape(flat),
        weight,
        bias.reshape(1, width),
        cotangent.reshape(flat),
        segment_ids,
        jnp.swapaxes(neighbour_offsets, 1, 2),
        jnp.swapaxes(neighbour_mask, 1, 2),
        jnp.swapaxes(halo_edges, 2, 3),
        jnp.swapaxes(halo_mask, 2, 3),
        boundary_rows,
    )
    activations, grad_features, grad_weight, grad_bias = finish(*held, rows)
    return (
        activations.reshape(features.shape),
        grad_features,
        grad_weight,
        grad_bias.reshape(-1),
    )


def solution(mesh):
    in_specs = (
        P("blk", None, None),
        P(),
        P(),
        P("blk", None, None),
        P("blk", None),
        P("blk", None, None),
        P("blk", None, None),
        P("blk", None, None, None),
        P("blk", None, None, None),
        P("blk", None, None),
    )
    out_specs = (P("blk", None, None), P("blk", None, None), P(), P())
    return jax.shard_map(
        per_device, mesh=mesh, in_specs=in_specs, out_specs=out_specs, check_vma=False
    )
```

```python
import functools

import jax
import jax.numpy as jnp
from jax import lax
from jax.experimental import pallas as pl
from jax.experimental.pallas import tpu as pltpu
from jax.sharding import PartitionSpec as P

bf16 = jnp.bfloat16
f32 = jnp.float32
MESH = pl.DeviceIdType.MESH
CH = 256
H = 128


def neighbours(me):
    core = me % 2
    bits = [core, (me // 2) % 2, (me // 4) % 2, (me // 8) % 2, me // 16]
    return bits, [me + (1 << i) - (2 << i) * b for i, b in enumerate(bits)]


def main_kernel(
    x, w, bias, cot, seg, offs, marks, edges, edge_marks, rims,
    act, xr, ag, gb,
    kt, ot, sc, mixed_v, w_v, bias_v, cot_v, gp_v,
    seg_v, offs_v, marks_v, edges_v, emarks_v, rims_v, qv, vv, hs, hr,
    snd, rc, fb, rf, ab, ra, sb, rs, rb, gb_v, gr,
    xsem, tsem, wsem, csem, ssem, rcsem, resem, rsem, bsem, brsem, hsem, hrsem,
):
    n = lax.axis_size("blk")
    me = lax.axis_index("blk")
    slots, deep, width = xr.shape
    rows = kt.shape[2]
    rim = rims_v.shape[2]
    near = offs_v.shape[1]
    halo = edges_v.shape[2]
    total = slots * rows
    nch = width // CH
    half = width // 2
    unit = half // U
    (core, bx, by, bz1, bz2), (pc, px, py, pz1, pz2) = neighbours(me)
    prev = lax.rem(me + n - 1, n)
    nxt = lax.rem(me + 1, n)
    first = [px * (1 - core) + py * core, py * (1 - core) + px * core]
    fbit = [bx * (1 - core) + by * core, by * (1 - core) + bx * core]
    second = [first[1], first[0]]
    sbit = [fbit[1], fbit[0]]

    def middle(u):
        pair = [(bz1, pz1), (sbit[u % 2], second[u % 2])]
        return pair[::-1] if u in TURNED else pair


    barrier = pltpu.get_barrier_semaphore()
    for p in (pc, px, py, pz1, pz2, prev, nxt):
        pl.semaphore_signal(barrier, inc=1, device_id=(p,), device_id_type=MESH)

    def local(src, dst, sem):
        return pltpu.make_async_copy(src, dst, sem)

    def cols(k):
        return pl.ds(pl.multiple_of(k * CH, CH), CH)

    def slot_rows(s):
        return pl.ds(pl.multiple_of(s * rows, 16), rows)

    def x_in(s):
        return local(x.at[slot_rows(s)], xr.at[s, pl.ds(0, rows)], xsem.at[s])

    def w_in(i):
        c = (pl.ds(0, CH), pl.ds(CH, width - CH))[i]
        return local(w.at[:, c], w_v.at[:, c], wsem.at[i])

    def cot_in(k):
        return local(cot.at[:, cols(k)], cot_v.at[k % 2], csem.at[k % 2])

    small = [
        local(src, dst, tsem.at[i])
        for i, (src, dst) in enumerate(
            (
                (rims, rims_v),
                (seg, seg_v),
                (offs, offs_v),
                (marks, marks_v),
                (edges, edges_v),
                (edge_marks, emarks_v),
                (bias, bias_v),
            )
        )
    ]
    small[0].start()
    x_in(0).start()
    x_in(slots - 1).start()
    for c in small[1:]:
        c.start()
    for s in range(1, slots - 1):
        x_in(s).start()

    def offer(s):
        picks = jnp.concatenate([rims_v[s, 0:1, :], rims_v[s, 1:2, :]], axis=1)
        order = lax.broadcasted_iota(jnp.int32, (rows, 2 * rim), 0)
        ot[s] = jnp.where(order == picks, 1.0, 0.0).astype(bf16)
        dims = (((0,), (0,)), ((), ()))
        return lax.dot_general(
            ot[s], xr[s, pl.ds(0, rows), :], dims, preferred_element_type=f32
        ).astype(bf16)

    def halo_send(j, q):
        s, to = ((0, nxt), (slots - 1, prev))[j]
        c = pl.ds(q * half, half)
        i = 2 * j + q
        return pltpu.make_async_remote_copy(
            hs.at[j, :, c], xr.at[s, pl.ds(rows + rim * j, rim), c], hsem.at[i], hrsem.at[i],
            device_id=(to,), device_id_type=MESH,
        )

    def back_send(j):
        to = (prev, nxt)[j]
        return pltpu.make_async_remote_copy(
            hs.at[2 + j], hr.at[j], hsem.at[4 + j], hrsem.at[4 + j],
            device_id=(to,), device_id_type=MESH,
        )

    small[0].wait()
    x_in(0).wait()
    out = offer(0)
    hs[1] = out[:rim]
    xr[1, pl.ds(rows, rim), :] = out[rim:]
    x_in(slots - 1).wait()
    out = offer(slots - 1)
    hs[0] = out[rim:]
    xr[slots - 2, pl.ds(rows + rim, rim), :] = out[:rim]
    pl.semaphore_wait(barrier, 7)
    for q in range(2):
        for j in range(2):
            halo_send(j, q).start()
    w_in(0).start()
    cot_in(0).start()
    cot_in(1).start()
    w_in(1).start()
    for c in small[1:]:
        c.wait()
    for s in range(1, slots - 1):
        x_in(s).wait()
        out = offer(s)
        xr[s - 1, pl.ds(rows + rim, rim), :] = out[:rim]
        xr[s + 1, pl.ds(rows, rim), :] = out[rim:]

    def tables(s, carry):
        seg_r = seg_v[pl.ds(s, 1), :].astype(f32)
        ri = lax.broadcasted_iota(jnp.int32, (rows, rows), 0)
        ci = lax.broadcasted_iota(jnp.int32, (rows, rows), 1)
        diag = ri == ci
        seg_c = jnp.sum(jnp.where(diag, seg_r, 0.0), axis=1, keepdims=True)
        start = jnp.sum(jnp.where(seg_r < seg_c, 1.0, 0.0), axis=1, keepdims=True)
        same = seg_r == seg_c
        size = jnp.sum(jnp.where(same, 1.0, 0.0), axis=0, keepdims=True)
        off = offs_v[s].astype(f32)
        rest = off - jnp.floor((off + 0.5) * (1.0 / size)) * size
        rest = jnp.where(rest < 0.0, rest + size, rest)
        rest = jnp.where(rest >= size, rest - size, rest)
        marked = marks_v[s]
        pick = jnp.where(marked == 1, rest.astype(jnp.int32), 200)
        qv[...] = pick >> 2
        vv[...] = 1 << ((pick & 3) << 3)
        q = lax.broadcasted_iota(jnp.int32, (Q, rows), 0)
        packed = jnp.zeros((Q, rows), jnp.int32)
        for k in range(near):
            packed = packed + jnp.where(qv[k : k + 1, :] == q, vv[k : k + 1, :], 0)
        counts = jnp.concatenate(
            [((packed >> (8 * r)) & 255).astype(f32) for r in range(4)], axis=0
        ).astype(bf16)
        rel = lax.broadcasted_iota(jnp.int32, (rows, 1), 0) - start.astype(jnp.int32)
        place = (rel & 3) * Q + (rel >> 2)
        lanes = lax.broadcasted_iota(jnp.int32, (rows, 4 * Q), 1)
        spread = jnp.where(lanes == place, 1.0, 0.0).astype(bf16)
        around = jnp.dot(spread, counts, preferred_element_type=f32)
        around = jnp.where(same, around, 0.0) + jnp.where(diag, 2.0, 0.0)
        kt[s, pl.ds(0, rows), :] = around.astype(bf16)
        degree = jnp.sum(marked, axis=0, keepdims=True)
        r = lax.broadcasted_iota(jnp.int32, (rim, rows), 0)
        for j in range(2):
            hot = emarks_v[s, j]
            degree = degree + jnp.sum(hot, axis=0, keepdims=True)
            pick = jnp.where(hot == 1, edges_v[s, j], 200)
            far = jnp.zeros((rim, rows), f32)
            for k in range(halo):
                far = far + jnp.where(pick[k : k + 1, :] == r, 1.0, 0.0)
            kt[s, pl.ds(rows + rim * j, rim), :] = far.astype(bf16)
        degree = jnp.sum(jnp.where(diag, degree.astype(f32), 0.0), axis=1, keepdims=True)
        sc[slot_rows(s), :] = 1.0 / (1.0 + degree)
        return carry

    lax.fori_loop(0, slots, tables, 0, unroll=True)

    def mix(s, tiles):
        d = slot_rows(s)
        dims = (((0,), (0,)), ((), ()))
        for j in tiles:
            c = pl.ds(j * (width // 4), width // 4)
            summed = lax.dot_general(kt[s], xr[s, :, c], dims, preferred_element_type=f32)
            mixed_v[d, c] = (sc[d, :] * summed).astype(bf16)

    def pre_part(k, start, count, more):
        d = pl.ds(start, count)
        b = bias_v[:, cols(k)]
        pre = jnp.dot(mixed_v[d, :], w_v[:, cols(k)], preferred_element_type=f32) + b
        sig = 0.5 * jnp.tanh(0.5 * pre) + 0.5
        out = pre * sig
        act[d, cols(k)] = out.astype(bf16)
        g = (cot_v[k % 2, d, :].astype(f32) * (sig + out * (1.0 - sig))).astype(bf16)
        gp_v[d, cols(k)] = g
        sums = jnp.sum(g.astype(f32), axis=0, keepdims=True)
        if more:
            sums = sums + gb_v[0, :, cols(k)]
        gb_v[0, :, cols(k)] = sums

    for s in range(1, slots - 1):
        mix(s, range(4))
    w_in(0).wait()
    cot_in(0).wait()
    pre_part(0, rows, total - 2 * rows, False)
    for q in range(2):
        for j in range(2):
            halo_send(j, q).wait_recv()
        mix(0, (2 * q, 2 * q + 1))
        mix(slots - 1, (2 * q, 2 * q + 1))
    pre_part(0, 0, rows, True)
    pre_part(0, total - rows, rows, True)

    def remote(src, dst, k, s, to):
        return pltpu.make_async_remote_copy(
            src,
            dst,
            ssem.at[s],
            rsem.at[k % 2, s - U],
            device_id=(to,),
            device_id_type=MESH,
        )

    def at(u, level, flip=False, base=0):
        r = base + unit * u
        size = unit
        picks = [bit for bit, _ in middle(u)]
        for j in range(level):
            size = size // 2
            b = picks[j]
            if flip and j == level - 1:
                b = 1 - b
            r = r + size * b
        return pl.ds(pl.multiple_of(r, 16), size)

    def part(k, j, u, level, flip=False):
        return ag.at[2 * k + j, at(u, level, flip, half * core)]

    def c_rs(k, u):
        return pltpu.make_async_remote_copy(
            snd.at[k % 2, :, at(u, 0)],
            rc.at[k % 4, :, at(u, 0)],
            ssem.at[u],
            rcsem.at[k % 4, u],
            device_id=(pc,),
            device_id_type=MESH,
        )

    def f_rs(k, u):
        return remote(fb.at[k % 2, u], rf.at[k, u], k, U + u, first[u % 2])

    def a_rs(k, u):
        return remote(ab.at[k % 2, u], ra.at[k, u], k, 2 * U + u, middle(u)[0][1])

    def s_rs(k, u):
        return remote(sb.at[k % 2, u], rs.at[k, u], k, 3 * U + u, middle(u)[1][1])

    def b_rs(k, u):
        return remote(part(k, fbit[u % 2], u, 2), rb.at[k, u], k, 4 * U + u, pz2)

    def s_ag(k, u):
        p = part(k, fbit[u % 2], u, 2)
        return remote(p, p, k, 5 * U + u, middle(u)[1][1])

    def a_ag(k, u):
        p = part(k, fbit[u % 2], u, 1)
        return remote(p, p, k, 6 * U + u, middle(u)[0][1])

    def e_ag(k, u):
        p = part(k, fbit[u % 2], u, 1)
        return pltpu.make_async_remote_copy(
            p,
            p,
            ssem.at[9 * U + u],
            resem.at[k % 4, u],
            device_id=(first[u % 2],),
            device_id_type=MESH,
        )

    def f_ag(k, u):
        p = part(k, fbit[u % 2], u, 1, True)
        return remote(p, p, k, 7 * U + u, first[u % 2])

    def c_ag(k, u):
        p = ag.at[pl.ds(2 * k, 2), at(u, 0, False, half * core)]
        return remote(p, p, k, 8 * U + u, pc)

    def free(send, k, u):
        @pl.when(k >= 1)
        def _():
            send(k - 1, u).wait_send()

    def fold_core(k, u):
        f = fbit[u % 2]
        free(f_rs, k, u)
        fb[k % 2, u] = part(k, 1 - f, u, 0)[...] + rc[k % 4, 1 - f, at(u, 0)]
        p = part(k, f, u, 0)
        p[...] = p[...] + rc[k % 4, f, at(u, 0)]

    def fold(level, buf, out, send):
        def run(k, u):
            f = fbit[u % 2]
            bit = middle(u)[level][0]
            size = (unit >> level) // 2
            free(send, k, u)
            away = pl.ds(pl.multiple_of(size * (1 - bit), 16), size)
            stay = pl.ds(pl.multiple_of(size * bit, 16), size)
            out[k % 2, u] = part(k, f, u, level + 1, True)[...] + buf[k, u, away]
            p = part(k, f, u, level + 1)
            p[...] = p[...] + buf[k, u, stay]

        return run

    def whole(buf):
        def run(k, u):
            p = part(k, fbit[u % 2], u, 2)
            p[...] = p[...] + buf[k, u]

        return run

    def last_fold(k, u):
        b_rs(k, u).wait_send()
        whole(rb)(k, u)

    hops = [
        ((c_rs,), fold_core, (f_rs,)),
        ((f_rs,), fold(0, rf, ab, a_rs), (a_rs,)),
        ((a_rs,), fold(1, ra, sb, s_rs), (s_rs,)),
        ((s_rs,), whole(rs), (b_rs,)),
        ((b_rs,), last_fold, (s_ag,)),
        ((s_ag,), None, (a_ag, e_ag)),
        ((a_ag,), None, (f_ag,)),
        ((e_ag, f_ag), None, (c_ag,)),
        ((c_ag,), None, ()),
    ]

    def serve(t, v, order):
        for h in order:
            took, work, sent = hops[h]
            back = v - DELAY[h]
            k = t + back // U
            u = back % U

            @pl.when((k >= 0) & (k < nch))
            def _():
                for copy in took:
                    copy(k, u).wait_recv()
                if work is not None:
                    work(k, u)
                for send in sent:
                    if h >= 4:
                        free(send, k, u)
                    send(k, u).start()

    def grad_part(k, side):
        start = pl.multiple_of(half * side, half)
        dims = (((0,), (0,)), ((), ()))
        return lax.dot_general(
            mixed_v[:, pl.ds(start, half)], gp_v[:, cols(k)], dims, preferred_element_type=f32
        )

    def there(k):
        grad = grad_part(k, 1 - core)
        snd[k % 2, 0] = grad[:, :H].astype(bf16)
        snd[k % 2, 1] = grad[:, H:].astype(bf16)

    def here(k):
        grad = grad_part(k, core)
        own = pl.ds(pl.multiple_of(half * core, half), half)
        ag[2 * k, own] = grad[:, :H].astype(bf16)
        ag[2 * k + 1, own] = grad[:, H:].astype(bf16)

    def early(t, more):
        serve(t, 0, ORDER)
        serve(t, 1, ORDER)

        @pl.when(t >= 1)
        def _():
            for u in range(U):
                c_rs(t - 1, u).wait_send()

        if more:
            cot_in(t + 1).wait()

            @pl.when(t == 0)
            def _():
                w_in(1).wait()

        there(t)
        if more:
            pre_part(t + 1, 0, total // 2, False)
        for u in range(U):
            c_rs(t, u).start()
        serve(t, 2, ORDER)
        serve(t, 3, ORDER)
        here(t)
        if more:
            pre_part(t + 1, total // 2, total // 2, True)

            @pl.when(t + 2 < nch)
            def _():
                cot_in(t + 2).start()

    def early_step(t, carry):
        early(t, True)
        return carry

    lax.fori_loop(0, nch - 1, early_step, 0)
    early(nch - 1, False)

    def bias_hop(j):
        to = pc
        for i, p in enumerate((px, py, pz1, pz2)):
            to = jnp.where(j == i + 1, p, to)
        return pltpu.make_async_remote_copy(
            gb_v.at[j], gr.at[j], bsem.at[j], brsem.at[j], device_id=(to,), device_id_type=MESH
        )

    def bias_step(i):
        @pl.when((i >= 1) & (i <= 5))
        def _():
            bias_hop(i - 1).wait_recv()
            gb_v[i] = gb_v[i - 1] + gr[i - 1]

        @pl.when(i < 5)
        def _():
            bias_hop(i).start()

    def late_mixed(i, carry):
        bias_step(i)
        s = jnp.where(i == 0, 0, jnp.where(i == 1, slots - 1, i - 1))
        d = slot_rows(s)
        tile = width // 4
        for v in range(U):
            serve(nch + i, v, ORDER)
            c = pl.ds(v * tile, tile)
            dims = (((1,), (1,)), ((), ()))
            back = lax.dot_general(gp_v[d, :], w_v[c, :], dims, preferred_element_type=f32)
            mixed_v[d, c] = (sc[d, :] * back).astype(bf16)
        out = jnp.dot(
            kt[s, pl.ds(rows, 2 * rim), :], mixed_v[d, :], preferred_element_type=f32
        ).astype(bf16)

        @pl.when(s > 0)
        def _():
            xr[s - 1, pl.ds(rows + rim, rim), :] = out[:rim]

        @pl.when(s < slots - 1)
        def _():
            xr[s + 1, pl.ds(rows, rim), :] = out[rim:]

        @pl.when(s == 0)
        def _():
            hs[2] = out[:rim]
            back_send(0).start()

        @pl.when(s == slots - 1)
        def _():
            hs[3] = out[rim:]
            back_send(1).start()

        return carry

    lax.fori_loop(0, slots, late_mixed, 0)
    back_send(0).wait_recv()
    back_send(1).wait_recv()
    xr[slots - 1, pl.ds(rows + rim, rim), :] = hr[0]
    xr[0, pl.ds(rows, rim), :] = hr[1]

    def late_features(s, carry):
        bias_step(s + slots)
        d = slot_rows(s)
        tile = width // 4
        for v in range(U):
            serve(nch + slots + s, v, ORDER)
            c = pl.ds(v * tile, tile)
            grad = jnp.dot(kt[s, pl.ds(0, rows), :], mixed_v[d, c], preferred_element_type=f32)
            grad = grad + jnp.dot(
                ot[s], xr[s, pl.ds(rows, 2 * rim), c], preferred_element_type=f32
            )
            xr[s, pl.ds(0, rows), c] = grad.astype(bf16)
        return carry

    lax.fori_loop(0, slots, late_features, 0)

    def late(t, carry):
        for v in range(U):
            serve(t, v, ORDER)
        return carry

    lax.fori_loop(nch + 2 * slots, nch + (DELAY[-1] + U - 1) // U, late, 0)
    gb[...] = gb_v[5]
    for j in range(5):
        bias_hop(j).wait_send()
    for j in range(2):
        for q in range(2):
            halo_send(j, q).wait_send()
        back_send(j).wait_send()
    for k in range(nch - 1, nch):
        for u in range(U):
            for f in (c_rs, f_rs, a_rs, s_rs, s_ag, a_ag, e_ag, f_ag, c_ag):
                f(k, u).wait_send()


U = 4
TURNED = (0,)
Q = 24
DELAY = [4 + 4 * h for h in range(9)]
ORDER = list(range(8, -1, -1))


def main_call(features, weight, bias, cot, seg, offs, marks, edges, edge_marks, rims):
    slots, rows = seg.shape
    total, width = cot.shape
    rim = rims.shape[2]
    nch = width // CH
    half = width // 2
    unit = half // U
    any_ = pl.BlockSpec(memory_space=pl.ANY)
    dma = pltpu.SemaphoreType.DMA
    i32 = jnp.int32
    return pl.pallas_call(
        main_kernel,
        out_shape=(
            pltpu.VMEM((total, width), bf16),
            pltpu.VMEM((slots, rows + 2 * rim, width), bf16),
            pltpu.VMEM((2 * nch, width, H), bf16),
            pltpu.VMEM((1, width), f32),
        ),
        in_specs=[any_] * 10,
        out_specs=[pl.BlockSpec(memory_space=pltpu.VMEM)] * 4,
        scratch_shapes=[
            pltpu.VMEM((slots, rows + 2 * rim, rows), bf16),
            pltpu.VMEM((slots, rows, 2 * rim), bf16),
            pltpu.VMEM((total, 1), f32),
            pltpu.VMEM((total, width), bf16),
            pltpu.VMEM((width, width), bf16),
            pltpu.VMEM((1, width), f32),
            pltpu.VMEM((2, total, CH), bf16),
            pltpu.VMEM((total, width), bf16),
            pltpu.VMEM(seg.shape, i32),
            pltpu.VMEM(offs.shape, i32),
            pltpu.VMEM(marks.shape, i32),
            pltpu.VMEM(edges.shape, i32),
            pltpu.VMEM(edge_marks.shape, i32),
            pltpu.VMEM(rims.shape, i32),
            pltpu.VMEM((offs.shape[1], rows), i32),
            pltpu.VMEM((offs.shape[1], rows), i32),
            pltpu.VMEM((4, rim, width), bf16),
            pltpu.VMEM((2, rim, width), bf16),
            pltpu.VMEM((2, 2, half, H), bf16),
            pltpu.VMEM((4, 2, half, H), bf16),
            pltpu.VMEM((2, U, unit, H), bf16),
            pltpu.VMEM((nch, U, unit, H), bf16),
            pltpu.VMEM((2, U, unit // 2, H), bf16),
            pltpu.VMEM((nch, U, unit // 2, H), bf16),
            pltpu.VMEM((2, U, unit // 4, H), bf16),
            pltpu.VMEM((nch, U, unit // 4, H), bf16),
            pltpu.VMEM((nch, U, unit // 4, H), bf16),
            pltpu.VMEM((6, 1, width), f32),
            pltpu.VMEM((5, 1, width), f32),
            dma((slots,)),
            dma((7,)),
            dma((2,)),
            dma((2,)),
            dma((10 * U,)),
            dma((4, U)),
            dma((4, U)),
            dma((2, 8 * U)),
            dma((5,)),
            dma((5,)),
            dma((6,)),
            dma((6,)),
        ],
        compiler_params=pltpu.CompilerParams(
            collective_id=0, has_side_effects=True, vmem_limit_bytes=40 << 20
        ),
        name="layer",
    )(features, weight, bias, cot, seg, offs, marks, edges, edge_marks, rims)


def finish_kernel(act, xr, ag, gb, act_o, gf_o, gw_o, gb_o, stage, sem, ssem):
    slots, rows, _ = gf_o.shape
    n, step, _ = stage.shape
    plain = [(gb, gb_o), (act, act_o)]
    plain += [(xr.at[s, pl.ds(0, rows)], gf_o.at[s]) for s in range(slots)]
    plain = [pltpu.make_async_copy(a, b, sem.at[i]) for i, (a, b) in enumerate(plain)]

    def out(i):
        return pltpu.make_async_copy(
            stage.at[i % n], gw_o.at[pl.ds(i * step, step)], ssem.at[i % n]
        )

    steps = gw_o.shape[0] // step
    for i in range(steps):
        if i >= n:
            out(i - n).wait()
        for j in range(ag.shape[0]):
            stage[i % n, :, j * H : (j + 1) * H] = ag[j, i * step : (i + 1) * step].astype(f32)
        out(i).start()
        if i == 0:
            for c in plain:
                c.start()
    for i in range(steps - n, steps):
        out(i).wait()
    for c in plain:
        c.wait()


def finish(act, xr, ag, gb, rows):
    slots, _, width = xr.shape
    vmem = pl.BlockSpec(memory_space=pltpu.VMEM)
    any_ = pl.BlockSpec(memory_space=pl.ANY)
    return pl.pallas_call(
        finish_kernel,
        out_shape=(
            jax.ShapeDtypeStruct(act.shape, bf16),
            jax.ShapeDtypeStruct((slots, rows, width), bf16),
            jax.ShapeDtypeStruct((width, width), f32),
            jax.ShapeDtypeStruct((1, width), f32),
        ),
        in_specs=[vmem] * 4,
        out_specs=[any_] * 4,
        scratch_shapes=[
            pltpu.VMEM((8, 64, width), f32),
            pltpu.SemaphoreType.DMA((2 + slots,)),
            pltpu.SemaphoreType.DMA((8,)),
        ],
        compiler_params=pltpu.CompilerParams(vmem_limit_bytes=6 << 20),
        name="finish",
    )(act, xr, ag, gb)


def passed_along(value, axis, steps):
    count = lax.axis_size(axis)
    pairs = [(source, (source + steps) % count) for source in range(count)]
    return lax.ppermute(value, axis, pairs)


def tables(seg, offsets, marks, edges, edge_marks, rim):
    slots, rows = seg.shape
    order = jnp.arange(rows, dtype=jnp.int32)
    same = seg[:, :, None] == seg[:, None, :]
    start = jnp.min(jnp.where(same, order, rows), axis=2)
    extent = jnp.sum(same.astype(jnp.int32), axis=2)
    picks = jnp.where(marks == 1, offsets % extent[:, :, None], -1)
    lanes = jnp.arange(128, dtype=jnp.int32)
    near = jnp.sum((picks[:, :, :, None] == lanes).astype(f32), axis=2).astype(bf16)
    spread = (lanes[None, :, None] == (order - start)[:, None, :]).astype(bf16)
    local = jnp.einsum("sio,soj->sij", near, spread, preferred_element_type=f32)
    local = jnp.where(same, local, 0.0) + 2.0 * (order[:, None] == order[None, :])
    joined = jnp.concatenate([edges[:, 0], edges[:, 1] + rim], axis=2)
    joined_marks = jnp.concatenate([edge_marks[:, 0], edge_marks[:, 1]], axis=2)
    cols = jnp.arange(2 * rim, dtype=jnp.int32)
    far = jnp.sum(jnp.where(joined[..., None] == cols, joined_marks[..., None], 0), axis=2)
    degree = jnp.sum(marks, axis=2) + jnp.sum(joined_marks, axis=2)
    return local.astype(bf16), far.astype(bf16), 1.0 / (1.0 + degree.astype(f32))


def spread_out(
    features,
    weight,
    bias,
    cotangent,
    segment_ids,
    neighbour_offsets,
    neighbour_mask,
    halo_edges,
    halo_mask,
    boundary_rows,
):
    slots, rows, width = features.shape
    rim = boundary_rows.shape[2]
    local_counts, halo_counts, scale = tables(
        segment_ids, neighbour_offsets, neighbour_mask, halo_edges, halo_mask, rim
    )
    chosen = (boundary_rows[..., None] == jnp.arange(rows, dtype=jnp.int32)).astype(bf16)
    sent = jnp.einsum("sjbr,srf->sjbf", chosen, features, preferred_element_type=f32).astype(bf16)
    from_prev = passed_along(sent[slots - 1, 1], "blk", 1)
    from_next = passed_along(sent[0, 0], "blk", -1)
    before = jnp.concatenate([from_prev[None], sent[: slots - 1, 1]], axis=0)
    after = jnp.concatenate([sent[1:, 0], from_next[None]], axis=0)
    received = jnp.concatenate([before, after], axis=1)
    summed = jnp.einsum("srk,skf->srf", local_counts, features, preferred_element_type=f32)
    summed = summed + jnp.einsum("srk,skf->srf", halo_counts, received, preferred_element_type=f32)
    mixed = (scale[:, :, None] * summed).astype(bf16).reshape(slots * rows, width)
    incoming = cotangent.reshape(slots * rows, width)
    pre = jnp.dot(mixed, weight, preferred_element_type=f32) + bias[None, :]
    sigma = jax.nn.sigmoid(pre)
    activations = (pre * sigma).astype(bf16)
    grad_pre = (incoming.astype(f32) * (sigma * (1.0 + pre * (1.0 - sigma)))).astype(bf16)
    bias_term = jnp.sum(grad_pre, axis=0, dtype=f32)
    weight_term = lax.dot_general(
        mixed, grad_pre, (((0,), (0,)), ((), ())), preferred_element_type=f32
    )
    grad_weight, grad_bias = lax.psum((weight_term, bias_term), "blk")
    grad_mixed = lax.dot_general(
        grad_pre, weight, (((1,), (1,)), ((), ())), preferred_element_type=f32
    )
    grad_summed = (scale.reshape(-1)[:, None] * grad_mixed).astype(bf16)
    grad_summed = grad_summed.reshape(slots, rows, width)
    grad_received = jnp.einsum(
        "srk,srf->skf", halo_counts, grad_summed, preferred_element_type=f32
    ).astype(bf16)
    toward_prev = grad_received[:, :rim]
    toward_next = grad_received[:, rim:]
    back_prev = passed_along(toward_next[slots - 1], "blk", 1)
    back_next = passed_along(toward_prev[0], "blk", -1)
    grad_first = jnp.concatenate([back_prev[None], toward_next[: slots - 1]], axis=0)
    grad_second = jnp.concatenate([toward_prev[1:], back_next[None]], axis=0)
    grad_sent = jnp.stack([grad_first, grad_second], axis=1)
    grad_features = jnp.einsum(
        "srk,srf->skf", local_counts, grad_summed, preferred_element_type=f32
    ) + jnp.einsum("sjbr,sjbf->srf", chosen, grad_sent, preferred_element_type=f32)
    return (
        activations.reshape(slots, rows, width),
        grad_features.astype(bf16),
        grad_weight,
        grad_bias,
    )


def per_device(
    features,
    weight,
    bias,
    cotangent,
    segment_ids,
    neighbour_offsets,
    neighbour_mask,
    halo_edges,
    halo_mask,
    boundary_rows,
):
    operands = (
        segment_ids,
        neighbour_offsets,
        neighbour_mask,
        halo_edges,
        halo_mask,
        boundary_rows,
    )
    if lax.axis_size("blk") != 32:
        return spread_out(features, weight, bias, cotangent, *operands)
    slots, rows, width = features.shape
    flat = (slots * rows, width)
    held = main_call(
        features.reshape(flat),
        weight,
        bias.reshape(1, width),
        cotangent.reshape(flat),
        segment_ids,
        jnp.swapaxes(neighbour_offsets, 1, 2),
        jnp.swapaxes(neighbour_mask, 1, 2),
        jnp.swapaxes(halo_edges, 2, 3),
        jnp.swapaxes(halo_mask, 2, 3),
        boundary_rows,
    )
    activations, grad_features, grad_weight, grad_bias = finish(*held, rows)
    return (
        activations.reshape(features.shape),
        grad_features,
        grad_weight,
        grad_bias.reshape(-1),
    )


def solution(mesh):
    in_specs = (
        P("blk", None, None),
        P(),
        P(),
        P("blk", None, None),
        P("blk", None),
        P("blk", None, None),
        P("blk", None, None),
        P("blk", None, None, None),
        P("blk", None, None, None),
        P("blk", None, None),
    )
    out_specs = (P("blk", None, None), P("blk", None, None), P(), P())
    return jax.shard_map(
        per_device, mesh=mesh, in_specs=in_specs, out_specs=out_specs, check_vma=False
    )
```
